128 devices in a mesh: gx: 16 (over y, x_hi, core), gy: 8 (over x_lo, z).
Axes of the slice: x: 4 (x_hi: 2, x_lo: 2; x = x_hi * 2 + x_lo), y: 4, z: 4, core: 2. Of those that a mesh axis runs over, the one named last changes fastest.
Arguments:
- ocean_depth: float32 [4096, 4096], P('gx', 'gy'), may hold values from 0.5 to 8
- wet_mask: int32 [4096, 4096], P('gx', 'gy'), may hold values 0 or 1
- manning: float32 [4096, 4096], P('gx', 'gy'), may hold values from 0.5 to 5
- fault_slip: float32 [2048], P(('gx', 'gy')), may hold values from 0.3 to 1.2
- pattern: float32 [32768, 8, 128], P(('gx', 'gy')), may hold values from -1 to 1
- foot_tile: int32 [32768, 1], P(('gx', 'gy')), may hold values from 0 to 127; in each aligned block of 256 rows (0 to 255, 256 to 511, ...) at most 4 rows name the same one
- foot_block: int32 [32768], P(('gx', 'gy')), may hold values from 0 to 127
- gauge_row: int32 [2048], replicated, may hold values from 0 to 4095, as said below
- gauge_col: int32 [2048], replicated, may hold values from 0 to 4095, as said below
- observed: float32 [4, 2048], replicated, may hold values from -6 to 6
Outputs:
- final_eta: float32 [4096, 4096], P('gx', 'gy')
- readings: float32 [4, 2048], replicated
- source_adjoint: float32 [4096, 4096], P('gx', 'gy')
- grad_slip: float32 [2048], P(('gx', 'gy'))
The draws below stay inside these ranges and needn't reach their ends.
Inputs may be any that keep to these rules, and one draw needn't show every extreme that they name: `foot_tile`: the 256 rows of one device name no tile more than 4 times, a bound that some block reaches. Tile t is the one at tile row t // 8 and tile column t % 8. `gauge_row`: gauges 16 * t to 16 * t + 15 lie in tile t, within three cells of one of its edges. `gauge_col`: see gauge_row.
All inputs are finite; a program needn't handle non-finite values. No bound on the sum of `wet_mask` on one device may be relied on, other than what follows from the above.
Results may differ from the reference program's by a relative error of at most 0.0003.
Values sent between devices are 32-bit elements; how exact they have to be, the bound alone decides.
No kernel may reach another device: no remote copies, remote signals or barrier semaphores. Data moves between devices by JAX's collectives and lax.ppermute only.
A program may use at most 128 MiB of HBM per device.

```python
import math
from functools import partial
import jax
import jax.numpy as jnp
import numpy as np

CR = 256
CC = 512
SUB_DEV = 16
FP = 16
GAUGE_DEV = 16
STEPS = 4
GRID_R = 4096
GRID_C = 4096
TILES_C = 8
NB = 128
SUB = 2048
GAUGES = 2048
CAP = 4
DEVICES = 128


def gauge_places(key):
    base = jax.random.fold_in(key, 41)
    first_key, second_key = jax.random.split(base)
    numbers = jnp.arange(GAUGES, dtype=jnp.int32)
    tile_index = numbers // GAUGE_DEV
    edge_side = numbers % 4
    inset = jax.random.randint(first_key, (GAUGES,), 0, 3, dtype=jnp.int32)
    along = jax.random.randint(second_key, (GAUGES,), 0, 1 << 20, dtype=jnp.int32)
    local_row = jnp.where(edge_side == 0, inset, jnp.where(edge_side == 1, CR - 1 - inset, along % CR))
    local_col = jnp.where(edge_side == 2, inset, jnp.where(edge_side == 3, CC - 1 - inset, along % CC))
    tiles_across = GRID_C // CC
    grid_row = tile_index // tiles_across * CR + local_row
    grid_col = tile_index % tiles_across * CC + local_col
    return (grid_row.astype(jnp.int32), grid_col.astype(jnp.int32))


def draw_gauge_row(key, part):
    return gauge_places(key)[0]


def draw_gauge_col(key, part):
    return gauge_places(key)[1]


def touch_ends(drawn, own_key, least, largest):
    longest = drawn.shape.index(max(drawn.shape))
    spots = []
    for shift in (0, 1):
        where = [jax.random.randint(jax.random.fold_in(own_key, axis), (), 0, length) for axis, length in enumerate(drawn.shape)]
        where[longest] = (where[longest] + shift) % drawn.shape[longest]
        spots.append(tuple(where))
    return drawn.at[spots[0]].set(least).at[spots[1]].set(largest)


def block_scale(stream_key, shape, pieces, low, top_value):
    loudness = 1.0
    for dim, parts in pieces:
        heights = jax.random.uniform(jax.random.fold_in(jax.random.fold_in(stream_key, 6), dim), (parts,), jnp.float32, low / len(pieces), top_value / len(pieces))
        loudness = loudness * jnp.repeat(jnp.exp(heights), shape[dim] // parts).reshape((-1,) + (1,) * (len(shape) - 1 - dim))
    return loudness


def shared_out(own_key, own, number, rows, count, top, bound, skew):
    order = jax.random.permutation(own_key, count)
    crowded, common = portions_of(count, rows * top, bound, skew, True), portions_of(count, rows * top, bound, skew, False)
    places = jnp.arange(count)

    def named(lengths, offset_by):
        used = int((lengths > 0).sum())
        fixed = max(1, used // 4)
        passed = fixed + (places - fixed + offset_by * (used - fixed)) % max(1, count - fixed)
        return jnp.zeros((count,), jnp.int32).at[order[jnp.where(places < fixed, places, passed)]].set(jnp.asarray(lengths, jnp.int32))

    lengths = jnp.where(number % 4 == 0, named(crowded, number // 4), named(common, number - number // 4 - 1))
    mixed = jax.random.permutation(jax.random.fold_in(own, 3), count)
    source_of, taker = mixed[0:count // 2 * 2:2], mixed[1:count // 2 * 2:2]
    room = jnp.minimum(lengths[source_of] - 1, bound - lengths[taker]) // 2
    room = jnp.where((source_of == order[0]) | (taker == order[0]) | (lengths[taker] == 0), 0, jnp.maximum(room, 0))
    passed = jax.random.randint(jax.random.fold_in(own, 4), (count // 2,), 0, 1 << 20) % (room + 1)
    lengths = lengths.at[source_of].add(-passed).at[taker].add(passed)
    items = jnp.searchsorted(jnp.cumsum(lengths), jnp.arange(rows * top), side="right").astype(jnp.int32)
    grid = items.reshape(top, rows).T
    grid = grid[jax.random.permutation(jax.random.fold_in(own, 1), rows)]
    offset_by = jax.random.randint(jax.random.fold_in(own, 2), (rows, 1), 0, top)
    return jnp.take_along_axis(grid, (jnp.arange(top)[None, :] + offset_by) % top, axis=1)


def portions_of(amount, total, reach, lean, full):
    portions = [(1 << 20) // math.isqrt(standing ** lean) + 1 for standing in range(1, amount + 1)]
    largest = reach if full else min(reach, max(-(-total // amount), total * portions[0] // sum(portions)))
    least = 1 if total - largest >= amount - 1 else 0
    counts, spare = [largest] + [least] * (amount - 1), total - largest - least * (amount - 1)
    while spare > 0:
        candidates = [i for i in range(1, amount) if counts[i] < largest] or [i for i in range(1, amount) if counts[i] < reach]
        mass, remaining = sum([portions[i] for i in candidates]), spare
        for i in candidates:
            more = min(reach - counts[i], max(1, remaining * portions[i] // mass), spare)
            counts[i] = counts[i] + more
            spare = spare - more
    return np.array(counts)


def normal_values(key, shape, deviation, reach, kind=jnp.bfloat16):
    entries = jax.random.normal(key, shape, jnp.float32) * deviation
    return jnp.minimum(jnp.maximum(entries, -reach), reach).astype(kind)


def setup_inputs(seed: int = 0) -> dict:
    seeds = jax.random.split(jax.random.key(seed), 11)
    ocean_depth = jnp.clip(jnp.exp(math.log(8.0) - 2.7725887 * jax.random.uniform(seeds[0], (GRID_R, GRID_C), jnp.float32) ** block_scale(seeds[0], (GRID_R, GRID_C), ((0, 16), (1, 8)), -0.2, 0.2)), 0.5, 8.0)
    wet_mask = touch_ends((jax.random.randint(seeds[1], (GRID_R, GRID_C), 0, 8) < 7).astype(jnp.int32), jax.random.fold_in(seeds[1], 1), 0, 1)
    manning = jnp.clip(jnp.exp(math.log(5.0) - 2.3025851 * jax.random.uniform(seeds[2], (GRID_R, GRID_C), jnp.float32) ** block_scale(seeds[2], (GRID_R, GRID_C), ((0, 16), (1, 8)), -0.2, 0.2)), 0.5, 5.0)
    fault_slip = jnp.clip(jnp.exp(math.log(1.2) - 1.3862944 * jax.random.uniform(seeds[3], (SUB,), jnp.float32) ** block_scale(seeds[3], (SUB,), ((0, 128),), -0.2, 0.2)), 0.3, 1.2)
    pattern = jnp.clip(jax.random.uniform(seeds[4], (SUB * FP, 8, 128), jnp.float32, -1.0, 1.0) * block_scale(seeds[4], (SUB * FP, 8, 128), ((0, 128),), -0.4, 0.0), -1.0, 1.0)
    foot_tile_keys = jax.random.split(jax.random.fold_in(seeds[5], 1), (SUB * FP) // (SUB_DEV * FP))
    foot_tile_turns = jax.random.permutation(jax.random.fold_in(seeds[5], 3), (SUB * FP) // (SUB_DEV * FP))
    foot_tile = jax.vmap(lambda own, number: shared_out(jax.random.fold_in(seeds[5], 2), own, number, SUB_DEV * FP, DEVICES, 1, CAP, 2))(foot_tile_keys, foot_tile_turns).reshape((SUB * FP, 1))
    foot_block = touch_ends(jax.random.randint(seeds[6], (SUB * FP,), 0, NB), jax.random.fold_in(seeds[6], 1), 0, NB - 1).astype(jnp.int32)
    gauge_row = draw_gauge_row(jax.random.fold_in(seeds[10], 71), 0)
    gauge_col = draw_gauge_col(jax.random.fold_in(seeds[10], 71), 0)
    observed = normal_values(seeds[9], (STEPS, GAUGES), 1.0, 6.0, jnp.float32)
    return {"ocean_depth": ocean_depth, "wet_mask": wet_mask, "manning": manning, "fault_slip": fault_slip, "pattern": pattern, "foot_tile": foot_tile, "foot_block": foot_block, "gauge_row": gauge_row, "gauge_col": gauge_col, "observed": observed}


wave_gain = 0.2
mass_gain = 0.2
min_depth = 0.25
speed_floor = 0.01

def eastward(field, column):
    return jnp.concatenate([field[:, 1:], column[:, None]], axis=1)

def southward(field, row_edge):
    return jnp.concatenate([field[1:], row_edge[None]], axis=0)

def face_flux(flux, here, there, depth_here, depth_there, wet_here, wet_there, fric_here, fric_there):
    total_depth = jnp.maximum(0.5 * (depth_here + here + depth_there + there), min_depth)
    pushed = flux - wave_gain * total_depth * (there - here)
    roughness = 0.5 * (fric_here + fric_there)
    drag_factor = 1.0 + roughness * jnp.sqrt(pushed * pushed + speed_floor) / jnp.power(total_depth, 7.0 / 3.0)
    return wet_here * wet_there * pushed / drag_factor

def fluxes(statics, static_east, static_south, surface, east_rim, south_rim, flux_east, flux_south):
    depth_here, wet_here, fric_here = (statics[0], statics[1], statics[2])
    next_east = face_flux(flux_east, surface, eastward(surface, east_rim), depth_here, eastward(depth_here, static_east[0]), wet_here, eastward(wet_here, static_east[1]), fric_here, eastward(fric_here, static_east[2]))
    next_south = face_flux(flux_south, surface, southward(surface, south_rim), depth_here, southward(depth_here, static_south[0]), wet_here, southward(wet_here, static_south[1]), fric_here, southward(fric_here, static_south[2]))
    return (next_east, next_south)

def surface_step(wet_cells, surface, next_east, next_south, west_rim, north_rim):
    left_flux = jnp.concatenate([west_rim[:, None], next_east[:, :-1]], axis=1)
    upper_flux = jnp.concatenate([north_rim[None], next_south[:-1]], axis=0)
    return wet_cells * (surface - mass_gain * (next_east - left_flux + next_south - upper_flux))

def tile_from_blocks(blocks, rows_here, cols_here):
    return blocks.reshape(rows_here // 8, cols_here // 128, 8, 128).transpose(0, 2, 1, 3).reshape(rows_here, cols_here)

def build_source(fault_slip, pattern, foot_tile, foot_block, wet_cells):
    tile_index = foot_tile[:, 0]
    per_row = CC // 128
    block_row = tile_index // TILES_C * (CR // 8) + foot_block // per_row
    block_col = tile_index % TILES_C * per_row + foot_block % per_row
    global_block = block_row * (GRID_C // 128) + block_col
    weights = jnp.repeat(fault_slip, FP)
    terms = weights[:, None] * pattern.reshape(SUB * FP, 1024)
    grid_blocks = jnp.zeros((GRID_R // 8 * (GRID_C // 128), 1024), jnp.float32).at[global_block].add(terms)
    return tile_from_blocks(grid_blocks, GRID_R, GRID_C) * wet_cells

def reference(ocean_depth, wet_mask, manning, fault_slip, pattern, foot_tile, foot_block, gauge_row, gauge_col, observed):
    wet_cells = wet_mask.astype(jnp.float32)
    statics = jnp.stack([ocean_depth, wet_cells, manning])
    zero_cols = jnp.zeros((3, GRID_R), jnp.float32)
    zero_rows = jnp.zeros((3, GRID_C), jnp.float32)
    edge_col = jnp.zeros((GRID_R,), jnp.float32)
    edge_row = jnp.zeros((GRID_C,), jnp.float32)

    def run(eta_start):
        surface = eta_start
        flux_east = jnp.zeros_like(eta_start)
        flux_south = jnp.zeros_like(eta_start)
        gathered = []
        for step_index in range(STEPS):
            next_east, next_south = fluxes(statics, zero_cols, zero_rows, surface, edge_col, edge_row, flux_east, flux_south)
            surface = surface_step(wet_cells, surface, next_east, next_south, edge_col, edge_row)
            flux_east, flux_south = (next_east, next_south)
            gathered.append(surface[gauge_row, gauge_col])
        return (surface, jnp.stack(gathered))
    eta_start, source_fn = jax.vjp(partial(build_source, pattern=pattern, foot_tile=foot_tile, foot_block=foot_block, wet_cells=wet_cells), fault_slip)
    (final_eta, readings), run_fn = jax.vjp(run, eta_start)
    misfit_terms = readings - observed
    source_adjoint, = run_fn((jnp.zeros_like(final_eta), misfit_terms))
    grad_slip, = source_fn(source_adjoint)
    return (final_eta, readings, source_adjoint, grad_slip)
```

```python
import math

import jax
import jax.numpy as jnp
from jax import lax
from jax.experimental import pallas as pl
from jax.experimental.pallas import tpu as pltpu
from jax.sharding import PartitionSpec as P

wave_gain = 0.2
mass_gain = 0.2
min_depth = 0.25
speed_floor = 0.01

HALO = 8
CHUNK = 33
SLOTS = 4
LN2 = math.log(2.0)
F32 = jnp.float32
I32 = jnp.int32


def vmem():
    return pl.BlockSpec(memory_space=pltpu.VMEM)


def smem():
    return pl.BlockSpec(memory_space=pltpu.SMEM)


def hbm():
    return pl.BlockSpec(memory_space=pl.ANY)


def shifted(shard, axis, by):
    devices = lax.axis_size(axis)
    pairs = [(i, i + by) for i in range(devices) if 0 <= i + by < devices]
    return lax.ppermute(shard, axis, pairs)


def pack_kernel(row_ref, slip_ref, pattern_ref, meta_ref, out_ref):
    rows = out_ref.shape[0]
    entries = pattern_ref.shape[0]
    per_fault = entries // slip_ref.shape[0]
    zero = jnp.zeros((8, 128), F32)

    def clear(i, c):
        out_ref[pl.ds(pl.multiple_of(i * 8, 8), 8), :] = zero
        return c

    lax.fori_loop(0, rows // 8, clear, 0, unroll=16)
    for t in range(rows // CHUNK):
        out_ref[pl.ds(t * CHUNK + 32, 1), :] = meta_ref[pl.ds(t, 1), :]

    def place(s, c):
        slip = slip_ref[s]
        for j in range(per_fault):
            i = s * per_fault + j
            out_ref[pl.ds(row_ref[i], 8), :] = pattern_ref[i] * slip
        return c

    lax.fori_loop(0, slip_ref.shape[0], place, 0)


def edges_of(first, last):
    lane = lax.broadcasted_iota(I32, first.shape, 1)
    both = jnp.where(lane < 64, first, last).T
    return both[0:8], both[120:128]


def side_block(east, west):
    rows = east.shape[1]
    gap = jnp.zeros((128 - 16, rows), F32)
    return jnp.concatenate([east, gap, west], axis=0).T


def scatter_kernel(block_ref, recv_ref, wet_ref, eta_ref, west_ref, east_ref, *acc):
    tiles = recv_ref.shape[0] // CHUNK
    rows, cols = eta_ref.shape
    across = cols // 128
    zero = jnp.zeros((8, 128), F32)

    def clear(i, c):
        for a in acc:
            a[i] = zero
        return c

    lax.fori_loop(0, acc[0].shape[0], clear, 0, unroll=8)

    def add(t, c):
        for j in range(SLOTS):
            b = block_ref[t * SLOTS + j]
            acc[j][b] = acc[j][b] + recv_ref[pl.ds(t * CHUNK + 8 * j, 8), :]
        return c

    lax.fori_loop(0, tiles, add, 0, unroll=4)

    def merge(i, c):
        r = pl.multiple_of(i * 8, 8)
        for q in range(across):
            b = i * across + q
            total = (acc[0][b] + acc[1][b]) + (acc[2][b] + acc[3][b])
            wet = wet_ref[pl.ds(r, 8), q * 128 : q * 128 + 128].astype(F32)
            eta_ref[pl.ds(r, 8), q * 128 : q * 128 + 128] = total * wet
        return c

    lax.fori_loop(0, rows // 8, merge, 0, unroll=2)
    west, east = edges_of(eta_ref[:, 0:128], eta_ref[:, cols - 128 : cols])
    west_ref[...] = west
    east_ref[...] = east


def static_edge_kernel(depth_ref, wet_ref, fric_ref, west_ref, east_ref):
    cols = depth_ref.shape[1]
    for n, ref in enumerate((depth_ref, wet_ref, fric_ref)):
        west, east = edges_of(ref[:, 0:128].astype(F32), ref[:, cols - 128 : cols].astype(F32))
        west_ref[8 * n : 8 * n + 8] = west
        east_ref[8 * n : 8 * n + 8] = east


def rim_kernel(*refs):
    fields = refs[:-4]
    east_ref, west_ref, top_ref, bottom_ref = refs[-4:]
    rows, cols = fields[0].shape
    for n, ref in enumerate(fields):
        block = side_block(east_ref[8 * n : 8 * n + 8], west_ref[8 * n : 8 * n + 8])
        top_ref[8 * n : 8 * n + 8, 0:cols] = ref[0:8, :].astype(F32)
        top_ref[8 * n : 8 * n + 8, cols:] = block[0:8]
        bottom_ref[8 * n : 8 * n + 8, 0:cols] = ref[rows - 8 : rows, :].astype(F32)
        bottom_ref[8 * n : 8 * n + 8, cols:] = block[rows - 8 : rows]


def assemble(out, n, ref, east_ref, west_ref, north_ref, south_ref):
    rows, cols = ref.shape
    out[0:8, :] = north_ref[8 * n : 8 * n + 8]
    out[8 : 8 + rows, 0:cols] = ref[...].astype(F32)
    out[8 : 8 + rows, cols:] = side_block(
        east_ref[8 * n : 8 * n + 8], west_ref[8 * n : 8 * n + 8]
    )
    out[8 + rows : 16 + rows, :] = south_ref[8 * n : 8 * n + 8]


def row_iota(shape):
    return lax.broadcasted_iota(I32, shape, 0)


def face_static_kernel(
    depth_ref, wet_ref, fric_ref, east_ref, west_ref, north_ref, south_ref,
    wet_out, dde, dds, rre, rrs, wwe, wws, depth_x, fric_x,
):
    halos = (east_ref, west_ref, north_ref, south_ref)
    assemble(depth_x, 0, depth_ref, *halos)
    assemble(wet_out, 1, wet_ref, *halos)
    assemble(fric_x, 2, fric_ref, *halos)
    rows, cols = depth_x.shape
    last = row_iota((8, cols)) == 7

    def step(i, c):
        r = pl.multiple_of(i * 8, 8)
        n = pl.multiple_of(jnp.minimum(r + 8, rows - 8), 8)
        for src, e_out, s_out, half in (
            (depth_x, dde, dds, True),
            (fric_x, rre, rrs, True),
            (wet_out, wwe, wws, False),
        ):
            here = src[pl.ds(r, 8), :]
            nxt = src[pl.ds(n, 8), :]
            east = pltpu.roll(here, cols - 1, 1)
            south = jnp.where(last, pltpu.roll(nxt, 7, 0), pltpu.roll(here, 7, 0))
            if half:
                e_out[pl.ds(r, 8), :] = 0.5 * (here + east)
                s_out[pl.ds(r, 8), :] = 0.5 * (here + south)
            else:
                e_out[pl.ds(r, 8), :] = here * east
                s_out[pl.ds(r, 8), :] = here * south
        return c

    lax.fori_loop(0, rows // 8, step, 0)


def gauge_kernel(place_ref, row_ref, col_ref, obs_ref, count_out, obs_out):
    steps, rows, cols = obs_out.shape
    own_rows = rows - 2 * HALO
    own_cols = cols - 128
    gx, gy, wx, wy = place_ref[0], place_ref[1], place_ref[2], place_ref[3]
    per = row_ref.shape[0] // (wx * wy)
    zero = jnp.zeros((8, cols), F32)

    def clear(i, c):
        r = pl.multiple_of(i * 8, 8)
        count_out[pl.ds(r, 8), :] = zero
        for k in range(steps):
            obs_out[k, pl.ds(r, 8), :] = zero
        return c

    lax.fori_loop(0, rows // 8, clear, 0)
    sub = row_iota((8, 128))
    lane = lax.broadcasted_iota(I32, (8, 128), 1)

    for dx in (-1, 0, 1):
        for dy in (-1, 0, 1):
            tx = gx + dx
            ty = gy + dy
            inside = (tx >= 0) & (tx < wx) & (ty >= 0) & (ty < wy)
            first = jnp.where(inside, (tx * wy + ty) * per, 0)

            def one(g, c, first=first, inside=inside):
                r = row_ref[first + g] - gx * own_rows + HALO
                q = col_ref[first + g] - gy * own_cols
                ok = inside & (r >= 0) & (r < rows) & (q >= -HALO) & (q < own_cols + HALO)
                q = jnp.where(q < 0, q + cols, q)

                @pl.when(ok)
                def _():
                    rb = pl.multiple_of(r // 8 * 8, 8)
                    cb = pl.multiple_of(q // 128 * 128, 128)
                    hit = (sub == r % 8) & (lane == q % 128)
                    at = (pl.ds(rb, 8), pl.ds(cb, 128))
                    count_out[at] = count_out[at] + jnp.where(hit, 1.0, 0.0)
                    for k in range(steps):
                        at_k = (k,) + at
                        obs_out[at_k] = obs_out[at_k] + jnp.where(hit, obs_ref[k, first + g], 0.0)

                return c

            lax.fori_loop(0, per, one, 0)


def face(f, s, sn, dd, rr, ww):
    x = dd + 0.5 * (s + sn)
    total = jnp.maximum(x, min_depth)
    diff = sn - s
    push = (-wave_gain) * (total * diff)
    if f is not None:
        push = push + f
    t = push * push + speed_floor
    rs = lax.rsqrt(t)
    log = jnp.log(total)
    rw = rr * jnp.exp2(log * (-7.0 / 3.0 / LN2))
    z = rw * (t * rs)
    inv = 1.0 / (1.0 + z)
    wi = ww * inv
    flux = wi * push
    a = wi * inv * (1.0 + speed_floor * (rw * rs))
    depth_part = (flux * inv) * (z * jnp.exp2(log * (-1.0 / LN2))) * (7.0 / 3.0)
    ga = wave_gain * a
    half = jnp.where(x > min_depth, 0.5, jnp.where(x == min_depth, 0.25, 0.0))
    u = half * (depth_part - ga * diff)
    v = ga * total
    return flux, a, u + v, u - v


def merge_rows(tiles):
    sub = row_iota((8, 128))
    for width in (1, 2, 4):
        low = (sub & width) == 0
        tiles = [
            jnp.where(low, p, q) + pltpu.roll(jnp.where(low, q, p), width, 0)
            for p, q in zip(tiles[0::2], tiles[1::2])
        ]
    return tiles[0]


def solve_kernel(
    place_ref, grow_ref, gcol_ref, block_ref,
    eta_ref, east_ref, west_ref, north_ref, south_ref,
    wet, dde, dds, rre, rrs, wwe, wws,
    count_hbm, obs_hbm, recv_hbm,
    final_ref, adj_ref, back_ref,
    surf, fe, fs, ae, pe, qe, as_, ps, qs, adj, ce, cs,
    count, obs, recv, parts, reads, sems,
):
    steps, rows, cols = obs.shape
    own_rows, own_cols = eta_ref.shape
    copies = [
        pltpu.make_async_copy(count_hbm, count, sems.at[0]),
        pltpu.make_async_copy(obs_hbm, obs, sems.at[1]),
        pltpu.make_async_copy(recv_hbm, recv, sems.at[2]),
    ]
    for c in copies:
        c.start()
    start = surf.at[0]
    assemble(start, 0, eta_ref, east_ref, west_ref, north_ref, south_ref)
    sub = row_iota((8, cols))
    last = sub == 7
    firstrow = sub == 0
    blocks = rows // 8

    def nxt(i):
        return pl.multiple_of(jnp.minimum(i * 8 + 8, rows - 8), 8)

    for k in range(steps):

        def forward(i, carry, k=k):
            s, s_up, f_down = carry
            r = pl.multiple_of(i * 8, 8)
            here = pl.ds(r, 8)
            sn = surf[k, pl.ds(nxt(i), 8), :]
            sn_up = pltpu.roll(sn, 7, 0)
            s_south = jnp.where(last, sn_up, s_up)
            s_east = pltpu.roll(s, cols - 1, 1)
            old_e = None if k == 0 else fe[here, :]
            old_s = None if k == 0 else fs[here, :]
            flux, a, p, q = face(old_e, s, s_east, dde[here, :], rre[here, :], wwe[here, :])
            fe[here, :] = flux
            if k > 0:
                ae[k - 1, here, :] = a
            pe[k, here, :] = p
            qe[k, here, :] = q
            div = flux - pltpu.roll(flux, 1, 1)
            flux, a, p, q = face(old_s, s, s_south, dds[here, :], rrs[here, :], wws[here, :])
            fs[here, :] = flux
            if k > 0:
                as_[k - 1, here, :] = a
            ps[k, here, :] = p
            qs[k, here, :] = q
            down = pltpu.roll(flux, 1, 0)
            div = div + (flux - jnp.where(firstrow, f_down, down))
            surf[k + 1, here, :] = wet[here, :] * (s - mass_gain * div)
            return sn, sn_up, down

        s0 = surf[k, 0:8, :]
        lax.fori_loop(
            0, blocks, forward, (s0, pltpu.roll(s0, 7, 0), jnp.zeros((8, cols), F32))
        )

    final_ref[...] = surf[steps, HALO : HALO + own_rows, 0:own_cols]

    gx, gy = place_ref[0], place_ref[1]
    lane8 = lax.broadcasted_iota(I32, (8, 128), 1)
    sub8 = row_iota((8, 128))
    per = grow_ref.shape[0] // (place_ref[2] * place_ref[3])
    per_tile = reads.shape[0] // steps
    first = (gx * place_ref[3] + gy) * per
    for g0 in range(0, per_tile, 8):
        spots = []
        for g in range(g0, g0 + 8):
            r = jnp.clip(grow_ref[first + g] - gx * own_rows, 0, own_rows - 1) + HALO
            q = jnp.clip(gcol_ref[first + g] - gy * own_cols, 0, own_cols - 1)
            at = (
                pl.ds(pl.multiple_of(r // 8 * 8, 8), 8),
                pl.ds(pl.multiple_of(q // 128 * 128, 128), 128),
            )
            spots.append((at, (sub8 == r % 8) & (lane8 == q % 128)))
        for k in range(steps):
            picked = [jnp.where(hit, surf[(k + 1,) + at], 0.0) for at, hit in spots]
            reads[k * per_tile + g0 : k * per_tile + g0 + 8, :] = merge_rows(picked)
    values = jnp.sum(reads[...], axis=1, keepdims=True)
    spots = row_iota(reads.shape) + SLOTS == lax.broadcasted_iota(I32, reads.shape, 1)
    reading_row = jnp.sum(jnp.where(spots, values, 0.0), axis=0, keepdims=True)

    for c in copies:
        c.wait()

    for k in reversed(range(steps)):

        def seeded(value, at, k):
            seed = count[at, :] * surf[k + 1, at, :] - obs[k, at, :]
            return seed if value is None else value + seed

        def b_of(r, k=k):
            at = pl.ds(r, 8)
            a = seeded(None, at, k) if k == steps - 1 else adj[at, :]
            return wet[at, :] * a

        def backward(i, carry, k=k):
            b, b_up, x_down = carry
            r = pl.multiple_of(i * 8, 8)
            here = pl.ds(r, 8)
            bn = b_of(nxt(i))
            bn_up = pltpu.roll(bn, 7, 0)
            b_south = jnp.where(last, bn_up, b_up)
            b_east = pltpu.roll(b, cols - 1, 1)
            ge = mass_gain * (b_east - b)
            gs = mass_gain * (b_south - b)
            if k < steps - 1:
                ge = ge + ce[here, :]
                gs = gs + cs[here, :]
            if k > 0:
                ce[here, :] = ge * ae[k - 1, here, :]
                cs[here, :] = gs * as_[k - 1, here, :]
            xe = ge * qe[k, here, :]
            xs = gs * qs[k, here, :]
            down = pltpu.roll(xs, 1, 0)
            out = b + ge * pe[k, here, :] + pltpu.roll(xe, 1, 1)
            out = out + gs * ps[k, here, :] + jnp.where(firstrow, x_down, down)
            if k > 0:
                out = seeded(out, here, k - 1)
            adj[here, :] = out
            return bn, bn_up, down

        b0 = b_of(0)
        lax.fori_loop(
            0, blocks, backward, (b0, pltpu.roll(b0, 7, 0), jnp.zeros((8, cols), F32))
        )

    adj_ref[...] = adj[HALO : HALO + own_rows, 0:own_cols]

    across = own_cols // 128
    tiles = recv.shape[0] // CHUNK

    def sens(i, c):
        for j in range(SLOTS):
            products = []
            for u in range(8):
                t = i * 8 + u
                b = block_ref[t * SLOTS + j]
                rb = pl.multiple_of(b // across * 8 + HALO, 8)
                cb = pl.multiple_of(b % across * 128, 128)
                at = (pl.ds(rb, 8), pl.ds(cb, 128))
                products.append(
                    (adj[at] * wet[at]) * recv[pl.ds(t * CHUNK + 8 * j, 8), :]
                )
            parts[j, pl.ds(pl.multiple_of(i * 8, 8), 8), :] = merge_rows(products)
        return c

    lax.fori_loop(0, tiles // 8, sens, 0)
    lanes = lax.broadcasted_iota(I32, (tiles, 128), 1)
    out = jnp.broadcast_to(reading_row, (tiles, 128))
    for j in range(SLOTS):
        out = jnp.where(lanes == j, jnp.sum(parts[j], axis=1, keepdims=True), out)
    back_ref[...] = out


def body(
    ocean_depth,
    wet_mask,
    manning,
    fault_slip,
    pattern,
    foot_tile,
    foot_block,
    gauge_row,
    gauge_col,
    observed,
):
    rows_here, cols_here = ocean_depth.shape
    steps, gauges = observed.shape
    width_x = lax.axis_size("gx")
    width_y = lax.axis_size("gy")
    devices = width_x * width_y
    entries = pattern.shape[0]
    faults = fault_slip.shape[0]
    per_fault = entries // faults
    per_tile = gauges // devices
    both = ("gx", "gy")
    rows, cols = rows_here + 2 * HALO, cols_here + 128
    f = jax.ShapeDtypeStruct

    target = foot_tile[:, 0]
    order = jnp.arange(entries, dtype=I32)
    earlier = (target[:, None] == target[None, :]) & (order[:, None] > order[None, :])
    rank = jnp.sum(earlier.astype(I32), axis=1)
    hot_tile = (jnp.arange(devices, dtype=I32)[:, None] == target[None, :]).astype(jnp.bfloat16)
    lane = jnp.arange(128, dtype=I32)[None, :]
    hot_slot = jnp.where(lane == rank[:, None], foot_block[:, None] + 1, 0)
    hot_fault = jnp.where(lane == rank[:, None] + 8, order[:, None] // per_fault + 1, 0)
    table = jnp.dot(
        hot_tile, (hot_slot + hot_fault).astype(jnp.bfloat16), preferred_element_type=F32
    )
    packed = pl.pallas_call(
        pack_kernel,
        out_shape=f((devices * CHUNK, 128), F32),
        in_specs=[smem(), smem(), vmem(), vmem()],
        out_specs=vmem(),
        name="pack",
    )(target * CHUNK + 8 * rank, fault_slip, pattern, table)
    recv = lax.all_to_all(packed.reshape(-1), both, split_axis=0, concat_axis=0, tiled=True)
    block_index = jnp.maximum(
        recv.reshape(devices, CHUNK * 128)[:, 4096 : 4096 + SLOTS].astype(I32) - 1, 0
    ).reshape(-1)
    recv = recv.reshape(devices * CHUNK, 128)

    west, east = pl.pallas_call(
        static_edge_kernel,
        out_shape=[f((24, rows_here), F32)] * 2,
        in_specs=[vmem()] * 3,
        out_specs=[vmem()] * 2,
        name="static_edges",
    )(ocean_depth, wet_mask, manning)
    from_east = shifted(west, "gy", -1)
    from_west = shifted(east, "gy", 1)
    top, bottom = pl.pallas_call(
        rim_kernel,
        out_shape=[f((24, cols), F32)] * 2,
        in_specs=[vmem()] * 5,
        out_specs=[vmem()] * 2,
        name="static_rims",
    )(ocean_depth, wet_mask, manning, from_east, from_west)
    from_south = shifted(top, "gx", -1)
    from_north = shifted(bottom, "gx", 1)
    grid = f((rows, cols), F32)
    faces = pl.pallas_call(
        face_static_kernel,
        out_shape=[grid] * 7,
        in_specs=[vmem()] * 7,
        out_specs=[vmem()] * 7,
        scratch_shapes=[pltpu.VMEM((rows, cols), F32)] * 2,
        name="faces",
    )(ocean_depth, wet_mask, manning, from_east, from_west, from_north, from_south)
    place = jnp.stack(
        [lax.axis_index("gx"), lax.axis_index("gy"), jnp.int32(width_x), jnp.int32(width_y)]
    ).astype(I32)
    count, obs = pl.pallas_call(
        gauge_kernel,
        out_shape=[grid, f((steps, rows, cols), F32)],
        in_specs=[smem()] * 4,
        out_specs=[vmem()] * 2,
        name="gauges",
    )(place, gauge_row, gauge_col, observed)

    eta, west, east = pl.pallas_call(
        scatter_kernel,
        out_shape=[f((rows_here, cols_here), F32)] + [f((8, rows_here), F32)] * 2,
        in_specs=[smem(), vmem(), vmem()],
        out_specs=[vmem()] * 3,
        scratch_shapes=[pltpu.VMEM((rows_here * cols_here // 1024, 8, 128), F32)] * SLOTS,
        name="scatter",
    )(block_index, recv, wet_mask)
    from_east = shifted(west, "gy", -1)
    from_west = shifted(east, "gy", 1)
    top, bottom = pl.pallas_call(
        rim_kernel,
        out_shape=[f((8, cols), F32)] * 2,
        in_specs=[vmem()] * 3,
        out_specs=[vmem()] * 2,
        name="eta_rims",
    )(eta, from_east, from_west)
    from_south = shifted(top, "gx", -1)
    from_north = shifted(bottom, "gx", 1)

    tile = f((rows_here, cols_here), F32)
    scratch = pltpu.VMEM((rows, cols), F32)
    final, adjoint, back = pl.pallas_call(
        solve_kernel,
        out_shape=[tile, tile, f((devices, 128), F32)],
        in_specs=[smem()] * 4 + [vmem()] * 12 + [hbm()] * 3,
        out_specs=[vmem()] * 3,
        scratch_shapes=[
            pltpu.VMEM((steps + 1, rows, cols), F32),
            scratch,
            scratch,
            pltpu.VMEM((steps - 1, rows, cols), F32),
            pltpu.VMEM((steps, rows, cols), F32),
            pltpu.VMEM((steps, rows, cols), F32),
            pltpu.VMEM((steps - 1, rows, cols), F32),
            pltpu.VMEM((steps, rows, cols), F32),
            pltpu.VMEM((steps, rows, cols), F32),
            scratch,
            scratch,
            scratch,
            scratch,
            pltpu.VMEM((steps, rows, cols), F32),
            pltpu.VMEM((devices * CHUNK, 128), F32),
            pltpu.VMEM((SLOTS, devices, 128), F32),
            pltpu.VMEM((steps * per_tile, 128), F32),
            pltpu.SemaphoreType.DMA((3,)),
        ],
        name="solve",
    )(
        place, gauge_row, gauge_col, block_index,
        eta, from_east, from_west, from_north, from_south,
        *faces, count, obs, recv,
    )
    returned = lax.all_to_all(back, both, split_axis=0, concat_axis=0, tiled=True)
    readings = (
        returned[:, SLOTS : SLOTS + steps * per_tile]
        .reshape(devices, steps, per_tile)
        .transpose(1, 0, 2)
        .reshape(steps, gauges)
    )
    fault_of = table[:, 8 : 8 + SLOTS].astype(I32) - 1
    mine = fault_of[:, :, None] == jnp.arange(faults, dtype=I32)[None, None, :]
    grad_slip = (
        jnp.sum(jnp.where(mine, returned[:, :SLOTS, None], 0.0), axis=(0, 1)) / fault_slip
    )
    return (final, readings, adjoint, grad_slip)


def solution(mesh):
    placed = (
        P("gx", "gy"),
        P("gx", "gy"),
        P("gx", "gy"),
        P(("gx", "gy")),
        P(("gx", "gy"), None, None),
        P(("gx", "gy"), None),
        P(("gx", "gy")),
        P(),
        P(),
        P(),
    )
    return jax.shard_map(
        body,
        mesh=mesh,
        in_specs=placed,
        out_specs=(P("gx", "gy"), P(), P("gx", "gy"), P(("gx", "gy"))),
        check_vma=False,
    )
```

```python
import math

import jax
import jax.numpy as jnp
from jax import lax
from jax.experimental import pallas as pl
from jax.experimental.pallas import tpu as pltpu
from jax.sharding import PartitionSpec as P

wave_gain = 0.2
mass_gain = 0.2
min_depth = 0.25
speed_floor = 0.01

HALO = 8
CHUNK = 33
SLOTS = 4
LN2 = math.log(2.0)
PUSH = -0.5 * wave_gain
assert abs(PUSH * PUSH - speed_floor) < 1e-12
ROUGH_SCALE = 0.5 * abs(PUSH) * 2.0 ** (7.0 / 3.0)
F32 = jnp.float32
I32 = jnp.int32


def vmem():
    return pl.BlockSpec(memory_space=pltpu.VMEM)


def smem():
    return pl.BlockSpec(memory_space=pltpu.SMEM)


def hbm():
    return pl.BlockSpec(memory_space=pl.ANY)


def shifted(shard, axis, by):
    devices = lax.axis_size(axis)
    pairs = [(i, i + by) for i in range(devices) if 0 <= i + by < devices]
    return lax.ppermute(shard, axis, pairs)


def pack_kernel(
    slip_ref, tile_ref, block_ref, pattern_hbm, out_ref, table_ref, pattern, row_v, row_s, sems
):
    load = pltpu.make_async_copy(pattern_hbm, pattern, sems.at[0])
    load.start()
    rows = out_ref.shape[0]
    tiles = rows // CHUNK
    entries = tile_ref.shape[1]
    faults = slip_ref.shape[0]
    per_fault = entries // faults
    tile_row = tile_ref[...]
    tile_f = tile_row.astype(F32)
    tile_col = jnp.broadcast_to(tile_f, (128, entries)).T
    here = lax.broadcasted_iota(I32, (entries, 128), 0)
    ranks = []
    for q in range(entries // 128):
        there = lax.broadcasted_iota(I32, (entries, 128), 1) + q * 128
        same = (tile_col == tile_f[:, q * 128 : q * 128 + 128]) & (here < there)
        ranks.append(jnp.sum(jnp.where(same, 1.0, 0.0), axis=0, keepdims=True))
    rank = jnp.concatenate(ranks, axis=1).astype(I32)
    row_v[...] = tile_row * CHUNK + rank * 8
    place_rows = pltpu.make_async_copy(row_v, row_s, sems.at[1])
    place_rows.start()
    fault = lax.broadcasted_iota(I32, (1, entries), 1) // per_fault
    slot = lax.broadcasted_iota(I32, (128, entries), 0)
    facts = jnp.where(slot == rank, block_ref[...], 0) + jnp.where(slot == rank + 8, fault + 1, 0)
    hot = jnp.where(lax.broadcasted_iota(I32, (tiles, entries), 0) == tile_row, 1.0, 0.0)
    table_ref[...] = lax.dot_general(
        hot.astype(jnp.bfloat16),
        facts.astype(F32).astype(jnp.bfloat16),
        (((1,), (1,)), ((), ())),
        preferred_element_type=F32,
    )
    zero = jnp.zeros((8, 128), F32)

    def clear(i, c):
        out_ref[pl.ds(pl.multiple_of(i * 8, 8), 8), :] = zero
        return c

    lax.fori_loop(0, rows // 8, clear, 0, unroll=16)
    for t in range(tiles):
        out_ref[t * CHUNK + 32 : t * CHUNK + 33, :] = table_ref[t : t + 1, :]
    place_rows.wait()
    load.wait()

    def place(s, c):
        slip = slip_ref[s]
        for j in range(per_fault):
            i = s * per_fault + j
            out_ref[pl.ds(row_s[0, i], 8), :] = pattern[i] * slip
        return c

    lax.fori_loop(0, faults, place, 0)


def edges_of(first, last):
    lane = lax.broadcasted_iota(I32, first.shape, 1)
    both = jnp.where(lane < 64, first, last).T
    return both[0:8], both[120:128]


def side_block(east, west):
    rows = east.shape[1]
    gap = jnp.zeros((128 - 16, rows), F32)
    return jnp.concatenate([east, gap, west], axis=0).T


def scatter_kernel(
    meta_hbm, recv_ref, wet_ref, after_a, after_b, eta_ref, west_ref, east_ref, block_ref, meta, sem, *acc
):
    del after_a, after_b
    load = pltpu.make_async_copy(meta_hbm.at[:, :, pl.ds(8 * SLOTS * 128, 128)], meta, sem)
    load.start()
    tiles = recv_ref.shape[0] // CHUNK
    rows, cols = eta_ref.shape
    across = cols // 128
    zero = jnp.zeros((8, 128), F32)

    def clear(i, c):
        for a in acc:
            a[i] = zero
        return c

    lax.fori_loop(0, acc[0].shape[0], clear, 0, unroll=8)
    load.wait()

    def add(t, c):
        for j in range(SLOTS):
            b = meta[t, 0, j].astype(I32)
            block_ref[t * SLOTS + j] = b
            acc[j][b] = acc[j][b] + recv_ref[pl.ds(t * CHUNK + 8 * j, 8), :]
        return c

    lax.fori_loop(0, tiles, add, 0, unroll=4)

    def merge(i, c):
        r = pl.multiple_of(i * 8, 8)
        for q in range(across):
            b = i * across + q
            total = (acc[0][b] + acc[1][b]) + (acc[2][b] + acc[3][b])
            wet = wet_ref[pl.ds(r, 8), q * 128 : q * 128 + 128].astype(F32)
            eta_ref[pl.ds(r, 8), q * 128 : q * 128 + 128] = total * wet
        return c

    lax.fori_loop(0, rows // 8, merge, 0, unroll=2)
    west, east = edges_of(eta_ref[:, 0:128], eta_ref[:, cols - 128 : cols])
    west_ref[...] = west
    east_ref[...] = east


def static_edge_kernel(depth_ref, wet_ref, fric_ref, west_ref, east_ref):
    cols = depth_ref.shape[1]
    for n, ref in enumerate((depth_ref, wet_ref, fric_ref)):
        west, east = edges_of(ref[:, 0:128].astype(F32), ref[:, cols - 128 : cols].astype(F32))
        west_ref[8 * n : 8 * n + 8] = west
        east_ref[8 * n : 8 * n + 8] = east


def rim_kernel(*refs):
    fields = refs[:-4]
    east_ref, west_ref, top_ref, bottom_ref = refs[-4:]
    rows, cols = fields[0].shape
    for n, ref in enumerate(fields):
        block = side_block(east_ref[8 * n : 8 * n + 8], west_ref[8 * n : 8 * n + 8])
        top_ref[8 * n : 8 * n + 8, 0:cols] = ref[0:8, :].astype(F32)
        top_ref[8 * n : 8 * n + 8, cols:] = block[0:8]
        bottom_ref[8 * n : 8 * n + 8, 0:cols] = ref[rows - 8 : rows, :].astype(F32)
        bottom_ref[8 * n : 8 * n + 8, cols:] = block[rows - 8 : rows]


def assemble(out, n, ref, east_ref, west_ref, north_ref, south_ref):
    rows, cols = ref.shape
    out[0:8, :] = north_ref[8 * n : 8 * n + 8]
    out[8 : 8 + rows, 0:cols] = ref[...].astype(F32)
    out[8 : 8 + rows, cols:] = side_block(
        east_ref[8 * n : 8 * n + 8], west_ref[8 * n : 8 * n + 8]
    )
    out[8 + rows : 16 + rows, :] = south_ref[8 * n : 8 * n + 8]


def row_iota(shape):
    return lax.broadcasted_iota(I32, shape, 0)


def face_static_kernel(
    depth_ref, wet_ref, fric_ref, east_ref, west_ref, north_ref, south_ref,
    wet_out, dde, dds, rre, rrs, wwe, wws, depth_x, fric_x,
):
    halos = (east_ref, west_ref, north_ref, south_ref)
    assemble(depth_x, 0, depth_ref, *halos)
    assemble(wet_out, 1, wet_ref, *halos)
    assemble(fric_x, 2, fric_ref, *halos)
    rows, cols = depth_x.shape
    last = row_iota((8, cols)) == 7

    def step(i, c):
        r = pl.multiple_of(i * 8, 8)
        n = pl.multiple_of(jnp.minimum(r + 8, rows - 8), 8)
        for src, e_out, s_out, scale in (
            (depth_x, dde, dds, 1.0),
            (fric_x, rre, rrs, ROUGH_SCALE),
            (wet_out, wwe, wws, None),
        ):
            here = src[pl.ds(r, 8), :]
            nxt = src[pl.ds(n, 8), :]
            east = pltpu.roll(here, cols - 1, 1)
            south = jnp.where(last, pltpu.roll(nxt, 7, 0), pltpu.roll(here, 7, 0))
            if scale is not None:
                e_out[pl.ds(r, 8), :] = scale * (here + east)
                s_out[pl.ds(r, 8), :] = scale * (here + south)
            else:
                e_out[pl.ds(r, 8), :] = here * east
                s_out[pl.ds(r, 8), :] = here * south
        return c

    lax.fori_loop(0, rows // 8, step, 0)


def gauge_kernel(place_ref, row_ref, col_ref, obs_ref, count_out, obs_out):
    steps, rows, cols = obs_out.shape
    own_rows = rows - 2 * HALO
    own_cols = cols - 128
    gx, gy, wx, wy = place_ref[0], place_ref[1], place_ref[2], place_ref[3]
    per = row_ref.shape[0] // (wx * wy)
    zero = jnp.zeros((8, cols), F32)

    def clear(i, c):
        r = pl.multiple_of(i * 8, 8)
        count_out[pl.ds(r, 8), :] = zero
        for k in range(steps):
            obs_out[k, pl.ds(r, 8), :] = zero
        return c

    lax.fori_loop(0, rows // 8, clear, 0)
    sub = row_iota((8, 128))
    lane = lax.broadcasted_iota(I32, (8, 128), 1)

    for dx in (-1, 0, 1):
        for dy in (-1, 0, 1):
            tx = gx + dx
            ty = gy + dy
            inside = (tx >= 0) & (tx < wx) & (ty >= 0) & (ty < wy)
            first = jnp.where(inside, (tx * wy + ty) * per, 0)

            def one(g, c, first=first, inside=inside):
                r = row_ref[first + g] - gx * own_rows + HALO
                q = col_ref[first + g] - gy * own_cols
                ok = inside & (r >= 0) & (r < rows) & (q >= -HALO) & (q < own_cols + HALO)
                q = jnp.where(q < 0, q + cols, q)

                @pl.when(ok)
                def _():
                    rb = pl.multiple_of(r // 8 * 8, 8)
                    cb = pl.multiple_of(q // 128 * 128, 128)
                    hit = (sub == r % 8) & (lane == q % 128)
                    at = (pl.ds(rb, 8), pl.ds(cb, 128))
                    count_out[at] = count_out[at] + jnp.where(hit, 1.0, 0.0)
                    for k in range(steps):
                        at_k = (k,) + at
                        obs_out[at_k] = obs_out[at_k] + jnp.where(hit, obs_ref[k, first + g], 0.0)

                return c

            lax.fori_loop(0, per, one, 0)


def face(f, s, sn, dd, rr, ww):
    x = dd + (s + sn)
    total = jnp.maximum(x, 2.0 * min_depth)
    diff = sn - s
    push = total * diff
    if f is not None:
        push = push + f
    t = push * push + 1.0
    y = (rr * jnp.exp2(jnp.log(total) * (-7.0 / 3.0 / LN2))) * lax.rsqrt(t)
    inv = 1.0 / (t * y + 1.0)
    wi = ww * inv
    flux = wi * push
    a = (wi * inv) * (y + 1.0)
    depth_part = (flux - flux * inv) * ((7.0 / 3.0) / total)
    share = jnp.where(
        x > 2.0 * min_depth, 1.0, jnp.where(x == 2.0 * min_depth, 0.5, 0.0)
    )
    u = share * (depth_part + a * diff)
    v = a * total
    return flux, a, u + v, u - v


def merge_rows(tiles):
    sub = row_iota((8, 128))
    for width in (1, 2, 4):
        low = (sub & width) == 0
        tiles = [
            jnp.where(low, p, q) + pltpu.roll(jnp.where(low, q, p), width, 0)
            for p, q in zip(tiles[0::2], tiles[1::2])
        ]
    return tiles[0]


def solve_kernel(
    place_ref, grow_ref, gcol_ref, block_ref,
    eta_ref, east_ref, west_ref, north_ref, south_ref,
    wet, dde, dds, rre, rrs, wwe, wws,
    count_hbm, obs_hbm, recv_hbm,
    final_ref, adj_ref, back_ref,
    surf, fe, fs, ae, pe, qe, as_, ps, qs, adj, ce, cs, grads,
    count, obs, recv, parts, reads, sems,
):
    steps, rows, cols = obs.shape
    own_rows, own_cols = eta_ref.shape
    copies = [
        pltpu.make_async_copy(count_hbm, count, sems.at[0]),
        pltpu.make_async_copy(obs_hbm, obs, sems.at[1]),
        pltpu.make_async_copy(recv_hbm, recv, sems.at[2]),
    ]
    for c in copies:
        c.start()
    start = surf.at[0]
    assemble(start, 0, eta_ref, east_ref, west_ref, north_ref, south_ref)
    sub = row_iota((8, cols))
    last = sub == 7
    firstrow = sub == 0
    blocks = rows // 8
    across = own_cols // 128

    def nxt(i):
        return pl.multiple_of(jnp.minimum(i * 8 + 8, rows - 8), 8)

    for k in range(steps):

        def forward(i, carry, k=k):
            s, s_up, f_down = carry
            r = pl.multiple_of(i * 8, 8)
            here = pl.ds(r, 8)
            sn = surf[k, pl.ds(nxt(i), 8), :]
            sn_up = pltpu.roll(sn, 7, 0)
            s_south = jnp.where(last, sn_up, s_up)
            s_east = pltpu.roll(s, cols - 1, 1)
            old_e = None if k == 0 else fe[here, :]
            old_s = None if k == 0 else fs[here, :]
            flux, a, p, q = face(old_e, s, s_east, dde[here, :], rre[here, :], wwe[here, :])
            fe[here, :] = flux
            if k > 0:
                ae[k - 1, here, :] = a
            pe[k, here, :] = p
            qe[k, here, :] = q
            div = flux - pltpu.roll(flux, 1, 1)
            flux, a, p, q = face(old_s, s, s_south, dds[here, :], rrs[here, :], wws[here, :])
            fs[here, :] = flux
            if k > 0:
                as_[k - 1, here, :] = a
            ps[k, here, :] = p
            qs[k, here, :] = q
            down = pltpu.roll(flux, 1, 0)
            div = div + (flux - jnp.where(firstrow, f_down, down))
            surf[k + 1, here, :] = wet[here, :] * (s - (mass_gain * PUSH) * div)
            return sn, sn_up, down

        s0 = surf[k, 0:8, :]
        lax.fori_loop(
            0, blocks, forward, (s0, pltpu.roll(s0, 7, 0), jnp.zeros((8, cols), F32))
        )

    final_ref[...] = surf[steps, HALO : HALO + own_rows, 0:own_cols]

    gx, gy = place_ref[0], place_ref[1]
    lane8 = lax.broadcasted_iota(I32, (8, 128), 1)
    sub8 = row_iota((8, 128))
    per = grow_ref.shape[0] // (place_ref[2] * place_ref[3])
    per_tile = reads.shape[0] // steps
    first = (gx * place_ref[3] + gy) * per
    for g0 in range(0, per_tile, 8):
        spots = []
        for g in range(g0, g0 + 8):
            r = jnp.clip(grow_ref[first + g] - gx * own_rows, 0, own_rows - 1) + HALO
            q = jnp.clip(gcol_ref[first + g] - gy * own_cols, 0, own_cols - 1)
            at = (
                pl.ds(pl.multiple_of(r // 8 * 8, 8), 8),
                pl.ds(pl.multiple_of(q // 128 * 128, 128), 128),
            )
            spots.append((at, (sub8 == r % 8) & (lane8 == q % 128)))
        for k in range(steps):
            picked = [jnp.where(hit, surf[(k + 1,) + at], 0.0) for at, hit in spots]
            reads[k * per_tile + g0 : k * per_tile + g0 + 8, :] = merge_rows(picked)
    values = jnp.sum(reads[...], axis=1, keepdims=True)
    spots = row_iota(reads.shape) + SLOTS == lax.broadcasted_iota(I32, reads.shape, 1)
    reading_row = jnp.sum(jnp.where(spots, values, 0.0), axis=0, keepdims=True)

    for c in copies:
        c.wait()

    for k in reversed(range(steps)):

        def seeded(value, at, k):
            seed = count[at, :] * surf[k + 1, at, :] - obs[k, at, :]
            return seed if value is None else value + seed

        def b_of(r, k=k):
            at = pl.ds(r, 8)
            a = seeded(None, at, k) if k == steps - 1 else adj[at, :]
            return wet[at, :] * a

        def backward(i, carry, k=k):
            b, b_up, x_down = carry
            r = pl.multiple_of(i * 8, 8)
            here = pl.ds(r, 8)
            bn = b_of(nxt(i))
            bn_up = pltpu.roll(bn, 7, 0)
            b_south = jnp.where(last, bn_up, b_up)
            b_east = pltpu.roll(b, cols - 1, 1)
            ge = (mass_gain * PUSH) * (b_east - b)
            gs = (mass_gain * PUSH) * (b_south - b)
            if k < steps - 1:
                ge = ge + ce[here, :]
                gs = gs + cs[here, :]
            if k > 0:
                ce[here, :] = ge * ae[k - 1, here, :]
                cs[here, :] = gs * as_[k - 1, here, :]
            xe = ge * pe[k, here, :]
            xs = gs * ps[k, here, :]
            down = pltpu.roll(xs, 1, 0)
            out = b + ge * qe[k, here, :] + pltpu.roll(xe, 1, 1)
            out = out + gs * qs[k, here, :] + jnp.where(firstrow, x_down, down)
            if k > 0:
                out = seeded(out, here, k - 1)
            adj[here, :] = out
            if k == 0:
                scaled = out * wet[here, :]
                for q in range(across):
                    grads[i * across + q] = scaled[:, q * 128 : q * 128 + 128]
            return bn, bn_up, down

        b0 = b_of(0)
        lax.fori_loop(
            0, blocks, backward, unroll=2, init_val=(b0, pltpu.roll(b0, 7, 0), jnp.zeros((8, cols), F32))
        )

    adj_ref[...] = adj[HALO : HALO + own_rows, 0:own_cols]

    tiles = recv.shape[0] // CHUNK

    def sens(i, c):
        for j in range(SLOTS):
            products = []
            for u in range(8):
                t = i * 8 + u
                b = block_ref[t * SLOTS + j] + HALO // 8 * across
                products.append(grads[b] * recv[pl.ds(t * CHUNK + 8 * j, 8), :])
            parts[j, pl.ds(pl.multiple_of(i * 8, 8), 8), :] = merge_rows(products)
        return c

    lax.fori_loop(0, tiles // 8, sens, 0)
    lanes = lax.broadcasted_iota(I32, (tiles, 128), 1)
    out = jnp.broadcast_to(reading_row, (tiles, 128))
    for j in range(SLOTS):
        out = jnp.where(lanes == j, jnp.sum(parts[j], axis=1, keepdims=True), out)
    back_ref[...] = out


def body(
    ocean_depth,
    wet_mask,
    manning,
    fault_slip,
    pattern,
    foot_tile,
    foot_block,
    gauge_row,
    gauge_col,
    observed,
):
    rows_here, cols_here = ocean_depth.shape
    steps, gauges = observed.shape
    width_x = lax.axis_size("gx")
    width_y = lax.axis_size("gy")
    devices = width_x * width_y
    entries = pattern.shape[0]
    faults = fault_slip.shape[0]
    per_fault = entries // faults
    per_tile = gauges // devices
    both = ("gx", "gy")
    rows, cols = rows_here + 2 * HALO, cols_here + 128
    f = jax.ShapeDtypeStruct

    packed, table = pl.pallas_call(
        pack_kernel,
        out_shape=[f((devices * CHUNK, 128), F32), f((devices, 128), F32)],
        in_specs=[smem(), vmem(), vmem(), hbm()],
        out_specs=[vmem()] * 2,
        scratch_shapes=[
            pltpu.VMEM(pattern.shape, F32),
            pltpu.VMEM((1, entries), I32),
            pltpu.SMEM((1, entries), I32),
            pltpu.SemaphoreType.DMA((2,)),
        ],
        name="pack",
    )(fault_slip, foot_tile.reshape(1, entries), foot_block.reshape(1, entries), pattern)
    recv_flat = lax.all_to_all(packed.reshape(-1), both, split_axis=0, concat_axis=0, tiled=True)
    recv = recv_flat.reshape(devices * CHUNK, 128)

    west, east = pl.pallas_call(
        static_edge_kernel,
        out_shape=[f((24, rows_here), F32)] * 2,
        in_specs=[vmem()] * 3,
        out_specs=[vmem()] * 2,
        name="static_edges",
    )(ocean_depth, wet_mask, manning)
    from_east = shifted(west, "gy", -1)
    from_west = shifted(east, "gy", 1)
    top, bottom = pl.pallas_call(
        rim_kernel,
        out_shape=[f((24, cols), F32)] * 2,
        in_specs=[vmem()] * 5,
        out_specs=[vmem()] * 2,
        name="static_rims",
    )(ocean_depth, wet_mask, manning, from_east, from_west)
    from_south = shifted(top, "gx", -1)
    from_north = shifted(bottom, "gx", 1)
    grid = f((rows, cols), F32)
    faces = pl.pallas_call(
        face_static_kernel,
        out_shape=[grid] * 7,
        in_specs=[vmem()] * 7,
        out_specs=[vmem()] * 7,
        scratch_shapes=[pltpu.VMEM((rows, cols), F32)] * 2,
        name="faces",
    )(ocean_depth, wet_mask, manning, from_east, from_west, from_north, from_south)
    place = jnp.stack(
        [lax.axis_index("gx"), lax.axis_index("gy"), jnp.int32(width_x), jnp.int32(width_y)]
    ).astype(I32)
    count, obs = pl.pallas_call(
        gauge_kernel,
        out_shape=[grid, f((steps, rows, cols), F32)],
        in_specs=[smem()] * 4,
        out_specs=[vmem()] * 2,
        name="gauges",
    )(place, gauge_row, gauge_col, observed)

    eta, west, east, block_index = pl.pallas_call(
        scatter_kernel,
        out_shape=[f((rows_here, cols_here), F32)]
        + [f((8, rows_here), F32)] * 2
        + [f((devices * SLOTS,), I32)],
        in_specs=[hbm(), vmem(), vmem(), hbm(), hbm()],
        out_specs=[vmem()] * 3 + [smem()],
        scratch_shapes=[pltpu.SMEM((devices, 1, 128), F32), pltpu.SemaphoreType.DMA]
        + [pltpu.VMEM((rows_here * cols_here // 1024, 8, 128), F32)] * SLOTS,
        name="scatter",
    )(recv_flat.reshape(devices, 1, CHUNK * 128), recv, wet_mask, faces[0], count)
    from_east = shifted(west, "gy", -1)
    from_west = shifted(east, "gy", 1)
    top, bottom = pl.pallas_call(
        rim_kernel,
        out_shape=[f((8, cols), F32)] * 2,
        in_specs=[vmem()] * 3,
        out_specs=[vmem()] * 2,
        name="eta_rims",
    )(eta, from_east, from_west)
    from_south = shifted(top, "gx", -1)
    from_north = shifted(bottom, "gx", 1)

    tile = f((rows_here, cols_here), F32)
    scratch = pltpu.VMEM((rows, cols), F32)
    final, adjoint, back = pl.pallas_call(
        solve_kernel,
        out_shape=[tile, tile, f((devices, 128), F32)],
        in_specs=[smem()] * 4 + [vmem()] * 12 + [hbm()] * 3,
        out_specs=[vmem()] * 3,
        scratch_shapes=[
            pltpu.VMEM((steps + 1, rows, cols), F32),
            scratch,
            scratch,
            pltpu.VMEM((steps - 1, rows, cols), F32),
            pltpu.VMEM((steps, rows, cols), F32),
            pltpu.VMEM((steps, rows, cols), F32),
            pltpu.VMEM((steps - 1, rows, cols), F32),
            pltpu.VMEM((steps, rows, cols), F32),
            pltpu.VMEM((steps, rows, cols), F32),
            scratch,
            scratch,
            scratch,
            pltpu.VMEM((rows // 8 * (cols_here // 128), 8, 128), F32),
            scratch,
            pltpu.VMEM((steps, rows, cols), F32),
            pltpu.VMEM((devices * CHUNK, 128), F32),
            pltpu.VMEM((SLOTS, devices, 128), F32),
            pltpu.VMEM((steps * per_tile, 128), F32),
            pltpu.SemaphoreType.DMA((3,)),
        ],
        name="solve",
    )(
        place, gauge_row, gauge_col, block_index,
        eta, from_east, from_west, from_north, from_south,
        *faces, count, obs, recv,
    )
    returned = lax.all_to_all(back, both, split_axis=0, concat_axis=0, tiled=True)
    readings = (
        returned[:, SLOTS : SLOTS + steps * per_tile]
        .reshape(devices, steps, per_tile)
        .transpose(1, 0, 2)
        .reshape(steps, gauges)
    )
    fault_of = table[:, 8 : 8 + SLOTS].astype(I32) - 1
    mine = fault_of[:, :, None] == jnp.arange(faults, dtype=I32)[None, None, :]
    grad_slip = (
        jnp.sum(jnp.where(mine, returned[:, :SLOTS, None], 0.0), axis=(0, 1)) / fault_slip
    )
    return (final, readings, adjoint, grad_slip)


def solution(mesh):
    placed = (
        P("gx", "gy"),
        P("gx", "gy"),
        P("gx", "gy"),
        P(("gx", "gy")),
        P(("gx", "gy"), None, None),
        P(("gx", "gy"), None),
        P(("gx", "gy")),
        P(),
        P(),
        P(),
    )
    return jax.shard_map(
        body,
        mesh=mesh,
        in_specs=placed,
        out_specs=(P("gx", "gy"), P(), P("gx", "gy"), P(("gx", "gy"))),
        check_vma=False,
    )
```

```python
import math

import jax
import jax.numpy as jnp
from jax import lax
from jax.experimental import pallas as pl
from jax.experimental.pallas import tpu as pltpu
from jax.sharding import PartitionSpec as P

wave_gain = 0.2
mass_gain = 0.2
min_depth = 0.25
speed_floor = 0.01

HALO = 8
CHUNK = 33
SLOTS = 4
LN2 = math.log(2.0)
PUSH = -0.5 * wave_gain
assert abs(PUSH * PUSH - speed_floor) < 1e-12
ROUGH_SCALE = 0.5 * abs(PUSH) * 2.0 ** (7.0 / 3.0)
F32 = jnp.float32
MIB = 1 << 20
UNROLL = 4
I32 = jnp.int32


def vmem():
    return pl.BlockSpec(memory_space=pltpu.VMEM)


def smem():
    return pl.BlockSpec(memory_space=pltpu.SMEM)


def hbm():
    return pl.BlockSpec(memory_space=pl.ANY)


def shifted(shard, axis, by):
    devices = lax.axis_size(axis)
    pairs = [(i, i + by) for i in range(devices) if 0 <= i + by < devices]
    return lax.ppermute(shard, axis, pairs)


def pack_kernel(
    slip_ref, tile_ref, block_ref, pattern_hbm, out_ref, table_ref, pattern, row_v, row_s, sems
):
    load = pltpu.make_async_copy(pattern_hbm, pattern, sems.at[0])
    load.start()
    rows = out_ref.shape[0]
    tiles = rows // CHUNK
    entries = tile_ref.shape[1]
    faults = slip_ref.shape[0]
    per_fault = entries // faults
    tile_row = tile_ref[...]
    tile_f = tile_row.astype(F32)
    tile_col = jnp.broadcast_to(tile_f, (128, entries)).T
    here = lax.broadcasted_iota(I32, (entries, 128), 0)
    ranks = []
    for q in range(entries // 128):
        there = lax.broadcasted_iota(I32, (entries, 128), 1) + q * 128
        same = (tile_col == tile_f[:, q * 128 : q * 128 + 128]) & (here < there)
        ranks.append(jnp.sum(jnp.where(same, 1.0, 0.0), axis=0, keepdims=True))
    rank = jnp.concatenate(ranks, axis=1).astype(I32)
    row_v[...] = tile_row * CHUNK + rank * 8
    place_rows = pltpu.make_async_copy(row_v, row_s, sems.at[1])
    place_rows.start()
    fault = lax.broadcasted_iota(I32, (1, entries), 1) // per_fault
    slot = lax.broadcasted_iota(I32, (128, entries), 0)
    facts = jnp.where(slot == rank, block_ref[...], 0) + jnp.where(slot == rank + 8, fault + 1, 0)
    hot = jnp.where(lax.broadcasted_iota(I32, (tiles, entries), 0) == tile_row, 1.0, 0.0)
    table_ref[...] = lax.dot_general(
        hot.astype(jnp.bfloat16),
        facts.astype(F32).astype(jnp.bfloat16),
        (((1,), (1,)), ((), ())),
        preferred_element_type=F32,
    )
    zero = jnp.zeros((8, 128), F32)

    def clear(i, c):
        out_ref[pl.ds(pl.multiple_of(i * 8, 8), 8), :] = zero
        return c

    lax.fori_loop(0, rows // 8, clear, 0, unroll=16)
    for t in range(tiles):
        out_ref[t * CHUNK + 32 : t * CHUNK + 33, :] = table_ref[t : t + 1, :]
    place_rows.wait()
    load.wait()

    def place(s, c):
        slip = slip_ref[s]
        for j in range(per_fault):
            i = s * per_fault + j
            out_ref[pl.ds(row_s[0, i], 8), :] = pattern[i] * slip
        return c

    lax.fori_loop(0, faults, place, 0)


def edges_of(first, last):
    lane = lax.broadcasted_iota(I32, first.shape, 1)
    both = jnp.where(lane < 64, first, last).T
    return both[0:8], both[120:128]


def side_block(east, west):
    rows = east.shape[1]
    gap = jnp.zeros((128 - 16, rows), F32)
    return jnp.concatenate([east, gap, west], axis=0).T


def meta_copy(meta_hbm, meta, sem):
    return pltpu.make_async_copy(meta_hbm.at[:, :, pl.ds(8 * SLOTS * 128, 128)], meta, sem)


def scatter_kernel(
    meta_hbm, recv_ref, wet_ref, west_in, east_in, top_in, bottom_in, after,
    eta_ref, west_ref, east_ref, top_ref, bottom_ref, meta, sem, *acc,
):
    del after
    load = meta_copy(meta_hbm, meta, sem)
    load.start()
    tiles = recv_ref.shape[0] // CHUNK
    rows, cols = eta_ref.shape
    across = cols // 128
    zero = jnp.zeros((8, 128), F32)

    def clear(i, c):
        for a in acc:
            a[i] = zero
        return c

    lax.fori_loop(0, acc[0].shape[0], clear, 0, unroll=8)
    for dst, src in (
        (west_ref, west_in), (east_ref, east_in), (top_ref, top_in), (bottom_ref, bottom_in)
    ):
        dst[0:24, :] = src[...]
    load.wait()

    def add(i, c):
        base = pl.multiple_of(i * (8 * CHUNK), 8)
        for u in range(8):
            for j in range(SLOTS):
                b = meta[i * 8 + u, 0, j].astype(I32)
                acc[j][b] = acc[j][b] + recv_ref[pl.ds(base + (u * CHUNK + 8 * j), 8), :]
        return c

    lax.fori_loop(0, tiles // 8, add, 0)

    def merge(i, c):
        r = pl.multiple_of(i * 8, 8)
        for q in range(across):
            b = i * across + q
            total = (acc[0][b] + acc[1][b]) + (acc[2][b] + acc[3][b])
            wet = wet_ref[pl.ds(r, 8), q * 128 : q * 128 + 128].astype(F32)
            eta_ref[pl.ds(r, 8), q * 128 : q * 128 + 128] = total * wet
        return c

    lax.fori_loop(0, rows // 8, merge, 0, unroll=2)
    west, east = edges_of(eta_ref[:, 0:128], eta_ref[:, cols - 128 : cols])
    west_ref[24:32] = west
    east_ref[24:32] = east
    top_ref[24:32] = eta_ref[0:8, :]
    bottom_ref[24:32] = eta_ref[rows - 8 : rows, :]


def static_edge_kernel(
    depth_ref, wet_ref, fric_ref, west_ref, east_ref, top_ref, bottom_ref
):
    rows, cols = depth_ref.shape
    for n, ref in enumerate((depth_ref, wet_ref, fric_ref)):
        at = slice(8 * n, 8 * n + 8)
        west, east = edges_of(ref[:, 0:128].astype(F32), ref[:, cols - 128 : cols].astype(F32))
        west_ref[at] = west
        east_ref[at] = east
        top_ref[at] = ref[0:8, :].astype(F32)
        bottom_ref[at] = ref[rows - 8 : rows, :].astype(F32)


def rim_kernel(east_ref, west_ref, top_in, bottom_in, top_ref, bottom_ref):
    fields = east_ref.shape[0] // 8
    rows = east_ref.shape[1]
    cols = top_in.shape[1]
    lane = lax.broadcasted_iota(I32, (8, 128), 1)
    for src, out, first, keep in (
        (top_in, top_ref, 0, slice(0, 8)),
        (bottom_in, bottom_ref, rows - 128, slice(120, 128)),
    ):
        pieces = []
        for n in range(fields):
            at = slice(8 * n, 8 * n + 8)
            pieces += [west_ref[at, first : first + 128], east_ref[at, first : first + 128]]
        pieces.append(jnp.zeros((128 - 16 * fields, 128), F32))
        corners = jnp.concatenate(pieces, axis=0).T[keep]
        for n in range(fields):
            at = slice(8 * n, 8 * n + 8)
            out[at, 0:cols] = src[at, :]
            out[at, cols:] = jnp.where(
                (lane < 8) | (lane >= 120), pltpu.roll(corners, 128 - 16 * n - 8, 1), 0.0
            )


def assemble(out, n, ref, east_ref, west_ref, north_ref, south_ref):
    rows, cols = ref.shape
    at = slice(8 * n, 8 * n + 8)
    out[0:8, :] = north_ref[at]
    out[8 : 8 + rows, 0:cols] = ref[...].astype(F32)
    out[8 : 8 + rows, cols:] = side_block(east_ref[at], west_ref[at])
    out[8 + rows : 16 + rows, :] = south_ref[at]


def row_iota(shape):
    return lax.broadcasted_iota(I32, shape, 0)


def gauge_kernel(place_ref, row_ref, col_ref, obs_ref, count_out, obs_out):
    steps, rows, cols = obs_out.shape
    own_rows = rows - 2 * HALO
    own_cols = cols - 128
    gx, gy, wx, wy = place_ref[0], place_ref[1], place_ref[2], place_ref[3]
    per = row_ref.shape[0] // (wx * wy)
    zero = jnp.zeros((8, cols), F32)

    def clear(i, c):
        r = pl.multiple_of(i * 8, 8)
        count_out[pl.ds(r, 8), :] = zero
        for k in range(steps):
            obs_out[k, pl.ds(r, 8), :] = zero
        return c

    lax.fori_loop(0, rows // 8, clear, 0)
    sub = row_iota((8, 128))
    lane = lax.broadcasted_iota(I32, (8, 128), 1)

    for dx in (-1, 0, 1):
        for dy in (-1, 0, 1):
            tx = gx + dx
            ty = gy + dy
            inside = (tx >= 0) & (tx < wx) & (ty >= 0) & (ty < wy)
            first = jnp.where(inside, (tx * wy + ty) * per, 0)

            def one(g, c, first=first, inside=inside):
                r = row_ref[first + g] - gx * own_rows + HALO
                q = col_ref[first + g] - gy * own_cols
                ok = inside & (r >= 0) & (r < rows) & (q >= -HALO) & (q < own_cols + HALO)
                q = jnp.where(q < 0, q + cols, q)

                @pl.when(ok)
                def _():
                    rb = pl.multiple_of(r // 8 * 8, 8)
                    cb = pl.multiple_of(q // 128 * 128, 128)
                    hit = (sub == r % 8) & (lane == q % 128)
                    at = (pl.ds(rb, 8), pl.ds(cb, 128))
                    count_out[at] = count_out[at] + jnp.where(hit, 1.0, 0.0)
                    for k in range(steps):
                        at_k = (k,) + at
                        obs_out[at_k] = obs_out[at_k] + jnp.where(hit, obs_ref[k, first + g], 0.0)

                return c

            lax.fori_loop(0, per, one, 0)


def face(f, s, sn, dd, rr, ww):
    x = dd + (s + sn)
    total = jnp.maximum(x, 2.0 * min_depth)
    diff = sn - s
    push = total * diff
    if f is not None:
        push = push + f
    t = push * push + 1.0
    y = (rr * jnp.exp2(jnp.log(total) * (-7.0 / 3.0 / LN2))) * lax.rsqrt(t)
    inv = 1.0 / (t * y + 1.0)
    wi = ww * inv
    flux = wi * push
    a = (wi * inv) * (y + 1.0)
    depth_part = (flux - flux * inv) * ((7.0 / 3.0) / total)
    share = jnp.where(
        x > 2.0 * min_depth, 1.0, jnp.where(x == 2.0 * min_depth, 0.5, 0.0)
    )
    u = share * (depth_part + a * diff)
    v = a * total
    return flux, a, u + v, u - v


def merge_rows(tiles):
    sub = row_iota((8, 128))
    for width in (1, 2, 4):
        low = (sub & width) == 0
        tiles = [
            jnp.where(low, p, q) + pltpu.roll(jnp.where(low, q, p), width, 0)
            for p, q in zip(tiles[0::2], tiles[1::2])
        ]
    return tiles[0]


def solve_kernel(
    place_ref, grow_ref, gcol_ref,
    eta_ref, depth_ref, wet_ref, fric_ref, east_ref, west_ref, north_ref, south_ref,
    count, obs, recv, meta_hbm,
    final_ref, adj_ref, back_ref,
    depth_x, wet, fric_x, dde, dds, rre, rrs, wwe, wws,
    surf, fe, fs, ae, pe, qe, as_, ps, qs, adj, ce, cs, grads,
    parts, reads, meta, sem,
):
    steps, rows, cols = obs.shape
    own_rows, own_cols = eta_ref.shape
    load = meta_copy(meta_hbm, meta, sem)
    load.start()
    halos = (east_ref, west_ref, north_ref, south_ref)
    assemble(depth_x, 0, depth_ref, *halos)
    assemble(wet, 1, wet_ref, *halos)
    assemble(fric_x, 2, fric_ref, *halos)
    assemble(surf.at[0], 3, eta_ref, *halos)
    sub = row_iota((8, cols))
    last = sub == 7
    firstrow = sub == 0
    blocks = rows // 8
    across = own_cols // 128

    def nxt(i):
        return pl.multiple_of(jnp.minimum(i * 8 + 8, rows - 8), 8)

    for k in range(steps):

        def eastward(i, c, k=k):
            here = pl.ds(pl.multiple_of(i * 8, 8), 8)
            if k == 0:
                d, w, m = depth_x[here, :], wet[here, :], fric_x[here, :]
                dde[here, :] = d + pltpu.roll(d, cols - 1, 1)
                wwe[here, :] = w * pltpu.roll(w, cols - 1, 1)
                rre[here, :] = ROUGH_SCALE * (m + pltpu.roll(m, cols - 1, 1))
            s = surf[k, here, :]
            old = None if k == 0 else fe[here, :]
            flux, a, p, q = face(
                old, s, pltpu.roll(s, cols - 1, 1), dde[here, :], rre[here, :], wwe[here, :]
            )
            fe[here, :] = flux
            if k > 0:
                ae[k - 1, here, :] = a
            pe[k, here, :] = p
            qe[k, here, :] = q
            return c

        def southward(i, carry, k=k):
            s, s_up, f_down = carry
            here = pl.ds(pl.multiple_of(i * 8, 8), 8)
            after = pl.ds(nxt(i), 8)
            if k == 0:

                def south(ref):
                    return jnp.where(last, pltpu.roll(ref[after, :], 7, 0), pltpu.roll(ref[here, :], 7, 0))

                dds[here, :] = depth_x[here, :] + south(depth_x)
                wws[here, :] = wet[here, :] * south(wet)
                rrs[here, :] = ROUGH_SCALE * (fric_x[here, :] + south(fric_x))
            sn = surf[k, after, :]
            sn_up = pltpu.roll(sn, 7, 0)
            old = None if k == 0 else fs[here, :]
            flux, a, p, q = face(
                old, s, jnp.where(last, sn_up, s_up), dds[here, :], rrs[here, :], wws[here, :]
            )
            fs[here, :] = flux
            if k > 0:
                as_[k - 1, here, :] = a
            ps[k, here, :] = p
            qs[k, here, :] = q
            down = pltpu.roll(flux, 1, 0)
            east = fe[here, :]
            div = east - pltpu.roll(east, 1, 1)
            div = div + (flux - jnp.where(firstrow, f_down, down))
            surf[k + 1, here, :] = wet[here, :] * (s - (mass_gain * PUSH) * div)
            return sn, sn_up, down

        s0 = surf[k, 0:8, :]
        lax.fori_loop(0, blocks, eastward, 0, unroll=UNROLL)
        lax.fori_loop(
            0,
            blocks,
            southward,
            (s0, pltpu.roll(s0, 7, 0), jnp.zeros((8, cols), F32)),
            unroll=UNROLL,
        )

    final_ref[...] = surf[steps, HALO : HALO + own_rows, 0:own_cols]

    gx, gy = place_ref[0], place_ref[1]
    lane8 = lax.broadcasted_iota(I32, (8, 128), 1)
    sub8 = row_iota((8, 128))
    per = grow_ref.shape[0] // (place_ref[2] * place_ref[3])
    per_tile = reads.shape[0] // steps
    first = (gx * place_ref[3] + gy) * per
    for g0 in range(0, per_tile, 8):
        spots = []
        for g in range(g0, g0 + 8):
            r = jnp.clip(grow_ref[first + g] - gx * own_rows, 0, own_rows - 1) + HALO
            q = jnp.clip(gcol_ref[first + g] - gy * own_cols, 0, own_cols - 1)
            at = (
                pl.ds(pl.multiple_of(r // 8 * 8, 8), 8),
                pl.ds(pl.multiple_of(q // 128 * 128, 128), 128),
            )
            spots.append((at, (sub8 == r % 8) & (lane8 == q % 128)))
        for k in range(steps):
            picked = [jnp.where(hit, surf[(k + 1,) + at], 0.0) for at, hit in spots]
            reads[k * per_tile + g0 : k * per_tile + g0 + 8, :] = merge_rows(picked)
    values = jnp.sum(reads[...], axis=1, keepdims=True)
    spots = row_iota(reads.shape) + SLOTS == lax.broadcasted_iota(I32, reads.shape, 1)
    reading_row = jnp.sum(jnp.where(spots, values, 0.0), axis=0, keepdims=True)

    load.wait()

    for k in reversed(range(steps)):

        def seeded(value, at, k):
            seed = count[at, :] * surf[k + 1, at, :] - obs[k, at, :]
            return seed if value is None else value + seed

        def b_of(r, k=k):
            at = pl.ds(r, 8)
            a = seeded(None, at, k) if k == steps - 1 else adj[at, :]
            return wet[at, :] * a

        def backward(i, carry, k=k):
            b, b_up, x_down = carry
            r = pl.multiple_of(i * 8, 8)
            here = pl.ds(r, 8)
            bn = b_of(nxt(i))
            bn_up = pltpu.roll(bn, 7, 0)
            b_south = jnp.where(last, bn_up, b_up)
            b_east = pltpu.roll(b, cols - 1, 1)
            ge = (mass_gain * PUSH) * (b_east - b)
            gs = (mass_gain * PUSH) * (b_south - b)
            if k < steps - 1:
                ge = ge + ce[here, :]
                gs = gs + cs[here, :]
            if k > 0:
                ce[here, :] = ge * ae[k - 1, here, :]
                cs[here, :] = gs * as_[k - 1, here, :]
            xe = ge * pe[k, here, :]
            xs = gs * ps[k, here, :]
            down = pltpu.roll(xs, 1, 0)
            out = b + ge * qe[k, here, :] + pltpu.roll(xe, 1, 1)
            out = out + gs * qs[k, here, :] + jnp.where(firstrow, x_down, down)
            if k > 0:
                out = seeded(out, here, k - 1)
            adj[here, :] = out
            if k == 0:
                scaled = out * wet[here, :]
                for q in range(across):
                    grads[i * across + q] = scaled[:, q * 128 : q * 128 + 128]
            return bn, bn_up, down

        b0 = b_of(0)
        lax.fori_loop(
            0,
            blocks,
            backward,
            (b0, pltpu.roll(b0, 7, 0), jnp.zeros((8, cols), F32)),
            unroll=2,
        )

    adj_ref[...] = adj[HALO : HALO + own_rows, 0:own_cols]

    tiles = recv.shape[0] // CHUNK

    def sens(i, c):
        for j in range(SLOTS):
            products = []
            for u in range(8):
                t = i * 8 + u
                b = meta[t, 0, j].astype(I32) + HALO // 8 * across
                products.append(grads[b] * recv[pl.ds(t * CHUNK + 8 * j, 8), :])
            parts[j, pl.ds(pl.multiple_of(i * 8, 8), 8), :] = merge_rows(products)
        return c

    lax.fori_loop(0, tiles // 8, sens, 0)
    lanes = lax.broadcasted_iota(I32, (tiles, 128), 1)
    out = jnp.broadcast_to(reading_row, (tiles, 128))
    for j in range(SLOTS):
        out = jnp.where(lanes == j, jnp.sum(parts[j], axis=1, keepdims=True), out)
    back_ref[...] = out


def body(
    ocean_depth,
    wet_mask,
    manning,
    fault_slip,
    pattern,
    foot_tile,
    foot_block,
    gauge_row,
    gauge_col,
    observed,
):
    rows_here, cols_here = ocean_depth.shape
    steps, gauges = observed.shape
    width_x = lax.axis_size("gx")
    width_y = lax.axis_size("gy")
    devices = width_x * width_y
    entries = pattern.shape[0]
    faults = fault_slip.shape[0]
    per_fault = entries // faults
    per_tile = gauges // devices
    both = ("gx", "gy")
    rows, cols = rows_here + 2 * HALO, cols_here + 128
    f = jax.ShapeDtypeStruct

    packed, table = pl.pallas_call(
        pack_kernel,
        out_shape=[f((devices * CHUNK, 128), F32), f((devices, 128), F32)],
        in_specs=[smem(), vmem(), vmem(), hbm()],
        out_specs=[vmem()] * 2,
        scratch_shapes=[
            pltpu.VMEM(pattern.shape, F32),
            pltpu.VMEM((1, entries), I32),
            pltpu.SMEM((1, entries), I32),
            pltpu.SemaphoreType.DMA((2,)),
        ],
        name="pack",
    )(fault_slip, foot_tile.reshape(1, entries), foot_block.reshape(1, entries), pattern)
    recv_flat = lax.all_to_all(packed.reshape(-1), both, split_axis=0, concat_axis=0, tiled=True)
    recv = recv_flat.reshape(devices * CHUNK, 128)

    edge = [f((24, rows_here), F32)] * 2 + [f((24, cols_here), F32)] * 2
    edges = pl.pallas_call(
        static_edge_kernel,
        out_shape=edge,
        in_specs=[vmem()] * 3,
        out_specs=[vmem()] * 4,
        name="static_edges",
        compiler_params=pltpu.CompilerParams(vmem_limit_bytes=4 * MIB),
    )(ocean_depth, wet_mask, manning)
    grid = f((rows, cols), F32)
    place = jnp.stack(
        [lax.axis_index("gx"), lax.axis_index("gy"), jnp.int32(width_x), jnp.int32(width_y)]
    ).astype(I32)
    count, obs = pl.pallas_call(
        gauge_kernel,
        out_shape=[grid, f((steps, rows, cols), F32)],
        in_specs=[smem()] * 4,
        out_specs=[vmem()] * 2,
        name="gauges",
        compiler_params=pltpu.CompilerParams(vmem_limit_bytes=2 * MIB),
    )(place, gauge_row, gauge_col, observed)

    slots_view = recv_flat.reshape(devices, 1, CHUNK * 128)
    eta, west, east, top, bottom = pl.pallas_call(
        scatter_kernel,
        out_shape=[f((rows_here, cols_here), F32)]
        + [f((32, rows_here), F32)] * 2
        + [f((32, cols_here), F32)] * 2,
        in_specs=[hbm()] + [vmem()] * 6 + [hbm()],
        out_specs=[vmem()] * 5,
        scratch_shapes=[pltpu.SMEM((devices, 1, 128), F32), pltpu.SemaphoreType.DMA]
        + [pltpu.VMEM((rows_here * cols_here // 1024, 8, 128), F32)] * SLOTS,
        name="scatter",
        compiler_params=pltpu.CompilerParams(vmem_limit_bytes=10 * MIB),
    )(slots_view, recv, wet_mask, *edges, count)
    from_east = shifted(west, "gy", -1)
    from_west = shifted(east, "gy", 1)
    top, bottom = pl.pallas_call(
        rim_kernel,
        out_shape=[f((32, cols), F32)] * 2,
        in_specs=[vmem()] * 4,
        out_specs=[vmem()] * 2,
        name="rims",
        compiler_params=pltpu.CompilerParams(vmem_limit_bytes=2 * MIB),
    )(from_east, from_west, top, bottom)
    from_south = shifted(top, "gx", -1)
    from_north = shifted(bottom, "gx", 1)

    tile = f((rows_here, cols_here), F32)
    scratch = pltpu.VMEM((rows, cols), F32)
    final, adjoint, back = pl.pallas_call(
        solve_kernel,
        out_shape=[tile, tile, f((devices, 128), F32)],
        in_specs=[smem()] * 3 + [vmem()] * 11 + [hbm()],
        out_specs=[vmem()] * 3,
        scratch_shapes=[scratch] * 9
        + [
            pltpu.VMEM((steps + 1, rows, cols), F32),
            scratch,
            scratch,
            pltpu.VMEM((steps - 1, rows, cols), F32),
            pltpu.VMEM((steps, rows, cols), F32),
            pltpu.VMEM((steps, rows, cols), F32),
            pltpu.VMEM((steps - 1, rows, cols), F32),
            pltpu.VMEM((steps, rows, cols), F32),
            pltpu.VMEM((steps, rows, cols), F32),
            scratch,
            scratch,
            scratch,
            pltpu.VMEM((rows // 8 * (cols_here // 128), 8, 128), F32),
            pltpu.VMEM((SLOTS, devices, 128), F32),
            pltpu.VMEM((steps * per_tile, 128), F32),
            pltpu.SMEM((devices, 1, 128), F32),
            pltpu.SemaphoreType.DMA,
        ],
        name="solve",
        compiler_params=pltpu.CompilerParams(vmem_limit_bytes=44 * MIB),
    )(
        place, gauge_row, gauge_col,
        eta, ocean_depth, wet_mask, manning, from_east, from_west, from_north, from_south,
        count, obs, recv, slots_view,
    )
    returned = lax.all_to_all(back, both, split_axis=0, concat_axis=0, tiled=True)
    readings = (
        returned[:, SLOTS : SLOTS + steps * per_tile]
        .reshape(devices, steps, per_tile)
        .transpose(1, 0, 2)
        .reshape(steps, gauges)
    )
    fault_of = table[:, 8 : 8 + SLOTS].astype(I32) - 1
    mine = fault_of[:, :, None] == jnp.arange(faults, dtype=I32)[None, None, :]
    grad_slip = (
        jnp.sum(jnp.where(mine, returned[:, :SLOTS, None], 0.0), axis=(0, 1)) / fault_slip
    )
    return (final, readings, adjoint, grad_slip)


def solution(mesh):
    placed = (
        P("gx", "gy"),
        P("gx", "gy"),
        P("gx", "gy"),
        P(("gx", "gy")),
        P(("gx", "gy"), None, None),
        P(("gx", "gy"), None),
        P(("gx", "gy")),
        P(),
        P(),
        P(),
    )
    return jax.shard_map(
        body,
        mesh=mesh,
        in_specs=placed,
        out_specs=(P("gx", "gy"), P(), P("gx", "gy"), P(("gx", "gy"))),
        check_vma=False,
    )
```

```python
import math

import jax
import jax.numpy as jnp
from jax import lax
from jax.experimental import pallas as pl
from jax.experimental.pallas import tpu as pltpu
from jax.sharding import PartitionSpec as P

wave_gain = 0.2
mass_gain = 0.2
min_depth = 0.25
speed_floor = 0.01

HALO = 8
CHUNK = 33
SLOTS = 4
LN2 = math.log(2.0)
PUSH = -0.5 * wave_gain
assert abs(PUSH * PUSH - speed_floor) < 1e-12
ROUGH_SCALE = 0.5 * abs(PUSH) * 2.0 ** (7.0 / 3.0)
F32 = jnp.float32
MIB = 1 << 20
UNROLL = 4
I32 = jnp.int32


def vmem():
    return pl.BlockSpec(memory_space=pltpu.VMEM)


def smem():
    return pl.BlockSpec(memory_space=pltpu.SMEM)


def hbm():
    return pl.BlockSpec(memory_space=pl.ANY)


def shifted(shard, axis, by):
    devices = lax.axis_size(axis)
    pairs = [(i, i + by) for i in range(devices) if 0 <= i + by < devices]
    return lax.ppermute(shard, axis, pairs)


def pack_kernel(
    slip_ref, tile_ref, block_ref, pattern_hbm, out_ref, table_ref, pattern, row_v, row_s, sems
):
    load = pltpu.make_async_copy(pattern_hbm, pattern, sems.at[0])
    load.start()
    rows = out_ref.shape[0]
    tiles = rows // CHUNK
    entries = tile_ref.shape[1]
    faults = slip_ref.shape[0]
    per_fault = entries // faults
    tile_row = tile_ref[...]
    tile_f = tile_row.astype(F32)
    tile_col = jnp.broadcast_to(tile_f, (128, entries)).T
    here = lax.broadcasted_iota(I32, (entries, 128), 0)
    ranks = []
    for q in range(entries // 128):
        there = lax.broadcasted_iota(I32, (entries, 128), 1) + q * 128
        same = (tile_col == tile_f[:, q * 128 : q * 128 + 128]) & (here < there)
        ranks.append(jnp.sum(jnp.where(same, 1.0, 0.0), axis=0, keepdims=True))
    rank = jnp.concatenate(ranks, axis=1).astype(I32)
    row_v[...] = tile_row * CHUNK + rank * 8
    place_rows = pltpu.make_async_copy(row_v, row_s, sems.at[1])
    place_rows.start()
    fault = lax.broadcasted_iota(I32, (1, entries), 1) // per_fault
    slot = lax.broadcasted_iota(I32, (128, entries), 0)
    facts = jnp.where(slot == rank, block_ref[...], 0) + jnp.where(slot == rank + 8, fault + 1, 0)
    hot = jnp.where(lax.broadcasted_iota(I32, (tiles, entries), 0) == tile_row, 1.0, 0.0)
    table_ref[...] = lax.dot_general(
        hot.astype(jnp.bfloat16),
        facts.astype(F32).astype(jnp.bfloat16),
        (((1,), (1,)), ((), ())),
        preferred_element_type=F32,
    )
    zero = jnp.zeros((8, 128), F32)

    def clear(i, c):
        out_ref[pl.ds(pl.multiple_of(i * 8, 8), 8), :] = zero
        return c

    lax.fori_loop(0, rows // 8, clear, 0, unroll=16)
    for t in range(tiles):
        out_ref[t * CHUNK + 32 : t * CHUNK + 33, :] = table_ref[t : t + 1, :]
    place_rows.wait()
    load.wait()

    def place(s, c):
        slip = slip_ref[s]
        for j in range(per_fault):
            i = s * per_fault + j
            out_ref[pl.ds(row_s[0, i], 8), :] = pattern[i] * slip
        return c

    lax.fori_loop(0, faults, place, 0)


def edges_of(first, last):
    lane = lax.broadcasted_iota(I32, first.shape, 1)
    both = jnp.where(lane < 64, first, last).T
    return both[0:8], both[120:128]


def side_block(east, west):
    rows = east.shape[1]
    gap = jnp.zeros((128 - 16, rows), F32)
    return jnp.concatenate([east, gap, west], axis=0).T


def meta_copy(meta_hbm, meta, sem):
    return pltpu.make_async_copy(meta_hbm.at[:, :, pl.ds(8 * SLOTS * 128, 128)], meta, sem)


def scatter_kernel(
    meta_hbm, recv_ref, wet_ref, west_in, east_in, top_in, bottom_in, after,
    eta_ref, west_ref, east_ref, top_ref, bottom_ref, meta, sem, *acc,
):
    del after
    load = meta_copy(meta_hbm, meta, sem)
    load.start()
    tiles = recv_ref.shape[0] // CHUNK
    rows, cols = eta_ref.shape
    across = cols // 128
    zero = jnp.zeros((8, 128), F32)

    def clear(i, c):
        for a in acc:
            a[i] = zero
        return c

    lax.fori_loop(0, acc[0].shape[0], clear, 0, unroll=8)
    for dst, src in (
        (west_ref, west_in), (east_ref, east_in), (top_ref, top_in), (bottom_ref, bottom_in)
    ):
        dst[0:24, :] = src[...]
    load.wait()

    def add(i, c):
        base = pl.multiple_of(i * (8 * CHUNK), 8)
        for u in range(8):
            for j in range(SLOTS):
                b = meta[i * 8 + u, 0, j].astype(I32)
                acc[j][b] = acc[j][b] + recv_ref[pl.ds(base + (u * CHUNK + 8 * j), 8), :]
        return c

    lax.fori_loop(0, tiles // 8, add, 0)

    def merge(i, c):
        r = pl.multiple_of(i * 8, 8)
        for q in range(across):
            b = i * across + q
            total = (acc[0][b] + acc[1][b]) + (acc[2][b] + acc[3][b])
            wet = wet_ref[pl.ds(r, 8), q * 128 : q * 128 + 128].astype(F32)
            eta_ref[pl.ds(r, 8), q * 128 : q * 128 + 128] = total * wet
        return c

    lax.fori_loop(0, rows // 8, merge, 0, unroll=2)
    west, east = edges_of(eta_ref[:, 0:128], eta_ref[:, cols - 128 : cols])
    west_ref[24:32] = west
    east_ref[24:32] = east
    top_ref[24:32] = eta_ref[0:8, :]
    bottom_ref[24:32] = eta_ref[rows - 8 : rows, :]


def static_edge_kernel(
    depth_ref, wet_ref, fric_ref, west_ref, east_ref, top_ref, bottom_ref
):
    rows, cols = depth_ref.shape
    for n, ref in enumerate((depth_ref, wet_ref, fric_ref)):
        at = slice(8 * n, 8 * n + 8)
        west, east = edges_of(ref[:, 0:128].astype(F32), ref[:, cols - 128 : cols].astype(F32))
        west_ref[at] = west
        east_ref[at] = east
        top_ref[at] = ref[0:8, :].astype(F32)
        bottom_ref[at] = ref[rows - 8 : rows, :].astype(F32)


def rim_kernel(east_ref, west_ref, top_in, bottom_in, after, top_ref, bottom_ref):
    del after
    fields = east_ref.shape[0] // 8
    rows = east_ref.shape[1]
    cols = top_in.shape[1]
    lane = lax.broadcasted_iota(I32, (8, 128), 1)
    for src, out, first, keep in (
        (top_in, top_ref, 0, slice(0, 8)),
        (bottom_in, bottom_ref, rows - 128, slice(120, 128)),
    ):
        pieces = []
        for n in range(fields):
            at = slice(8 * n, 8 * n + 8)
            pieces += [west_ref[at, first : first + 128], east_ref[at, first : first + 128]]
        pieces.append(jnp.zeros((128 - 16 * fields, 128), F32))
        corners = jnp.concatenate(pieces, axis=0).T[keep]
        for n in range(fields):
            at = slice(8 * n, 8 * n + 8)
            out[at, 0:cols] = src[at, :]
            out[at, cols:] = jnp.where(
                (lane < 8) | (lane >= 120), pltpu.roll(corners, 128 - 16 * n - 8, 1), 0.0
            )


def row_iota(shape):
    return lax.broadcasted_iota(I32, shape, 0)


def gauge_kernel(place_ref, row_ref, col_ref, obs_ref, count_out, obs_out, token_out):
    token_out[...] = jnp.zeros(token_out.shape, F32)
    steps, rows, cols = obs_out.shape
    own_rows = rows - 2 * HALO
    own_cols = cols - 128
    gx, gy, wx, wy = place_ref[0], place_ref[1], place_ref[2], place_ref[3]
    per = row_ref.shape[0] // (wx * wy)
    zero = jnp.zeros((8, cols), F32)

    def clear(i, c):
        r = pl.multiple_of(i * 8, 8)
        count_out[pl.ds(r, 8), :] = zero
        for k in range(steps):
            obs_out[k, pl.ds(r, 8), :] = zero
        return c

    lax.fori_loop(0, rows // 8, clear, 0)
    sub = row_iota((8, 128))
    lane = lax.broadcasted_iota(I32, (8, 128), 1)

    for dx in (-1, 0, 1):
        for dy in (-1, 0, 1):
            tx = gx + dx
            ty = gy + dy
            inside = (tx >= 0) & (tx < wx) & (ty >= 0) & (ty < wy)
            first = jnp.where(inside, (tx * wy + ty) * per, 0)

            def one(g, c, first=first, inside=inside):
                r = row_ref[first + g] - gx * own_rows + HALO
                q = col_ref[first + g] - gy * own_cols
                ok = inside & (r >= 0) & (r < rows) & (q >= -HALO) & (q < own_cols + HALO)
                q = jnp.where(q < 0, q + cols, q)

                @pl.when(ok)
                def _():
                    rb = pl.multiple_of(r // 8 * 8, 8)
                    cb = pl.multiple_of(q // 128 * 128, 128)
                    hit = (sub == r % 8) & (lane == q % 128)
                    at = (pl.ds(rb, 8), pl.ds(cb, 128))
                    count_out[at] = count_out[at] + jnp.where(hit, 1.0, 0.0)
                    for k in range(steps):
                        at_k = (k,) + at
                        obs_out[at_k] = obs_out[at_k] + jnp.where(hit, obs_ref[k, first + g], 0.0)

                return c

            lax.fori_loop(0, per, one, 0)


def face(f, s, sn, dd, rr, ww):
    x = dd + (s + sn)
    total = jnp.maximum(x, 2.0 * min_depth)
    diff = sn - s
    push = total * diff
    if f is not None:
        push = push + f
    t = push * push + 1.0
    y = (rr * jnp.exp2(jnp.log(total) * (-7.0 / 3.0 / LN2))) * lax.rsqrt(t)
    inv = 1.0 / (t * y + 1.0)
    wi = ww * inv
    flux = wi * push
    a = (wi * inv) * (y + 1.0)
    depth_part = (flux - flux * inv) * ((7.0 / 3.0) / total)
    share = jnp.where(
        x > 2.0 * min_depth, 1.0, jnp.where(x == 2.0 * min_depth, 0.5, 0.0)
    )
    u = share * (depth_part + a * diff)
    v = a * total
    return flux, a, u + v, u - v


def merge_rows(tiles):
    sub = row_iota((8, 128))
    for width in (1, 2, 4):
        low = (sub & width) == 0
        tiles = [
            jnp.where(low, p, q) + pltpu.roll(jnp.where(low, q, p), width, 0)
            for p, q in zip(tiles[0::2], tiles[1::2])
        ]
    return tiles[0]


def statics_of(d, w, m, d_next, w_next, m_next):
    return d + d_next, ROUGH_SCALE * (m + m_next), w * w_next


def south_of(here, after):
    last = row_iota(here.shape) == 7
    return jnp.where(last, pltpu.roll(after, 7, 0), pltpu.roll(here, 7, 0))


def north_of(flux, before):
    first = row_iota(flux.shape) == 0
    return jnp.where(first, pltpu.roll(before, 1, 0), pltpu.roll(flux, 1, 0))


def rows_at(i):
    return pl.ds(pl.multiple_of(i * 8, 8), 8)


def divergence(east, south, before):
    return (east - pltpu.roll(east, 1, 1)) + (south - north_of(south, before))


def store_face(refs, at, statics, made):
    flux, _, p, q = made
    for ref, value in zip(refs, (*statics, flux, p, q)):
        ref[at] = value


def tile_kernel(eta_ref, depth_ref, wet_ref, fric_ref, *out):
    east, south = out[:6], out[6:]
    rows, cols = eta_ref.shape
    fields = (depth_ref, wet_ref, fric_ref, eta_ref)
    keep = cols - 128

    def eastward(i, c):
        here = [ref[rows_at(i), :].astype(F32) for ref in fields]
        there = [pltpu.roll(v, cols - 1, 1)[:, :keep] for v in here]
        here = [v[:, :keep] for v in here]
        statics = statics_of(*here[:3], *there[:3])
        store_face(east, (rows_at(i + 1), slice(0, keep)), statics, face(None, here[3], there[3], *statics))
        return c

    def southward(i, c):
        here = [ref[rows_at(i), :].astype(F32) for ref in fields]
        there = [south_of(v, ref[rows_at(i + 1), :].astype(F32)) for v, ref in zip(here, fields)]
        statics = statics_of(*here[:3], *there[:3])
        store_face(south, (rows_at(i + 1), slice(0, cols)), statics, face(None, here[3], there[3], *statics))
        return c

    lax.fori_loop(0, rows // 8, eastward, 0, unroll=4)
    lax.fori_loop(0, rows // 8 - 1, southward, 0, unroll=3)


def frame_kernel(
    eta_ref, depth_ref, wet_ref, fric_ref, east_ref, west_ref, dde, rre, wwe, fe, fs, *refs
):
    east, south = refs[:6], refs[6:12]
    surf0, wet, surf1, fe1, ae1, pe1, qe1 = refs[12:19]
    sides = refs[19:]
    rows, cols = eta_ref.shape
    fields = (depth_ref, wet_ref, fric_ref, eta_ref)
    blocks = rows // 8
    for n, side in enumerate(sides):
        side[...] = side_block(east_ref[8 * n : 8 * n + 8], west_ref[8 * n : 8 * n + 8])

    def frame(i, c):
        at = rows_at(i)
        out = rows_at(i + 1)
        after = rows_at(jnp.minimum(i + 1, blocks - 1))
        corner = [side[at, :] for side in sides]
        tail = [ref[at, cols - 128 :].astype(F32) for ref in fields]
        head = [ref[at, 0:128].astype(F32) for ref in fields]
        here = [jnp.concatenate(p, axis=1) for p in zip(tail, corner)]
        there = [
            pltpu.roll(jnp.concatenate(p, axis=1), 3 * 128 - 1, 1)[:, :256]
            for p in zip(tail, corner, head)
        ]
        statics = statics_of(*here[:3], *there[:3])
        store_face(east, (out, slice(None)), statics, face(None, here[3], there[3], *statics))
        there = [south_of(v, side[after, :]) for v, side in zip(corner, sides)]
        statics = statics_of(*corner[:3], *there[:3])
        store_face(south, (out, slice(None)), statics, face(None, corner[3], there[3], *statics))
        for ref, n in ((wet, 1), (surf0, 3)):
            ref[out, 0:cols] = fields[n][at, :].astype(F32)
            ref[out, cols:] = corner[n]
        return c

    lax.fori_loop(0, blocks, frame, 0, unroll=2)
    cut = cols - 128

    def whole(left, right, at):
        width = left.shape[1] - right.shape[1]
        return jnp.concatenate([left[at, 0:width], right[at, :]], axis=1)

    def surface(i, before):
        at = rows_at(i)
        flux = whole(fs, south[3], at)
        div = divergence(whole(fe, east[3], at), flux, before)
        surf1[at, :] = wet[at, :] * (surf0[at, :] - (mass_gain * PUSH) * div)
        return flux

    lax.fori_loop(2, blocks, surface, whole(fs, south[3], rows_at(1)), unroll=2)

    def eastward(i, c):
        at = rows_at(i)
        s = surf1[at, :]
        statics = [whole(a, b, at) for a, b in ((dde, east[0]), (rre, east[1]), (wwe, east[2]))]
        made = face(whole(fe, east[3], at), s, pltpu.roll(s, s.shape[1] - 1, 1), *statics)
        for ref, value in zip((fe1, ae1, pe1, qe1), made):
            ref[at, :] = value
        return c

    lax.fori_loop(2, blocks, eastward, 0, unroll=3)


def solve_kernel(*refs):
    place_ref, grow_ref, gcol_ref = refs[:3]
    east0, south0, east_part, south_part = (refs[3 + 6 * n : 9 + 6 * n] for n in range(4))
    surf0, wet, surf1, fe1, ae1, pe1, qe1 = refs[27:34]
    north_ref, south_ref, top_ref, bottom_ref, count, obs, recv, meta_hbm = refs[34:42]
    final_ref, adj_ref, back_ref = refs[42:45]
    (
        surf_s, ae_s, as_s, pe_s, qe_s, ps_s, qs_s,
        adj, ce, cs, grads, parts, reads, meta, sem,
    ) = refs[45:]
    steps, rows, cols = obs.shape
    own_rows, own_cols = final_ref.shape
    dde, rre, wwe, fe0, pe0, qe0 = east0
    dds, rrs, wws, fs, ps0, qs0 = south0
    surf = [surf0, surf1] + [surf_s.at[n] for n in range(steps - 1)]
    ae = [None, ae1] + [ae_s.at[n] for n in range(steps - 2)]
    pe = [pe0, pe1] + [pe_s.at[n] for n in range(steps - 2)]
    qe = [qe0, qe1] + [qe_s.at[n] for n in range(steps - 2)]
    as_ = [None] + [as_s.at[n] for n in range(steps - 1)]
    ps = [ps0] + [ps_s.at[n] for n in range(steps - 1)]
    qs = [qs0] + [qs_s.at[n] for n in range(steps - 1)]
    load = meta_copy(meta_hbm, meta, sem)
    load.start()
    sub = row_iota((8, cols))
    last = sub == 7
    firstrow = sub == 0
    blocks = rows // 8
    across = own_cols // 128

    def nxt(i):
        return pl.multiple_of(jnp.minimum(i * 8 + 8, rows - 8), 8)

    def take(i, c):
        at = rows_at(i)
        for whole, part in zip(east0 + south0, east_part + south_part):
            whole[at, cols - part.shape[1] :] = part[at, :]
        return c

    lax.fori_loop(1, blocks - 1, take, 0, unroll=2)

    def field(ref, n):
        return ref[8 * n : 8 * n + 8, :]

    def edge_face(refs, i, ref, neighbour):
        here = [field(ref, n) for n in range(4)]
        there = neighbour(here)
        statics = statics_of(*here[:3], *there[:3])
        store_face(refs, (rows_at(i), slice(None)), statics, face(None, here[3], there[3], *statics))

    def east_of(here):
        return [pltpu.roll(v, cols - 1, 1) for v in here]

    def above(ref):
        return lambda here: [south_of(v, field(ref, n)) for n, v in enumerate(here)]

    for i, ref in ((0, north_ref), (blocks - 1, south_ref)):
        surf0[rows_at(i), :] = field(ref, 3)
        wet[rows_at(i), :] = field(ref, 1)
        edge_face(east0, i, ref, east_of)
    edge_face(south0, 0, north_ref, above(top_ref))
    edge_face(south0, blocks - 2, bottom_ref, above(south_ref))
    edge_face(south0, blocks - 1, south_ref, above(south_ref))
    rim = (0, 1, blocks - 2, blocks - 1)
    for i in rim:
        at = rows_at(i)
        before = fs[rows_at(max(i - 1, 0)), :]
        div = divergence(fe0[at, :], fs[at, :], before)
        surf1[at, :] = wet[at, :] * (surf0[at, :] - (mass_gain * PUSH) * div)

    for k in range(1, steps):

        def eastward(i, c, k=k):
            here = rows_at(i)
            s = surf[k][here, :]
            old = fe0 if k == 1 else fe1
            flux, a, p, q = face(
                old[here, :], s, pltpu.roll(s, cols - 1, 1), dde[here, :], rre[here, :], wwe[here, :]
            )
            fe1[here, :] = flux
            ae[k][here, :] = a
            pe[k][here, :] = p
            qe[k][here, :] = q
            return c

        def southward(i, carry, k=k):
            s, s_up, f_down = carry
            here = rows_at(i)
            sn = surf[k][pl.ds(nxt(i), 8), :]
            sn_up = pltpu.roll(sn, 7, 0)
            flux, a, p, q = face(
                fs[here, :], s, jnp.where(last, sn_up, s_up), dds[here, :], rrs[here, :], wws[here, :]
            )
            fs[here, :] = flux
            as_[k][here, :] = a
            ps[k][here, :] = p
            qs[k][here, :] = q
            down = pltpu.roll(flux, 1, 0)
            east = fe1[here, :]
            div = east - pltpu.roll(east, 1, 1)
            div = div + (flux - jnp.where(firstrow, f_down, down))
            surf[k + 1][here, :] = wet[here, :] * (s - (mass_gain * PUSH) * div)
            return sn, sn_up, down

        s0 = surf[k][0:8, :]
        if k == 1:
            for i in rim:
                eastward(i, 0)
        else:
            lax.fori_loop(0, blocks, eastward, 0, unroll=UNROLL)
        lax.fori_loop(
            0,
            blocks,
            southward,
            (s0, pltpu.roll(s0, 7, 0), jnp.zeros((8, cols), F32)),
            unroll=UNROLL,
        )

    final_ref[...] = surf[steps][HALO : HALO + own_rows, 0:own_cols]

    gx, gy = place_ref[0], place_ref[1]
    lane8 = lax.broadcasted_iota(I32, (8, 128), 1)
    sub8 = row_iota((8, 128))
    per = grow_ref.shape[0] // (place_ref[2] * place_ref[3])
    per_tile = reads.shape[0] // steps
    first = (gx * place_ref[3] + gy) * per
    for g0 in range(0, per_tile, 8):
        spots = []
        for g in range(g0, g0 + 8):
            r = jnp.clip(grow_ref[first + g] - gx * own_rows, 0, own_rows - 1) + HALO
            q = jnp.clip(gcol_ref[first + g] - gy * own_cols, 0, own_cols - 1)
            at = (
                pl.ds(pl.multiple_of(r // 8 * 8, 8), 8),
                pl.ds(pl.multiple_of(q // 128 * 128, 128), 128),
            )
            spots.append((at, (sub8 == r % 8) & (lane8 == q % 128)))
        for k in range(steps):
            picked = [jnp.where(hit, surf[k + 1][at], 0.0) for at, hit in spots]
            reads[k * per_tile + g0 : k * per_tile + g0 + 8, :] = merge_rows(picked)
    values = jnp.sum(reads[...], axis=1, keepdims=True)
    spots = row_iota(reads.shape) + SLOTS == lax.broadcasted_iota(I32, reads.shape, 1)
    reading_row = jnp.sum(jnp.where(spots, values, 0.0), axis=0, keepdims=True)

    load.wait()

    for k in reversed(range(steps)):

        def seeded(value, at, k):
            seed = count[at, :] * surf[k + 1][at, :] - obs[k, at, :]
            return seed if value is None else value + seed

        def b_of(r, k=k):
            at = pl.ds(r, 8)
            a = seeded(None, at, k) if k == steps - 1 else adj[at, :]
            return wet[at, :] * a

        def backward(i, carry, k=k):
            b, b_up, x_down = carry
            r = pl.multiple_of(i * 8, 8)
            here = pl.ds(r, 8)
            bn = b_of(nxt(i))
            bn_up = pltpu.roll(bn, 7, 0)
            b_south = jnp.where(last, bn_up, b_up)
            b_east = pltpu.roll(b, cols - 1, 1)
            ge = (mass_gain * PUSH) * (b_east - b)
            gs = (mass_gain * PUSH) * (b_south - b)
            if k < steps - 1:
                ge = ge + ce[here, :]
                gs = gs + cs[here, :]
            if k > 0:
                ce[here, :] = ge * ae[k][here, :]
                cs[here, :] = gs * as_[k][here, :]
            xe = ge * pe[k][here, :]
            xs = gs * ps[k][here, :]
            down = pltpu.roll(xs, 1, 0)
            out = b + ge * qe[k][here, :] + pltpu.roll(xe, 1, 1)
            out = out + gs * qs[k][here, :] + jnp.where(firstrow, x_down, down)
            if k > 0:
                out = seeded(out, here, k - 1)
            adj[here, :] = out
            if k == 0:
                scaled = out * wet[here, :]
                for q in range(across):
                    grads[i * across + q] = scaled[:, q * 128 : q * 128 + 128]
            return bn, bn_up, down

        b0 = b_of(0)
        lax.fori_loop(
            0,
            blocks,
            backward,
            (b0, pltpu.roll(b0, 7, 0), jnp.zeros((8, cols), F32)),
            unroll=2,
        )

    adj_ref[...] = adj[HALO : HALO + own_rows, 0:own_cols]

    tiles = recv.shape[0] // CHUNK

    def sens(i, c):
        for j in range(SLOTS):
            products = []
            for u in range(8):
                t = i * 8 + u
                b = meta[t, 0, j].astype(I32) + HALO // 8 * across
                products.append(grads[b] * recv[pl.ds(t * CHUNK + 8 * j, 8), :])
            parts[j, pl.ds(pl.multiple_of(i * 8, 8), 8), :] = merge_rows(products)
        return c

    lax.fori_loop(0, tiles // 8, sens, 0)
    lanes = lax.broadcasted_iota(I32, (tiles, 128), 1)
    out = jnp.broadcast_to(reading_row, (tiles, 128))
    for j in range(SLOTS):
        out = jnp.where(lanes == j, jnp.sum(parts[j], axis=1, keepdims=True), out)
    back_ref[...] = out


def body(
    ocean_depth,
    wet_mask,
    manning,
    fault_slip,
    pattern,
    foot_tile,
    foot_block,
    gauge_row,
    gauge_col,
    observed,
):
    rows_here, cols_here = ocean_depth.shape
    steps, gauges = observed.shape
    width_x = lax.axis_size("gx")
    width_y = lax.axis_size("gy")
    devices = width_x * width_y
    entries = pattern.shape[0]
    faults = fault_slip.shape[0]
    per_fault = entries // faults
    per_tile = gauges // devices
    both = ("gx", "gy")
    rows, cols = rows_here + 2 * HALO, cols_here + 128
    f = jax.ShapeDtypeStruct

    packed, table = pl.pallas_call(
        pack_kernel,
        out_shape=[f((devices * CHUNK, 128), F32), f((devices, 128), F32)],
        in_specs=[smem(), vmem(), vmem(), hbm()],
        out_specs=[vmem()] * 2,
        scratch_shapes=[
            pltpu.VMEM(pattern.shape, F32),
            pltpu.VMEM((1, entries), I32),
            pltpu.SMEM((1, entries), I32),
            pltpu.SemaphoreType.DMA((2,)),
        ],
        name="pack",
    )(fault_slip, foot_tile.reshape(1, entries), foot_block.reshape(1, entries), pattern)
    recv_flat = lax.all_to_all(packed.reshape(-1), both, split_axis=0, concat_axis=0, tiled=True)
    recv = recv_flat.reshape(devices * CHUNK, 128)

    edge = [f((24, rows_here), F32)] * 2 + [f((24, cols_here), F32)] * 2
    edges = pl.pallas_call(
        static_edge_kernel,
        out_shape=edge,
        in_specs=[vmem()] * 3,
        out_specs=[vmem()] * 4,
        name="static_edges",
        compiler_params=pltpu.CompilerParams(vmem_limit_bytes=4 * MIB),
    )(ocean_depth, wet_mask, manning)
    grid = f((rows, cols), F32)
    place = jnp.stack(
        [lax.axis_index("gx"), lax.axis_index("gy"), jnp.int32(width_x), jnp.int32(width_y)]
    ).astype(I32)
    count, obs, token = pl.pallas_call(
        gauge_kernel,
        out_shape=[grid, f((steps, rows, cols), F32), f((8, 128), F32)],
        in_specs=[smem()] * 4,
        out_specs=[vmem()] * 3,
        name="gauges",
        compiler_params=pltpu.CompilerParams(vmem_limit_bytes=2 * MIB),
    )(place, gauge_row, gauge_col, observed)

    slots_view = recv_flat.reshape(devices, 1, CHUNK * 128)
    eta, west, east, top, bottom = pl.pallas_call(
        scatter_kernel,
        out_shape=[f((rows_here, cols_here), F32)]
        + [f((32, rows_here), F32)] * 2
        + [f((32, cols_here), F32)] * 2,
        in_specs=[hbm()] + [vmem()] * 6 + [hbm()],
        out_specs=[vmem()] * 5,
        scratch_shapes=[pltpu.SMEM((devices, 1, 128), F32), pltpu.SemaphoreType.DMA]
        + [pltpu.VMEM((rows_here * cols_here // 1024, 8, 128), F32)] * SLOTS,
        name="scatter",
        compiler_params=pltpu.CompilerParams(vmem_limit_bytes=10 * MIB),
    )(slots_view, recv, wet_mask, *edges, token)
    from_east = shifted(west, "gy", -1)
    from_west = shifted(east, "gy", 1)
    tiles = (eta, ocean_depth, wet_mask, manning)
    made = pl.pallas_call(
        tile_kernel,
        out_shape=[grid] * 12,
        in_specs=[vmem()] * 4,
        out_specs=[vmem()] * 12,
        compiler_params=pltpu.CompilerParams(vmem_limit_bytes=MIB),
        name="tile",
    )(*tiles)
    top, bottom = pl.pallas_call(
        rim_kernel,
        out_shape=[f((32, cols), F32)] * 2,
        in_specs=[vmem()] * 4 + [hbm()],
        out_specs=[vmem()] * 2,
        compiler_params=pltpu.CompilerParams(vmem_limit_bytes=MIB),
        name="rims",
    )(from_east, from_west, top, bottom, made[0])
    from_south = shifted(top, "gx", -1)
    from_north = shifted(bottom, "gx", 1)
    framed = pl.pallas_call(
        frame_kernel,
        out_shape=[f((rows, 256), F32)] * 6 + [f((rows, 128), F32)] * 6 + [grid] * 7,
        in_specs=[vmem()] * 11,
        out_specs=[vmem()] * 19,
        scratch_shapes=[pltpu.VMEM((rows_here, 128), F32)] * 4,
        compiler_params=pltpu.CompilerParams(vmem_limit_bytes=2 * MIB),
        name="frame",
    )(*tiles, from_east, from_west, *made[:4], made[9])

    tile = f((rows_here, cols_here), F32)

    def many(n):
        return pltpu.VMEM((n, rows, cols), F32)

    final, adjoint, back = pl.pallas_call(
        solve_kernel,
        out_shape=[tile, tile, f((devices, 128), F32)],
        in_specs=[smem()] * 3 + [vmem()] * 38 + [hbm()],
        out_specs=[vmem()] * 3,
        scratch_shapes=[
            many(steps - 1),
            many(steps - 2),
            many(steps - 1),
            many(steps - 2),
            many(steps - 2),
            many(steps - 1),
            many(steps - 1),
            pltpu.VMEM((rows, cols), F32),
            pltpu.VMEM((rows, cols), F32),
            pltpu.VMEM((rows, cols), F32),
            pltpu.VMEM((rows // 8 * (cols_here // 128), 8, 128), F32),
            pltpu.VMEM((SLOTS, devices, 128), F32),
            pltpu.VMEM((steps * per_tile, 128), F32),
            pltpu.SMEM((devices, 1, 128), F32),
            pltpu.SemaphoreType.DMA,
        ],
        compiler_params=pltpu.CompilerParams(vmem_limit_bytes=22 * MIB),
        name="solve",
    )(
        place, gauge_row, gauge_col, *made, *framed,
        from_north, from_south, top, bottom, count, obs, recv, slots_view,
    )
    returned = lax.all_to_all(back, both, split_axis=0, concat_axis=0, tiled=True)
    readings = (
        returned[:, SLOTS : SLOTS + steps * per_tile]
        .reshape(devices, steps, per_tile)
        .transpose(1, 0, 2)
        .reshape(steps, gauges)
    )
    fault_of = table[:, 8 : 8 + SLOTS].astype(I32) - 1
    mine = fault_of[:, :, None] == jnp.arange(faults, dtype=I32)[None, None, :]
    grad_slip = (
        jnp.sum(jnp.where(mine, returned[:, :SLOTS, None], 0.0), axis=(0, 1)) / fault_slip
    )
    return (final, readings, adjoint, grad_slip)


def solution(mesh):
    placed = (
        P("gx", "gy"),
        P("gx", "gy"),
        P("gx", "gy"),
        P(("gx", "gy")),
        P(("gx", "gy"), None, None),
        P(("gx", "gy"), None),
        P(("gx", "gy")),
        P(),
        P(),
        P(),
    )
    return jax.shard_map(
        body,
        mesh=mesh,
        in_specs=placed,
        out_specs=(P("gx", "gy"), P(), P("gx", "gy"), P(("gx", "gy"))),
        check_vma=False,
    )
```

```python
import math

import jax
import jax.numpy as jnp
from jax import lax
from jax.experimental import pallas as pl
from jax.experimental.pallas import tpu as pltpu
from jax.sharding import PartitionSpec as P

wave_gain = 0.2
mass_gain = 0.2
min_depth = 0.25
speed_floor = 0.01

HALO = 8
CHUNK = 33
SLOTS = 4
LN2 = math.log(2.0)
PUSH = -0.5 * wave_gain
assert abs(PUSH * PUSH - speed_floor) < 1e-12
ROUGH_SCALE = 0.5 * abs(PUSH) * 2.0 ** (7.0 / 3.0)
F32 = jnp.float32
MIB = 1 << 20
GROUP = 8
I32 = jnp.int32


def vmem():
    return pl.BlockSpec(memory_space=pltpu.VMEM)


def smem():
    return pl.BlockSpec(memory_space=pltpu.SMEM)


def hbm():
    return pl.BlockSpec(memory_space=pl.ANY)


def shifted(shard, axis, by):
    devices = lax.axis_size(axis)
    pairs = [(i, i + by) for i in range(devices) if 0 <= i + by < devices]
    return lax.ppermute(shard, axis, pairs)


def pack_kernel(
    slip_ref, tile_ref, block_ref, pattern_hbm, out_ref, table_ref, pattern, row_v, row_s, sems
):
    load = pltpu.make_async_copy(pattern_hbm, pattern, sems.at[0])
    load.start()
    rows = out_ref.shape[0]
    tiles = rows // CHUNK
    entries = tile_ref.shape[1]
    faults = slip_ref.shape[0]
    per_fault = entries // faults
    tile_row = tile_ref[...]
    tile_f = tile_row.astype(F32)
    tile_col = jnp.broadcast_to(tile_f, (128, entries)).T
    here = lax.broadcasted_iota(I32, (entries, 128), 0)
    ranks = []
    for q in range(entries // 128):
        there = lax.broadcasted_iota(I32, (entries, 128), 1) + q * 128
        same = (tile_col == tile_f[:, q * 128 : q * 128 + 128]) & (here < there)
        ranks.append(jnp.sum(jnp.where(same, 1.0, 0.0), axis=0, keepdims=True))
    rank = jnp.concatenate(ranks, axis=1).astype(I32)
    row_v[...] = tile_row * CHUNK + rank * 8
    place_rows = pltpu.make_async_copy(row_v, row_s, sems.at[1])
    place_rows.start()
    fault = lax.broadcasted_iota(I32, (1, entries), 1) // per_fault
    slot = lax.broadcasted_iota(I32, (128, entries), 0)
    facts = jnp.where(slot == rank, block_ref[...], 0) + jnp.where(slot == rank + 8, fault + 1, 0)
    hot = jnp.where(lax.broadcasted_iota(I32, (tiles, entries), 0) == tile_row, 1.0, 0.0)
    table_ref[...] = lax.dot_general(
        hot.astype(jnp.bfloat16),
        facts.astype(F32).astype(jnp.bfloat16),
        (((1,), (1,)), ((), ())),
        preferred_element_type=F32,
    )
    zero = jnp.zeros((8, 128), F32)

    def clear(i, c):
        out_ref[pl.ds(pl.multiple_of(i * 8, 8), 8), :] = zero
        return c

    lax.fori_loop(0, rows // 8, clear, 0, unroll=16)
    for t in range(tiles):
        out_ref[t * CHUNK + 32 : t * CHUNK + 33, :] = table_ref[t : t + 1, :]
    place_rows.wait()
    load.wait()

    def place(s, c):
        slip = slip_ref[s]
        for j in range(per_fault):
            i = s * per_fault + j
            out_ref[pl.ds(row_s[0, i], 8), :] = pattern[i] * slip
        return c

    lax.fori_loop(0, faults, place, 0)


def edges_of(first, last):
    lane = lax.broadcasted_iota(I32, first.shape, 1)
    both = jnp.where(lane < 64, first, last).T
    return both[0:8], both[120:128]


def side_block(east, west):
    rows = east.shape[1]
    gap = jnp.zeros((128 - 16, rows), F32)
    return jnp.concatenate([east, gap, west], axis=0).T


def meta_copy(meta_hbm, meta, sem):
    return pltpu.make_async_copy(meta_hbm.at[:, :, pl.ds(8 * SLOTS * 128, 128)], meta, sem)


def scatter_kernel(
    meta_hbm, recv_ref, wet_ref, west_in, east_in, top_in, bottom_in, after,
    eta_ref, west_ref, east_ref, top_ref, bottom_ref, meta, sem, *acc,
):
    del after
    load = meta_copy(meta_hbm, meta, sem)
    load.start()
    tiles = recv_ref.shape[0] // CHUNK
    rows, cols = eta_ref.shape
    across = cols // 128
    zero = jnp.zeros((8, 128), F32)

    def clear(i, c):
        for a in acc:
            a[i] = zero
        return c

    lax.fori_loop(0, acc[0].shape[0], clear, 0, unroll=8)
    for dst, src in (
        (west_ref, west_in), (east_ref, east_in), (top_ref, top_in), (bottom_ref, bottom_in)
    ):
        dst[0:24, :] = src[...]
    load.wait()

    def add(i, c):
        base = pl.multiple_of(i * (8 * CHUNK), 8)
        for u in range(8):
            for j in range(SLOTS):
                b = meta[i * 8 + u, 0, j].astype(I32)
                acc[j][b] = acc[j][b] + recv_ref[pl.ds(base + (u * CHUNK + 8 * j), 8), :]
        return c

    lax.fori_loop(0, tiles // 8, add, 0)

    def merge(i, c):
        r = pl.multiple_of(i * 8, 8)
        for q in range(across):
            b = i * across + q
            total = (acc[0][b] + acc[1][b]) + (acc[2][b] + acc[3][b])
            wet = wet_ref[pl.ds(r, 8), q * 128 : q * 128 + 128].astype(F32)
            eta_ref[pl.ds(r, 8), q * 128 : q * 128 + 128] = total * wet
        return c

    lax.fori_loop(0, rows // 8, merge, 0, unroll=2)
    west, east = edges_of(eta_ref[:, 0:128], eta_ref[:, cols - 128 : cols])
    west_ref[24:32] = west
    east_ref[24:32] = east
    top_ref[24:32] = eta_ref[0:8, :]
    bottom_ref[24:32] = eta_ref[rows - 8 : rows, :]


def static_edge_kernel(
    depth_ref, wet_ref, fric_ref, west_ref, east_ref, top_ref, bottom_ref
):
    rows, cols = depth_ref.shape
    for n, ref in enumerate((depth_ref, wet_ref, fric_ref)):
        at = slice(8 * n, 8 * n + 8)
        west, east = edges_of(ref[:, 0:128].astype(F32), ref[:, cols - 128 : cols].astype(F32))
        west_ref[at] = west
        east_ref[at] = east
        top_ref[at] = ref[0:8, :].astype(F32)
        bottom_ref[at] = ref[rows - 8 : rows, :].astype(F32)


def rim_kernel(east_ref, west_ref, top_in, bottom_in, after, top_ref, bottom_ref):
    del after
    fields = east_ref.shape[0] // 8
    rows = east_ref.shape[1]
    cols = top_in.shape[1]
    lane = lax.broadcasted_iota(I32, (8, 128), 1)
    for src, out, first, keep in (
        (top_in, top_ref, 0, slice(0, 8)),
        (bottom_in, bottom_ref, rows - 128, slice(120, 128)),
    ):
        pieces = []
        for n in range(fields):
            at = slice(8 * n, 8 * n + 8)
            pieces += [west_ref[at, first : first + 128], east_ref[at, first : first + 128]]
        pieces.append(jnp.zeros((128 - 16 * fields, 128), F32))
        corners = jnp.concatenate(pieces, axis=0).T[keep]
        for n in range(fields):
            at = slice(8 * n, 8 * n + 8)
            out[at, 0:cols] = src[at, :]
            out[at, cols:] = jnp.where(
                (lane < 8) | (lane >= 120), pltpu.roll(corners, 128 - 16 * n - 8, 1), 0.0
            )


def row_iota(shape):
    return lax.broadcasted_iota(I32, shape, 0)


def gauge_kernel(place_ref, row_ref, col_ref, obs_ref, count_out, obs_out, token_out):
    token_out[...] = jnp.zeros(token_out.shape, F32)
    steps, rows, cols = obs_out.shape
    own_rows = rows - 2 * HALO
    own_cols = cols - 128
    gx, gy, wx, wy = place_ref[0], place_ref[1], place_ref[2], place_ref[3]
    per = row_ref.shape[0] // (wx * wy)
    zero = jnp.zeros((8, cols), F32)

    def clear(i, c):
        r = pl.multiple_of(i * 8, 8)
        count_out[pl.ds(r, 8), :] = zero
        for k in range(steps):
            obs_out[k, pl.ds(r, 8), :] = zero
        return c

    lax.fori_loop(0, rows // 8, clear, 0)
    sub = row_iota((8, 128))
    lane = lax.broadcasted_iota(I32, (8, 128), 1)

    for dx in (-1, 0, 1):
        for dy in (-1, 0, 1):
            tx = gx + dx
            ty = gy + dy
            inside = (tx >= 0) & (tx < wx) & (ty >= 0) & (ty < wy)
            first = jnp.where(inside, (tx * wy + ty) * per, 0)

            def one(g, c, first=first, inside=inside):
                r = row_ref[first + g] - gx * own_rows + HALO
                q = col_ref[first + g] - gy * own_cols
                ok = inside & (r >= 0) & (r < rows) & (q >= -HALO) & (q < own_cols + HALO)
                q = jnp.where(q < 0, q + cols, q)

                @pl.when(ok)
                def _():
                    rb = pl.multiple_of(r // 8 * 8, 8)
                    cb = pl.multiple_of(q // 128 * 128, 128)
                    hit = (sub == r % 8) & (lane == q % 128)
                    at = (pl.ds(rb, 8), pl.ds(cb, 128))
                    count_out[at] = count_out[at] + jnp.where(hit, 1.0, 0.0)
                    for k in range(steps):
                        at_k = (k,) + at
                        obs_out[at_k] = obs_out[at_k] + jnp.where(hit, obs_ref[k, first + g], 0.0)

                return c

            lax.fori_loop(0, per, one, 0)


def face(f, s, sn, dd, rr, ww):
    x = dd + (s + sn)
    total = jnp.maximum(x, 2.0 * min_depth)
    diff = sn - s
    push = total * diff
    if f is not None:
        push = push + f
    t = push * push + 1.0
    y = (rr * jnp.exp2(jnp.log(total) * (-7.0 / 3.0 / LN2))) * lax.rsqrt(t)
    inv = 1.0 / (t * y + 1.0)
    wi = ww * inv
    flux = wi * push
    a = (wi * inv) * (y + 1.0)
    depth_part = (flux - flux * inv) * ((7.0 / 3.0) / total)
    share = jnp.where(
        x > 2.0 * min_depth, 1.0, jnp.where(x == 2.0 * min_depth, 0.5, 0.0)
    )
    u = share * (depth_part + a * diff)
    v = a * total
    return flux, a, u + v, u - v


def merge_rows(tiles):
    sub = row_iota((8, 128))
    for width in (1, 2, 4):
        low = (sub & width) == 0
        tiles = [
            jnp.where(low, p, q) + pltpu.roll(jnp.where(low, q, p), width, 0)
            for p, q in zip(tiles[0::2], tiles[1::2])
        ]
    return tiles[0]


def statics_of(d, w, m, d_next, w_next, m_next):
    return d + d_next, ROUGH_SCALE * (m + m_next), w * w_next


def south_of(here, after):
    last = row_iota(here.shape) == 7
    return jnp.where(last, pltpu.roll(after, 7, 0), pltpu.roll(here, 7, 0))


def north_of(flux, before):
    first = row_iota(flux.shape) == 0
    return jnp.where(first, pltpu.roll(before, 1, 0), pltpu.roll(flux, 1, 0))


def rows_at(i):
    return pl.ds(pl.multiple_of(i * 8, 8), 8)


def divergence(east, south, before):
    return (east - pltpu.roll(east, 1, 1)) + (south - north_of(south, before))


def store_face(refs, at, statics, made):
    flux, _, p, q = made
    for ref, value in zip(refs, (*statics, flux, p, q)):
        ref[at] = value


def tile_kernel(eta_ref, depth_ref, wet_ref, fric_ref, *out):
    east, south = out[:6], out[6:]
    rows, cols = eta_ref.shape
    fields = (depth_ref, wet_ref, fric_ref, eta_ref)
    keep = cols - 128

    def eastward(i, c):
        here = [ref[rows_at(i), :].astype(F32) for ref in fields]
        there = [pltpu.roll(v, cols - 1, 1)[:, :keep] for v in here]
        here = [v[:, :keep] for v in here]
        statics = statics_of(*here[:3], *there[:3])
        store_face(east, (rows_at(i + 1), slice(0, keep)), statics, face(None, here[3], there[3], *statics))
        return c

    def southward(i, c):
        here = [ref[rows_at(i), :].astype(F32) for ref in fields]
        there = [south_of(v, ref[rows_at(i + 1), :].astype(F32)) for v, ref in zip(here, fields)]
        statics = statics_of(*here[:3], *there[:3])
        store_face(south, (rows_at(i + 1), slice(0, cols)), statics, face(None, here[3], there[3], *statics))
        return c

    lax.fori_loop(0, rows // 8, eastward, 0, unroll=4)
    lax.fori_loop(0, rows // 8 - 1, southward, 0, unroll=3)


def frame_kernel(
    eta_ref, depth_ref, wet_ref, fric_ref, east_ref, west_ref, dde, rre, wwe, fe, fs, *refs
):
    east, south = refs[:6], refs[6:12]
    surf0, wet, surf1, fe1, ae1, pe1, qe1 = refs[12:19]
    sides = refs[19:]
    rows, cols = eta_ref.shape
    fields = (depth_ref, wet_ref, fric_ref, eta_ref)
    blocks = rows // 8
    for n, side in enumerate(sides):
        side[...] = side_block(east_ref[8 * n : 8 * n + 8], west_ref[8 * n : 8 * n + 8])

    def frame(i, c):
        at = rows_at(i)
        out = rows_at(i + 1)
        after = rows_at(jnp.minimum(i + 1, blocks - 1))
        corner = [side[at, :] for side in sides]
        tail = [ref[at, cols - 128 :].astype(F32) for ref in fields]
        head = [ref[at, 0:128].astype(F32) for ref in fields]
        here = [jnp.concatenate(p, axis=1) for p in zip(tail, corner)]
        there = [
            pltpu.roll(jnp.concatenate(p, axis=1), 3 * 128 - 1, 1)[:, :256]
            for p in zip(tail, corner, head)
        ]
        statics = statics_of(*here[:3], *there[:3])
        store_face(east, (out, slice(None)), statics, face(None, here[3], there[3], *statics))
        there = [south_of(v, side[after, :]) for v, side in zip(corner, sides)]
        statics = statics_of(*corner[:3], *there[:3])
        store_face(south, (out, slice(None)), statics, face(None, corner[3], there[3], *statics))
        for ref, n in ((wet, 1), (surf0, 3)):
            ref[out, 0:cols] = fields[n][at, :].astype(F32)
            ref[out, cols:] = corner[n]
        return c

    lax.fori_loop(0, blocks, frame, 0, unroll=4)
    cut = cols - 128

    def whole(left, right, at):
        width = left.shape[1] - right.shape[1]
        return jnp.concatenate([left[at, 0:width], right[at, :]], axis=1)

    def surface(i, before):
        at = rows_at(i)
        flux = whole(fs, south[3], at)
        div = divergence(whole(fe, east[3], at), flux, before)
        surf1[at, :] = wet[at, :] * (surf0[at, :] - (mass_gain * PUSH) * div)
        return flux

    lax.fori_loop(2, blocks, surface, whole(fs, south[3], rows_at(1)), unroll=6)

    def eastward(i, c):
        at = rows_at(i)
        s = surf1[at, :]
        statics = [whole(a, b, at) for a, b in ((dde, east[0]), (rre, east[1]), (wwe, east[2]))]
        made = face(whole(fe, east[3], at), s, pltpu.roll(s, s.shape[1] - 1, 1), *statics)
        for ref, value in zip((fe1, ae1, pe1, qe1), made):
            ref[at, :] = value
        return c

    lax.fori_loop(2, blocks, eastward, 0, unroll=6)


def solve_kernel(*refs):
    place_ref, grow_ref, gcol_ref = refs[:3]
    east0, south0, east_part, south_part = (refs[3 + 6 * n : 9 + 6 * n] for n in range(4))
    surf0, wet, surf1, fe1, ae1, pe1, qe1 = refs[27:34]
    north_ref, south_ref, top_ref, bottom_ref, count, obs, recv, meta_hbm = refs[34:42]
    final_ref, adj_ref, back_ref = refs[42:45]
    (
        surf_s, ae_s, as_s, pe_s, qe_s, ps_s, qs_s,
        adj, ce, cs, spread, turned, west, xe, xs, grads, parts, reads, meta, sem,
    ) = refs[45:]
    steps, rows, cols = obs.shape
    own_rows, own_cols = final_ref.shape
    dde, rre, wwe, fe0, pe0, qe0 = east0
    dds, rrs, wws, fs, ps0, qs0 = south0
    surf = [surf0, surf1] + [surf_s.at[n] for n in range(steps - 1)]
    ae = [None, ae1] + [ae_s.at[n] for n in range(steps - 2)]
    pe = [pe0, pe1] + [pe_s.at[n] for n in range(steps - 2)]
    qe = [qe0, qe1] + [qe_s.at[n] for n in range(steps - 2)]
    as_ = [None] + [as_s.at[n] for n in range(steps - 1)]
    ps = [ps0] + [ps_s.at[n] for n in range(steps - 1)]
    qs = [qs0] + [qs_s.at[n] for n in range(steps - 1)]
    load = meta_copy(meta_hbm, meta, sem)
    load.start()
    sub = row_iota((8, cols))
    last = sub == 7
    firstrow = sub == 0
    blocks = rows // 8
    across = own_cols // 128

    def nxt(i):
        return pl.multiple_of(jnp.minimum(i * 8 + 8, rows - 8), 8)

    def take(i, c):
        at = rows_at(i)
        for whole, part in zip(east0 + south0, east_part + south_part):
            whole[at, cols - part.shape[1] :] = part[at, :]
        return c

    lax.fori_loop(1, blocks - 1, take, 0, unroll=2)

    def field(ref, n):
        return ref[8 * n : 8 * n + 8, :]

    def edge_face(refs, i, ref, neighbour):
        here = [field(ref, n) for n in range(4)]
        there = neighbour(here)
        statics = statics_of(*here[:3], *there[:3])
        store_face(refs, (rows_at(i), slice(None)), statics, face(None, here[3], there[3], *statics))

    def east_of(here):
        return [pltpu.roll(v, cols - 1, 1) for v in here]

    def above(ref):
        return lambda here: [south_of(v, field(ref, n)) for n, v in enumerate(here)]

    for i, ref in ((0, north_ref), (blocks - 1, south_ref)):
        surf0[rows_at(i), :] = field(ref, 3)
        wet[rows_at(i), :] = field(ref, 1)
        edge_face(east0, i, ref, east_of)
    edge_face(south0, 0, north_ref, above(top_ref))
    edge_face(south0, blocks - 2, bottom_ref, above(south_ref))
    edge_face(south0, blocks - 1, south_ref, above(south_ref))
    rim = (0, 1, blocks - 2, blocks - 1)
    for i in rim:
        at = rows_at(i)
        before = fs[rows_at(max(i - 1, 0)), :]
        div = divergence(fe0[at, :], fs[at, :], before)
        surf1[at, :] = wet[at, :] * (surf0[at, :] - (mass_gain * PUSH) * div)

    def pipelined(first, end, main, carry, begin, finish):
        groups = (end - first) // GROUP

        def step(g, carry):
            base = first + g * GROUP
            prior = jnp.maximum(base - GROUP, first)
            held = [begin(prior + u) for u in range(GROUP)]
            for u in range(GROUP):
                carry = main(base + u, carry)
            for u in range(GROUP):
                finish(prior + u, held[u])
            return carry

        carry = lax.fori_loop(0, groups, step, carry)
        done = first + groups * GROUP
        held = [begin(done - GROUP + u) for u in range(GROUP)]
        for i in range(done, end):
            carry = main(i, carry)
        for u in range(GROUP):
            finish(done - GROUP + u, held[u])
        held = [begin(i) for i in range(done, end)]
        for i in range(done, end):
            finish(i, held[i - done])
        return carry

    def rotate_into(src, dst, by):
        def begin(i):
            return pltpu.roll(src[rows_at(i), :], by, 1)

        def finish(i, value):
            dst[rows_at(i), :] = value

        return begin, finish

    def nothing(i, c):
        return c

    for k in range(1, steps):

        def eastward(i, c, k=k):
            here = rows_at(i)
            s = surf[k][here, :]
            s_east = pltpu.roll(s, cols - 1, 1) if k == 1 else turned[here, :]
            old = fe0 if k == 1 else fe1
            flux, a, p, q = face(old[here, :], s, s_east, dde[here, :], rre[here, :], wwe[here, :])
            fe1[here, :] = flux
            ae[k][here, :] = a
            pe[k][here, :] = p
            qe[k][here, :] = q
            return c

        def southward(i, carry, k=k):
            s, s_up, f_down = carry
            here = rows_at(i)
            sn = surf[k][pl.ds(nxt(i), 8), :]
            sn_up = pltpu.roll(sn, 7, 0)
            flux, a, p, q = face(
                fs[here, :], s, jnp.where(last, sn_up, s_up), dds[here, :], rrs[here, :], wws[here, :]
            )
            fs[here, :] = flux
            as_[k][here, :] = a
            ps[k][here, :] = p
            qs[k][here, :] = q
            down = pltpu.roll(flux, 1, 0)
            div = fe1[here, :] - west[here, :]
            div = div + (flux - jnp.where(firstrow, f_down, down))
            surf[k + 1][here, :] = wet[here, :] * (s - (mass_gain * PUSH) * div)
            return sn, sn_up, down

        turn_flux = rotate_into(fe1, west, 1)
        if k == 1:
            for i in rim:
                eastward(i, 0)
            pipelined(0, blocks, nothing, 0, *turn_flux)
        else:
            pipelined(0, blocks, eastward, 0, *turn_flux)
        s0 = surf[k][0:8, :]
        start = (s0, pltpu.roll(s0, 7, 0), jnp.zeros((8, cols), F32))
        if k < steps - 1:
            pipelined(0, blocks, southward, start, *rotate_into(surf[k + 1], turned, cols - 1))
        else:
            lax.fori_loop(0, blocks, southward, start, unroll=GROUP)

    final_ref[...] = surf[steps][HALO : HALO + own_rows, 0:own_cols]

    gx, gy = place_ref[0], place_ref[1]
    lane8 = lax.broadcasted_iota(I32, (8, 128), 1)
    sub8 = row_iota((8, 128))
    per = grow_ref.shape[0] // (place_ref[2] * place_ref[3])
    per_tile = reads.shape[0] // steps
    first = (gx * place_ref[3] + gy) * per
    for g0 in range(0, per_tile, 8):
        spots = []
        for g in range(g0, g0 + 8):
            r = jnp.clip(grow_ref[first + g] - gx * own_rows, 0, own_rows - 1) + HALO
            q = jnp.clip(gcol_ref[first + g] - gy * own_cols, 0, own_cols - 1)
            at = (
                pl.ds(pl.multiple_of(r // 8 * 8, 8), 8),
                pl.ds(pl.multiple_of(q // 128 * 128, 128), 128),
            )
            spots.append((at, (sub8 == r % 8) & (lane8 == q % 128)))
        for k in range(steps):
            picked = [jnp.where(hit, surf[k + 1][at], 0.0) for at, hit in spots]
            reads[k * per_tile + g0 : k * per_tile + g0 + 8, :] = merge_rows(picked)
    values = jnp.sum(reads[...], axis=1, keepdims=True)
    spots = row_iota(reads.shape) + SLOTS == lax.broadcasted_iota(I32, reads.shape, 1)
    reading_row = jnp.sum(jnp.where(spots, values, 0.0), axis=0, keepdims=True)

    load.wait()

    def seed(at, k):
        return count[at, :] * surf[k + 1][at, :] - obs[k, at, :]

    def begin_adjoint(i, c):
        at = rows_at(i)
        spread[at, :] = wet[at, :] * seed(at, steps - 1)
        return c

    turn_spread = rotate_into(spread, turned, cols - 1)
    turn_x = rotate_into(xe, west, 1)
    pipelined(0, blocks, begin_adjoint, 0, *turn_spread)
    for k in reversed(range(steps)):

        def gather(i, c, k=k):
            at = rows_at(i)
            b = spread[at, :]
            ge = (mass_gain * PUSH) * (turned[at, :] - b)
            gs = (mass_gain * PUSH) * (south_of(b, spread[pl.ds(nxt(i), 8), :]) - b)
            if k < steps - 1:
                ge = ge + ce[at, :]
                gs = gs + cs[at, :]
            if k > 0:
                ce[at, :] = ge * ae[k][at, :]
                cs[at, :] = gs * as_[k][at, :]
            xe[at, :] = ge * pe[k][at, :]
            xs[at, :] = gs * ps[k][at, :]
            adj[at, :] = (b + ge * qe[k][at, :]) + gs * qs[k][at, :]
            return c

        def collect(i, c, k=k):
            at = rows_at(i)
            before = xs[pl.ds(pl.multiple_of(jnp.maximum(i * 8 - 8, 0), 8), 8), :]
            out = (adj[at, :] + west[at, :]) + north_of(xs[at, :], before)
            if k > 0:
                spread[at, :] = wet[at, :] * (out + seed(at, k - 1))
            else:
                out = out[:, 0:own_cols]
                adj_ref[rows_at(i - HALO // 8), :] = out
                scaled = out * wet[at, 0:own_cols]
                for q in range(across):
                    grads[(i - HALO // 8) * across + q] = scaled[:, q * 128 : q * 128 + 128]
            return c

        pipelined(0, blocks, gather, 0, *turn_x)
        if k > 0:
            pipelined(0, blocks, collect, 0, *turn_spread)
        else:
            lax.fori_loop(HALO // 8, blocks - HALO // 8, collect, 0, unroll=GROUP)

    tiles = recv.shape[0] // CHUNK

    def sens(i, c):
        for j in range(SLOTS):
            products = []
            for u in range(8):
                t = i * 8 + u
                b = meta[t, 0, j].astype(I32)
                products.append(grads[b] * recv[pl.ds(t * CHUNK + 8 * j, 8), :])
            parts[j, pl.ds(pl.multiple_of(i * 8, 8), 8), :] = merge_rows(products)
        return c

    lax.fori_loop(0, tiles // 8, sens, 0)
    lanes = lax.broadcasted_iota(I32, (tiles, 128), 1)
    out = jnp.broadcast_to(reading_row, (tiles, 128))
    for j in range(SLOTS):
        out = jnp.where(lanes == j, jnp.sum(parts[j], axis=1, keepdims=True), out)
    back_ref[...] = out


def body(
    ocean_depth,
    wet_mask,
    manning,
    fault_slip,
    pattern,
    foot_tile,
    foot_block,
    gauge_row,
    gauge_col,
    observed,
):
    rows_here, cols_here = ocean_depth.shape
    steps, gauges = observed.shape
    width_x = lax.axis_size("gx")
    width_y = lax.axis_size("gy")
    devices = width_x * width_y
    entries = pattern.shape[0]
    faults = fault_slip.shape[0]
    per_fault = entries // faults
    per_tile = gauges // devices
    both = ("gx", "gy")
    rows, cols = rows_here + 2 * HALO, cols_here + 128
    f = jax.ShapeDtypeStruct

    packed, table = pl.pallas_call(
        pack_kernel,
        out_shape=[f((devices * CHUNK, 128), F32), f((devices, 128), F32)],
        in_specs=[smem(), vmem(), vmem(), hbm()],
        out_specs=[vmem()] * 2,
        scratch_shapes=[
            pltpu.VMEM(pattern.shape, F32),
            pltpu.VMEM((1, entries), I32),
            pltpu.SMEM((1, entries), I32),
            pltpu.SemaphoreType.DMA((2,)),
        ],
        name="pack",
    )(fault_slip, foot_tile.reshape(1, entries), foot_block.reshape(1, entries), pattern)
    recv_flat = lax.all_to_all(packed.reshape(-1), both, split_axis=0, concat_axis=0, tiled=True)
    recv = recv_flat.reshape(devices * CHUNK, 128)

    edge = [f((24, rows_here), F32)] * 2 + [f((24, cols_here), F32)] * 2
    edges = pl.pallas_call(
        static_edge_kernel,
        out_shape=edge,
        in_specs=[vmem()] * 3,
        out_specs=[vmem()] * 4,
        name="static_edges",
        compiler_params=pltpu.CompilerParams(vmem_limit_bytes=4 * MIB),
    )(ocean_depth, wet_mask, manning)
    grid = f((rows, cols), F32)
    place = jnp.stack(
        [lax.axis_index("gx"), lax.axis_index("gy"), jnp.int32(width_x), jnp.int32(width_y)]
    ).astype(I32)
    count, obs, token = pl.pallas_call(
        gauge_kernel,
        out_shape=[grid, f((steps, rows, cols), F32), f((8, 128), F32)],
        in_specs=[smem()] * 4,
        out_specs=[vmem()] * 3,
        name="gauges",
        compiler_params=pltpu.CompilerParams(vmem_limit_bytes=2 * MIB),
    )(place, gauge_row, gauge_col, observed)

    slots_view = recv_flat.reshape(devices, 1, CHUNK * 128)
    eta, west, east, top, bottom = pl.pallas_call(
        scatter_kernel,
        out_shape=[f((rows_here, cols_here), F32)]
        + [f((32, rows_here), F32)] * 2
        + [f((32, cols_here), F32)] * 2,
        in_specs=[hbm()] + [vmem()] * 6 + [hbm()],
        out_specs=[vmem()] * 5,
        scratch_shapes=[pltpu.SMEM((devices, 1, 128), F32), pltpu.SemaphoreType.DMA]
        + [pltpu.VMEM((rows_here * cols_here // 1024, 8, 128), F32)] * SLOTS,
        name="scatter",
        compiler_params=pltpu.CompilerParams(vmem_limit_bytes=10 * MIB),
    )(slots_view, recv, wet_mask, *edges, token)
    from_east = shifted(west, "gy", -1)
    from_west = shifted(east, "gy", 1)
    tiles = (eta, ocean_depth, wet_mask, manning)
    made = pl.pallas_call(
        tile_kernel,
        out_shape=[grid] * 12,
        in_specs=[vmem()] * 4,
        out_specs=[vmem()] * 12,
        compiler_params=pltpu.CompilerParams(vmem_limit_bytes=MIB),
        name="tile",
    )(*tiles)
    top, bottom = pl.pallas_call(
        rim_kernel,
        out_shape=[f((32, cols), F32)] * 2,
        in_specs=[vmem()] * 4 + [hbm()],
        out_specs=[vmem()] * 2,
        compiler_params=pltpu.CompilerParams(vmem_limit_bytes=MIB),
        name="rims",
    )(from_east, from_west, top, bottom, made[0])
    from_south = shifted(top, "gx", -1)
    from_north = shifted(bottom, "gx", 1)
    framed = pl.pallas_call(
        frame_kernel,
        out_shape=[f((rows, 256), F32)] * 6 + [f((rows, 128), F32)] * 6 + [grid] * 7,
        in_specs=[vmem()] * 11,
        out_specs=[vmem()] * 19,
        scratch_shapes=[pltpu.VMEM((rows_here, 128), F32)] * 4,
        compiler_params=pltpu.CompilerParams(vmem_limit_bytes=2 * MIB),
        name="frame",
    )(*tiles, from_east, from_west, *made[:4], made[9])

    tile = f((rows_here, cols_here), F32)

    def many(n):
        return pltpu.VMEM((n, rows, cols), F32)

    final, adjoint, back = pl.pallas_call(
        solve_kernel,
        out_shape=[tile, tile, f((devices, 128), F32)],
        in_specs=[smem()] * 3 + [vmem()] * 38 + [hbm()],
        out_specs=[vmem()] * 3,
        scratch_shapes=[
            many(steps - 1),
            many(steps - 2),
            many(steps - 1),
            many(steps - 2),
            many(steps - 2),
            many(steps - 1),
            many(steps - 1),
            *[pltpu.VMEM((rows, cols), F32)] * 8,
            pltpu.VMEM((rows_here // 8 * (cols_here // 128), 8, 128), F32),
            pltpu.VMEM((SLOTS, devices, 128), F32),
            pltpu.VMEM((steps * per_tile, 128), F32),
            pltpu.SMEM((devices, 1, 128), F32),
            pltpu.SemaphoreType.DMA,
        ],
        compiler_params=pltpu.CompilerParams(vmem_limit_bytes=26 * MIB),
        name="solve",
    )(
        place, gauge_row, gauge_col, *made, *framed,
        from_north, from_south, top, bottom, count, obs, recv, slots_view,
    )
    returned = lax.all_to_all(back, both, split_axis=0, concat_axis=0, tiled=True)
    readings = (
        returned[:, SLOTS : SLOTS + steps * per_tile]
        .reshape(devices, steps, per_tile)
        .transpose(1, 0, 2)
        .reshape(steps, gauges)
    )
    fault_of = table[:, 8 : 8 + SLOTS].astype(I32) - 1
    mine = fault_of[:, :, None] == jnp.arange(faults, dtype=I32)[None, None, :]
    grad_slip = (
        jnp.sum(jnp.where(mine, returned[:, :SLOTS, None], 0.0), axis=(0, 1)) / fault_slip
    )
    return (final, readings, adjoint, grad_slip)


def solution(mesh):
    placed = (
        P("gx", "gy"),
        P("gx", "gy"),
        P("gx", "gy"),
        P(("gx", "gy")),
        P(("gx", "gy"), None, None),
        P(("gx", "gy"), None),
        P(("gx", "gy")),
        P(),
        P(),
        P(),
    )
    return jax.shard_map(
        body,
        mesh=mesh,
        in_specs=placed,
        out_specs=(P("gx", "gy"), P(), P("gx", "gy"), P(("gx", "gy"))),
        check_vma=False,
    )
```

```python
import math

import jax
import jax.numpy as jnp
from jax import lax
from jax.experimental import pallas as pl
from jax.experimental.pallas import tpu as pltpu
from jax.sharding import PartitionSpec as P

wave_gain = 0.2
mass_gain = 0.2
min_depth = 0.25
speed_floor = 0.01

HALO = 8
CHUNK = 33
SLOTS = 4
LN2 = math.log(2.0)
PUSH = -0.5 * wave_gain
assert abs(PUSH * PUSH - speed_floor) < 1e-12
ROUGH_SCALE = 0.5 * abs(PUSH) * 2.0 ** (7.0 / 3.0)
F32 = jnp.float32
MIB = 1 << 20
GROUP = 8
I32 = jnp.int32


def vmem():
    return pl.BlockSpec(memory_space=pltpu.VMEM)


def smem():
    return pl.BlockSpec(memory_space=pltpu.SMEM)


def hbm():
    return pl.BlockSpec(memory_space=pl.ANY)


def shifted(shard, axis, by):
    devices = lax.axis_size(axis)
    pairs = [(i, i + by) for i in range(devices) if 0 <= i + by < devices]
    return lax.ppermute(shard, axis, pairs)


def pack_kernel(
    slip_ref, tile_ref, block_ref, pattern_hbm, out_ref, table_ref, pattern, row_v, row_s, sems
):
    load = pltpu.make_async_copy(pattern_hbm, pattern, sems.at[0])
    load.start()
    rows = out_ref.shape[0]
    tiles = rows // CHUNK
    entries = tile_ref.shape[1]
    faults = slip_ref.shape[0]
    per_fault = entries // faults
    tile_row = tile_ref[...]
    tile_f = tile_row.astype(F32)
    tile_col = jnp.broadcast_to(tile_f, (128, entries)).T
    here = lax.broadcasted_iota(I32, (entries, 128), 0)
    ranks = []
    for q in range(entries // 128):
        there = lax.broadcasted_iota(I32, (entries, 128), 1) + q * 128
        same = (tile_col == tile_f[:, q * 128 : q * 128 + 128]) & (here < there)
        ranks.append(jnp.sum(jnp.where(same, 1.0, 0.0), axis=0, keepdims=True))
    rank = jnp.concatenate(ranks, axis=1).astype(I32)
    row_v[...] = tile_row * CHUNK + rank * 8
    place_rows = pltpu.make_async_copy(row_v, row_s, sems.at[1])
    place_rows.start()
    fault = lax.broadcasted_iota(I32, (1, entries), 1) // per_fault
    slot = lax.broadcasted_iota(I32, (128, entries), 0)
    facts = jnp.where(slot == rank, block_ref[...], 0) + jnp.where(slot == rank + 8, fault + 1, 0)
    hot = jnp.where(lax.broadcasted_iota(I32, (tiles, entries), 0) == tile_row, 1.0, 0.0)
    table_ref[...] = lax.dot_general(
        hot.astype(jnp.bfloat16),
        facts.astype(F32).astype(jnp.bfloat16),
        (((1,), (1,)), ((), ())),
        preferred_element_type=F32,
    )
    zero = jnp.zeros((8, 128), F32)

    def clear(i, c):
        out_ref[pl.ds(pl.multiple_of(i * 8, 8), 8), :] = zero
        return c

    lax.fori_loop(0, rows // 8, clear, 0, unroll=16)
    for t in range(tiles):
        out_ref[t * CHUNK + 32 : t * CHUNK + 33, :] = table_ref[t : t + 1, :]
    place_rows.wait()
    load.wait()

    def place(s, c):
        slip = slip_ref[s]
        for j in range(per_fault):
            i = s * per_fault + j
            out_ref[pl.ds(row_s[0, i], 8), :] = pattern[i] * slip
        return c

    lax.fori_loop(0, faults, place, 0)


def edges_of(first, last):
    lane = lax.broadcasted_iota(I32, first.shape, 1)
    both = jnp.where(lane < 64, first, last).T
    return both[0:8], both[120:128]


def side_block(east, west):
    rows = east.shape[1]
    gap = jnp.zeros((128 - 16, rows), F32)
    return jnp.concatenate([east, gap, west], axis=0).T


def scatter_kernel(
    recv_ref, wet_ref, west_in, east_in, top_in, bottom_in, after,
    eta_ref, west_ref, east_ref, top_ref, bottom_ref, block_out, block_s, sem, *acc,
):
    del after
    tiles = recv_ref.shape[0] // CHUNK
    facts = recv_ref[pl.ds(8 * SLOTS, tiles, stride=CHUNK), :]
    block_out[...] = facts.T[0:8].astype(I32)
    load = pltpu.make_async_copy(block_out, block_s, sem)
    load.start()
    rows, cols = eta_ref.shape
    across = cols // 128
    zero = jnp.zeros((8, 128), F32)

    def clear(i, c):
        for a in acc:
            a[i] = zero
        return c

    lax.fori_loop(0, acc[0].shape[0], clear, 0, unroll=8)
    for dst, src in (
        (west_ref, west_in), (east_ref, east_in), (top_ref, top_in), (bottom_ref, bottom_in)
    ):
        dst[0:24, :] = src[...]
    load.wait()

    def add(i, c):
        base = pl.multiple_of(i * (8 * CHUNK), 8)
        for u in range(8):
            for j in range(SLOTS):
                b = block_s[j, i * 8 + u]
                acc[j][b] = acc[j][b] + recv_ref[pl.ds(base + (u * CHUNK + 8 * j), 8), :]
        return c

    lax.fori_loop(0, tiles // 8, add, 0)

    def merge(i, c):
        r = pl.multiple_of(i * 8, 8)
        for q in range(across):
            b = i * across + q
            total = (acc[0][b] + acc[1][b]) + (acc[2][b] + acc[3][b])
            wet = wet_ref[pl.ds(r, 8), q * 128 : q * 128 + 128].astype(F32)
            eta_ref[pl.ds(r, 8), q * 128 : q * 128 + 128] = total * wet
        return c

    lax.fori_loop(0, rows // 8, merge, 0, unroll=2)
    west, east = edges_of(eta_ref[:, 0:128], eta_ref[:, cols - 128 : cols])
    west_ref[24:32] = west
    east_ref[24:32] = east
    top_ref[24:32] = eta_ref[0:8, :]
    bottom_ref[24:32] = eta_ref[rows - 8 : rows, :]


def static_edge_kernel(
    depth_ref, wet_ref, fric_ref, west_ref, east_ref, top_ref, bottom_ref
):
    rows, cols = depth_ref.shape
    for n, ref in enumerate((depth_ref, wet_ref, fric_ref)):
        at = slice(8 * n, 8 * n + 8)
        west, east = edges_of(ref[:, 0:128].astype(F32), ref[:, cols - 128 : cols].astype(F32))
        west_ref[at] = west
        east_ref[at] = east
        top_ref[at] = ref[0:8, :].astype(F32)
        bottom_ref[at] = ref[rows - 8 : rows, :].astype(F32)


def rim_kernel(east_ref, west_ref, top_in, bottom_in, after, top_ref, bottom_ref):
    del after
    fields = east_ref.shape[0] // 8
    rows = east_ref.shape[1]
    cols = top_in.shape[1]
    lane = lax.broadcasted_iota(I32, (8, 128), 1)
    for src, out, first, keep in (
        (top_in, top_ref, 0, slice(0, 8)),
        (bottom_in, bottom_ref, rows - 128, slice(120, 128)),
    ):
        pieces = []
        for n in range(fields):
            at = slice(8 * n, 8 * n + 8)
            pieces += [west_ref[at, first : first + 128], east_ref[at, first : first + 128]]
        pieces.append(jnp.zeros((128 - 16 * fields, 128), F32))
        corners = jnp.concatenate(pieces, axis=0).T[keep]
        for n in range(fields):
            at = slice(8 * n, 8 * n + 8)
            out[at, 0:cols] = src[at, :]
            out[at, cols:] = jnp.where(
                (lane < 8) | (lane >= 120), pltpu.roll(corners, 128 - 16 * n - 8, 1), 0.0
            )


def row_iota(shape):
    return lax.broadcasted_iota(I32, shape, 0)


def gauge_kernel(place_ref, row_ref, col_ref, obs_ref, count_out, obs_out, token_out):
    token_out[...] = jnp.zeros(token_out.shape, F32)
    steps, rows, cols = obs_out.shape
    own_rows = rows - 2 * HALO
    own_cols = cols - 128
    gx, gy, wx, wy = place_ref[0], place_ref[1], place_ref[2], place_ref[3]
    per = row_ref.shape[0] // (wx * wy)
    zero = jnp.zeros((8, cols), F32)

    def clear(i, c):
        r = pl.multiple_of(i * 8, 8)
        count_out[pl.ds(r, 8), :] = zero
        for k in range(steps):
            obs_out[k, pl.ds(r, 8), :] = zero
        return c

    lax.fori_loop(0, rows // 8, clear, 0)
    sub = row_iota((8, 128))
    lane = lax.broadcasted_iota(I32, (8, 128), 1)

    for dx in (-1, 0, 1):
        for dy in (-1, 0, 1):
            tx = gx + dx
            ty = gy + dy
            inside = (tx >= 0) & (tx < wx) & (ty >= 0) & (ty < wy)
            first = jnp.where(inside, (tx * wy + ty) * per, 0)

            def one(g, c, first=first, inside=inside):
                r = row_ref[first + g] - gx * own_rows + HALO
                q = col_ref[first + g] - gy * own_cols
                ok = inside & (r >= 0) & (r < rows) & (q >= -HALO) & (q < own_cols + HALO)
                q = jnp.where(q < 0, q + cols, q)

                @pl.when(ok)
                def _():
                    rb = pl.multiple_of(r // 8 * 8, 8)
                    cb = pl.multiple_of(q // 128 * 128, 128)
                    hit = (sub == r % 8) & (lane == q % 128)
                    at = (pl.ds(rb, 8), pl.ds(cb, 128))
                    count_out[at] = count_out[at] + jnp.where(hit, 1.0, 0.0)
                    for k in range(steps):
                        at_k = (k,) + at
                        obs_out[at_k] = obs_out[at_k] + jnp.where(hit, obs_ref[k, first + g], 0.0)

                return c

            lax.fori_loop(0, per, one, 0)


def face(f, s, sn, dd, rr, ww):
    x = dd + (s + sn)
    total = jnp.maximum(x, 2.0 * min_depth)
    diff = sn - s
    push = total * diff
    if f is not None:
        push = push + f
    t = push * push + 1.0
    y = (rr * jnp.exp2(jnp.log(total) * (-7.0 / 3.0 / LN2))) * lax.rsqrt(t)
    inv = 1.0 / (t * y + 1.0)
    wi = ww * inv
    flux = wi * push
    a = (wi * inv) * (y + 1.0)
    depth_part = (flux - flux * inv) * ((7.0 / 3.0) / total)
    share = jnp.where(
        x > 2.0 * min_depth, 1.0, jnp.where(x == 2.0 * min_depth, 0.5, 0.0)
    )
    u = share * (depth_part + a * diff)
    v = a * total
    return flux, a, u + v, u - v


def merge_rows(tiles):
    sub = row_iota((8, 128))
    for width in (1, 2, 4):
        low = (sub & width) == 0
        tiles = [
            jnp.where(low, p, q) + pltpu.roll(jnp.where(low, q, p), width, 0)
            for p, q in zip(tiles[0::2], tiles[1::2])
        ]
    return tiles[0]


def statics_of(d, w, m, d_next, w_next, m_next):
    return d + d_next, ROUGH_SCALE * (m + m_next), w * w_next


def south_of(here, after):
    last = row_iota(here.shape) == 7
    return jnp.where(last, pltpu.roll(after, 7, 0), pltpu.roll(here, 7, 0))


def north_of(flux, before):
    first = row_iota(flux.shape) == 0
    return jnp.where(first, pltpu.roll(before, 1, 0), pltpu.roll(flux, 1, 0))


def rows_at(i):
    return pl.ds(pl.multiple_of(i * 8, 8), 8)


def divergence(east, south, before):
    return (east - pltpu.roll(east, 1, 1)) + (south - north_of(south, before))


def store_face(refs, at, statics, made):
    flux, _, p, q = made
    for ref, value in zip(refs, (*statics, flux, p, q)):
        ref[at] = value


def tile_kernel(eta_ref, depth_ref, wet_ref, fric_ref, *out):
    east, south = out[:6], out[6:]
    rows, cols = eta_ref.shape
    fields = (depth_ref, wet_ref, fric_ref, eta_ref)
    keep = cols - 128

    def eastward(i, c):
        here = [ref[rows_at(i), :].astype(F32) for ref in fields]
        there = [pltpu.roll(v, cols - 1, 1)[:, :keep] for v in here]
        here = [v[:, :keep] for v in here]
        statics = statics_of(*here[:3], *there[:3])
        store_face(east, (rows_at(i + 1), slice(0, keep)), statics, face(None, here[3], there[3], *statics))
        return c

    def southward(i, c):
        here = [ref[rows_at(i), :].astype(F32) for ref in fields]
        there = [south_of(v, ref[rows_at(i + 1), :].astype(F32)) for v, ref in zip(here, fields)]
        statics = statics_of(*here[:3], *there[:3])
        store_face(south, (rows_at(i + 1), slice(0, cols)), statics, face(None, here[3], there[3], *statics))
        return c

    lax.fori_loop(0, rows // 8, eastward, 0, unroll=4)
    lax.fori_loop(0, rows // 8 - 1, southward, 0, unroll=3)


def frame_kernel(
    eta_ref, depth_ref, wet_ref, fric_ref, east_ref, west_ref, dde, rre, wwe, fe, fs, *refs
):
    east, south = refs[:6], refs[6:12]
    surf0, wet, surf1, fe1, ae1, pe1, qe1 = refs[12:19]
    sides = refs[19:]
    rows, cols = eta_ref.shape
    fields = (depth_ref, wet_ref, fric_ref, eta_ref)
    blocks = rows // 8
    for n, side in enumerate(sides):
        side[...] = side_block(east_ref[8 * n : 8 * n + 8], west_ref[8 * n : 8 * n + 8])

    def frame(i, c):
        at = rows_at(i)
        out = rows_at(i + 1)
        after = rows_at(jnp.minimum(i + 1, blocks - 1))
        corner = [side[at, :] for side in sides]
        tail = [ref[at, cols - 128 :].astype(F32) for ref in fields]
        head = [ref[at, 0:128].astype(F32) for ref in fields]
        here = [jnp.concatenate(p, axis=1) for p in zip(tail, corner)]
        there = [
            pltpu.roll(jnp.concatenate(p, axis=1), 3 * 128 - 1, 1)[:, :256]
            for p in zip(tail, corner, head)
        ]
        statics = statics_of(*here[:3], *there[:3])
        store_face(east, (out, slice(None)), statics, face(None, here[3], there[3], *statics))
        there = [south_of(v, side[after, :]) for v, side in zip(corner, sides)]
        statics = statics_of(*corner[:3], *there[:3])
        store_face(south, (out, slice(None)), statics, face(None, corner[3], there[3], *statics))
        for ref, n in ((wet, 1), (surf0, 3)):
            ref[out, 0:cols] = fields[n][at, :].astype(F32)
            ref[out, cols:] = corner[n]
        return c

    lax.fori_loop(0, blocks, frame, 0, unroll=4)
    cut = cols - 128

    def whole(left, right, at):
        width = left.shape[1] - right.shape[1]
        return jnp.concatenate([left[at, 0:width], right[at, :]], axis=1)

    def surface(i, before):
        at = rows_at(i)
        flux = whole(fs, south[3], at)
        div = divergence(whole(fe, east[3], at), flux, before)
        surf1[at, :] = wet[at, :] * (surf0[at, :] - (mass_gain * PUSH) * div)
        return flux

    lax.fori_loop(2, blocks, surface, whole(fs, south[3], rows_at(1)), unroll=6)

    def eastward(i, c):
        at = rows_at(i)
        s = surf1[at, :]
        statics = [whole(a, b, at) for a, b in ((dde, east[0]), (rre, east[1]), (wwe, east[2]))]
        made = face(whole(fe, east[3], at), s, pltpu.roll(s, s.shape[1] - 1, 1), *statics)
        for ref, value in zip((fe1, ae1, pe1, qe1), made):
            ref[at, :] = value
        return c

    lax.fori_loop(2, blocks, eastward, 0, unroll=6)


def solve_kernel(*refs):
    place_ref, grow_ref, gcol_ref = refs[:3]
    east0, south0, east_part, south_part = (refs[3 + 6 * n : 9 + 6 * n] for n in range(4))
    surf0, wet, surf1, fe1, ae1, pe1, qe1 = refs[27:34]
    north_ref, south_ref, top_ref, bottom_ref, count, obs, recv, block_ref = refs[34:42]
    final_ref, adj_ref, back_ref = refs[42:45]
    steps, rows, cols = obs.shape
    scratch = list(refs[45:])

    def take_scratch(n):
        taken = scratch[:n]
        del scratch[:n]
        return taken

    surf = [surf0, surf1] + take_scratch(steps - 1)
    ae = [None, ae1] + take_scratch(steps - 2)
    own_rows, own_cols = final_ref.shape
    dde, rre, wwe, fe0, pe0, qe0 = east0
    dds, rrs, wws, fs, ps0, qs0 = south0
    as_ = [None] + take_scratch(steps - 1)
    pe = [pe0, pe1] + take_scratch(steps - 2)
    qe = [qe0, qe1] + take_scratch(steps - 2)
    ps = [ps0] + take_scratch(steps - 1)
    qs = [qs0] + take_scratch(steps - 1)
    adj, ce, cs, spread, turned, west, xe, xs, grads, parts, reads = scratch
    sub = row_iota((8, cols))
    last = sub == 7
    firstrow = sub == 0
    blocks = rows // 8
    across = own_cols // 128

    def nxt(i):
        return pl.multiple_of(jnp.minimum(i * 8 + 8, rows - 8), 8)

    def take(i, c):
        at = rows_at(i)
        for whole, part in zip(east0 + south0, east_part + south_part):
            whole[at, cols - part.shape[1] :] = part[at, :]
        return c

    lax.fori_loop(1, blocks - 1, take, 0, unroll=2)

    def field(ref, n):
        return ref[8 * n : 8 * n + 8, :]

    def edge_face(refs, i, ref, neighbour):
        here = [field(ref, n) for n in range(4)]
        there = neighbour(here)
        statics = statics_of(*here[:3], *there[:3])
        store_face(refs, (rows_at(i), slice(None)), statics, face(None, here[3], there[3], *statics))

    def east_of(here):
        return [pltpu.roll(v, cols - 1, 1) for v in here]

    def above(ref):
        return lambda here: [south_of(v, field(ref, n)) for n, v in enumerate(here)]

    for i, ref in ((0, north_ref), (blocks - 1, south_ref)):
        surf0[rows_at(i), :] = field(ref, 3)
        wet[rows_at(i), :] = field(ref, 1)
        edge_face(east0, i, ref, east_of)
    edge_face(south0, 0, north_ref, above(top_ref))
    edge_face(south0, blocks - 2, bottom_ref, above(south_ref))
    edge_face(south0, blocks - 1, south_ref, above(south_ref))
    rim = (0, 1, blocks - 2, blocks - 1)
    for i in rim:
        at = rows_at(i)
        before = fs[rows_at(max(i - 1, 0)), :]
        div = divergence(fe0[at, :], fs[at, :], before)
        surf1[at, :] = wet[at, :] * (surf0[at, :] - (mass_gain * PUSH) * div)

    def pipelined(first, end, main, carry, begin, finish):
        groups = (end - first) // GROUP

        def step(g, carry):
            base = first + g * GROUP
            prior = jnp.maximum(base - GROUP, first)
            held = [begin(prior + u) for u in range(GROUP)]
            for u in range(GROUP):
                carry = main(base + u, carry)
            for u in range(GROUP):
                finish(prior + u, held[u])
            return carry

        carry = lax.fori_loop(0, groups, step, carry)
        done = first + groups * GROUP
        held = [begin(done - GROUP + u) for u in range(GROUP)]
        for i in range(done, end):
            carry = main(i, carry)
        for u in range(GROUP):
            finish(done - GROUP + u, held[u])
        held = [begin(i) for i in range(done, end)]
        for i in range(done, end):
            finish(i, held[i - done])
        return carry

    def rotate_into(src, dst, by):
        def begin(i):
            return pltpu.roll(src[rows_at(i), :], by, 1)

        def finish(i, value):
            dst[rows_at(i), :] = value

        return begin, finish

    def nothing(i, c):
        return c

    for k in range(1, steps):

        def eastward(i, c, k=k):
            here = rows_at(i)
            s = surf[k][here, :]
            s_east = pltpu.roll(s, cols - 1, 1) if k == 1 else turned[here, :]
            old = fe0 if k == 1 else fe1
            flux, a, p, q = face(old[here, :], s, s_east, dde[here, :], rre[here, :], wwe[here, :])
            fe1[here, :] = flux
            ae[k][here, :] = a
            pe[k][here, :] = p
            qe[k][here, :] = q
            return c

        def southward(i, carry, k=k):
            s, s_up, f_down = carry
            here = rows_at(i)
            sn = surf[k][pl.ds(nxt(i), 8), :]
            sn_up = pltpu.roll(sn, 7, 0)
            flux, a, p, q = face(
                fs[here, :], s, jnp.where(last, sn_up, s_up), dds[here, :], rrs[here, :], wws[here, :]
            )
            fs[here, :] = flux
            as_[k][here, :] = a
            ps[k][here, :] = p
            qs[k][here, :] = q
            down = pltpu.roll(flux, 1, 0)
            div = fe1[here, :] - west[here, :]
            div = div + (flux - jnp.where(firstrow, f_down, down))
            surf[k + 1][here, :] = wet[here, :] * (s - (mass_gain * PUSH) * div)
            return sn, sn_up, down

        turn_flux = rotate_into(fe1, west, 1)
        if k == 1:
            for i in rim:
                eastward(i, 0)
            pipelined(0, blocks, nothing, 0, *turn_flux)
        else:
            pipelined(0, blocks, eastward, 0, *turn_flux)
        s0 = surf[k][0:8, :]
        start = (s0, pltpu.roll(s0, 7, 0), jnp.zeros((8, cols), F32))
        if k < steps - 1:
            pipelined(0, blocks, southward, start, *rotate_into(surf[k + 1], turned, cols - 1))
        else:
            lax.fori_loop(0, blocks, southward, start, unroll=GROUP)

    final_ref[...] = surf[steps][HALO : HALO + own_rows, 0:own_cols]

    gx, gy = place_ref[0], place_ref[1]
    lane8 = lax.broadcasted_iota(I32, (8, 128), 1)
    sub8 = row_iota((8, 128))
    per = grow_ref.shape[0] // (place_ref[2] * place_ref[3])
    per_tile = reads.shape[0] // steps
    first = (gx * place_ref[3] + gy) * per
    for g0 in range(0, per_tile, 8):
        spots = []
        for g in range(g0, g0 + 8):
            r = jnp.clip(grow_ref[first + g] - gx * own_rows, 0, own_rows - 1) + HALO
            q = jnp.clip(gcol_ref[first + g] - gy * own_cols, 0, own_cols - 1)
            at = (
                pl.ds(pl.multiple_of(r // 8 * 8, 8), 8),
                pl.ds(pl.multiple_of(q // 128 * 128, 128), 128),
            )
            spots.append((at, (sub8 == r % 8) & (lane8 == q % 128)))
        for k in range(steps):
            picked = [jnp.where(hit, surf[k + 1][at], 0.0) for at, hit in spots]
            reads[k * per_tile + g0 : k * per_tile + g0 + 8, :] = merge_rows(picked)
    values = jnp.sum(reads[...], axis=1, keepdims=True)
    spots = row_iota(reads.shape) + SLOTS == lax.broadcasted_iota(I32, reads.shape, 1)
    reading_row = jnp.sum(jnp.where(spots, values, 0.0), axis=0, keepdims=True)

    def seed(at, k):
        return count[at, :] * surf[k + 1][at, :] - obs[k, at, :]

    def begin_adjoint(i, c):
        at = rows_at(i)
        spread[at, :] = wet[at, :] * seed(at, steps - 1)
        return c

    turn_spread = rotate_into(spread, turned, cols - 1)
    turn_x = rotate_into(xe, west, 1)
    pipelined(0, blocks, begin_adjoint, 0, *turn_spread)
    for k in reversed(range(steps)):

        def gather(i, c, k=k):
            at = rows_at(i)
            b = spread[at, :]
            ge = (mass_gain * PUSH) * (turned[at, :] - b)
            gs = (mass_gain * PUSH) * (south_of(b, spread[pl.ds(nxt(i), 8), :]) - b)
            if k < steps - 1:
                ge = ge + ce[at, :]
                gs = gs + cs[at, :]
            if k > 0:
                ce[at, :] = ge * ae[k][at, :]
                cs[at, :] = gs * as_[k][at, :]
            xe[at, :] = ge * pe[k][at, :]
            xs[at, :] = gs * ps[k][at, :]
            adj[at, :] = (b + ge * qe[k][at, :]) + gs * qs[k][at, :]
            return c

        def collect(i, c, k=k):
            at = rows_at(i)
            before = xs[pl.ds(pl.multiple_of(jnp.maximum(i * 8 - 8, 0), 8), 8), :]
            out = (adj[at, :] + west[at, :]) + north_of(xs[at, :], before)
            if k > 0:
                spread[at, :] = wet[at, :] * (out + seed(at, k - 1))
            else:
                out = out[:, 0:own_cols]
                adj_ref[rows_at(i - HALO // 8), :] = out
                scaled = out * wet[at, 0:own_cols]
                for q in range(across):
                    grads[(i - HALO // 8) * across + q] = scaled[:, q * 128 : q * 128 + 128]
            return c

        pipelined(0, blocks, gather, 0, *turn_x)
        if k > 0:
            pipelined(0, blocks, collect, 0, *turn_spread)
        else:
            lax.fori_loop(HALO // 8, blocks - HALO // 8, collect, 0, unroll=GROUP)

    tiles = recv.shape[0] // CHUNK

    def sens(i, c):
        for j in range(SLOTS):
            products = []
            for u in range(8):
                t = i * 8 + u
                b = block_ref[j, t]
                products.append(grads[b] * recv[pl.ds(t * CHUNK + 8 * j, 8), :])
            parts[j, pl.ds(pl.multiple_of(i * 8, 8), 8), :] = merge_rows(products)
        return c

    lax.fori_loop(0, tiles // 8, sens, 0)
    lanes = lax.broadcasted_iota(I32, (tiles, 128), 1)
    out = jnp.broadcast_to(reading_row, (tiles, 128))
    for j in range(SLOTS):
        out = jnp.where(lanes == j, jnp.sum(parts[j], axis=1, keepdims=True), out)
    back_ref[...] = out


def closing_kernel(back_ref, table_ref, slip_ref, readings_ref, grad_ref):
    tiles = back_ref.shape[0]
    steps, gauges = readings_ref.shape
    faults = grad_ref.shape[0]
    per = gauges // tiles
    width = 128 // per
    lane = lax.broadcasted_iota(I32, (8, 128), 1)
    sub = row_iota((8, 128))

    turned = [
        pltpu.roll(back_ref[8 * c : 8 * c + 8, :], 0, 1, stride=per, stride_axis=0)
        for c in range(tiles // width)
    ]
    for k in range(steps):
        keep = (lane + 128 - SLOTS) % 128 // per == (sub + k) % width
        for c0 in range(0, tiles // width, 8):
            rows = merge_rows([jnp.where(keep, v, 0.0) for v in turned[c0 : c0 + 8]])
            rows = pltpu.roll(rows, 128 - SLOTS - per * k, 1)
            for c in range(8):
                at = slice((c0 + c) * 128, (c0 + c + 1) * 128)
                readings_ref[k : k + 1, at] = rows[c : c + 1, :]

    totals = [jnp.zeros((8, 128), F32)] * faults
    for c in range(tiles // 8):
        fault = pltpu.roll(table_ref[8 * c : 8 * c + 8, :], 128 - 8, 1)
        value = jnp.where(lane < SLOTS, back_ref[8 * c : 8 * c + 8, :], 0.0)
        totals = [
            t + jnp.where(fault == s + 1.0, value, 0.0) for s, t in enumerate(totals)
        ]
    total = jnp.concatenate([merge_rows(totals[i : i + 8]) for i in range(0, faults, 8)], axis=0)
    total = jnp.sum(total, axis=1, keepdims=True)
    mine = row_iota((faults, 128)) == lax.broadcasted_iota(I32, (faults, 128), 1)
    grad = jnp.sum(jnp.where(mine, total, 0.0), axis=0)
    grad_ref[...] = grad[0:faults] / slip_ref[...]


def body(
    ocean_depth,
    wet_mask,
    manning,
    fault_slip,
    pattern,
    foot_tile,
    foot_block,
    gauge_row,
    gauge_col,
    observed,
):
    rows_here, cols_here = ocean_depth.shape
    steps, gauges = observed.shape
    width_x = lax.axis_size("gx")
    width_y = lax.axis_size("gy")
    devices = width_x * width_y
    entries = pattern.shape[0]
    faults = fault_slip.shape[0]
    per_fault = entries // faults
    per_tile = gauges // devices
    both = ("gx", "gy")
    rows, cols = rows_here + 2 * HALO, cols_here + 128
    f = jax.ShapeDtypeStruct

    packed, table = pl.pallas_call(
        pack_kernel,
        out_shape=[f((devices * CHUNK, 128), F32), f((devices, 128), F32)],
        in_specs=[smem(), vmem(), vmem(), hbm()],
        out_specs=[vmem()] * 2,
        scratch_shapes=[
            pltpu.VMEM(pattern.shape, F32),
            pltpu.VMEM((1, entries), I32),
            pltpu.SMEM((1, entries), I32),
            pltpu.SemaphoreType.DMA((2,)),
        ],
        name="pack",
    )(fault_slip, foot_tile.reshape(1, entries), foot_block.reshape(1, entries), pattern)
    recv_flat = lax.all_to_all(packed.reshape(-1), both, split_axis=0, concat_axis=0, tiled=True)
    recv = recv_flat.reshape(devices * CHUNK, 128)

    edge = [f((24, rows_here), F32)] * 2 + [f((24, cols_here), F32)] * 2
    edges = pl.pallas_call(
        static_edge_kernel,
        out_shape=edge,
        in_specs=[vmem()] * 3,
        out_specs=[vmem()] * 4,
        name="static_edges",
        compiler_params=pltpu.CompilerParams(vmem_limit_bytes=4 * MIB),
    )(ocean_depth, wet_mask, manning)
    grid = f((rows, cols), F32)
    place = jnp.stack(
        [lax.axis_index("gx"), lax.axis_index("gy"), jnp.int32(width_x), jnp.int32(width_y)]
    ).astype(I32)
    count, obs, token = pl.pallas_call(
        gauge_kernel,
        out_shape=[grid, f((steps, rows, cols), F32), f((8, 128), F32)],
        in_specs=[smem()] * 4,
        out_specs=[vmem()] * 3,
        name="gauges",
        compiler_params=pltpu.CompilerParams(vmem_limit_bytes=2 * MIB),
    )(place, gauge_row, gauge_col, observed)

    eta, west, east, top, bottom, block_of = pl.pallas_call(
        scatter_kernel,
        out_shape=[f((rows_here, cols_here), F32)]
        + [f((32, rows_here), F32)] * 2
        + [f((32, cols_here), F32)] * 2
        + [f((8, devices), I32)],
        in_specs=[vmem()] * 6 + [hbm()],
        out_specs=[vmem()] * 6,
        scratch_shapes=[pltpu.SMEM((8, devices), I32), pltpu.SemaphoreType.DMA]
        + [pltpu.VMEM((rows_here * cols_here // 1024, 8, 128), F32)] * SLOTS,
        name="scatter",
        compiler_params=pltpu.CompilerParams(vmem_limit_bytes=10 * MIB),
    )(recv, wet_mask, *edges, token)
    from_east = shifted(west, "gy", -1)
    from_west = shifted(east, "gy", 1)
    tiles = (eta, ocean_depth, wet_mask, manning)
    made = pl.pallas_call(
        tile_kernel,
        out_shape=[grid] * 12,
        in_specs=[vmem()] * 4,
        out_specs=[vmem()] * 12,
        compiler_params=pltpu.CompilerParams(vmem_limit_bytes=MIB),
        name="tile",
    )(*tiles)
    top, bottom = pl.pallas_call(
        rim_kernel,
        out_shape=[f((32, cols), F32)] * 2,
        in_specs=[vmem()] * 4 + [hbm()],
        out_specs=[vmem()] * 2,
        compiler_params=pltpu.CompilerParams(vmem_limit_bytes=MIB),
        name="rims",
    )(from_east, from_west, top, bottom, made[0])
    from_south = shifted(top, "gx", -1)
    from_north = shifted(bottom, "gx", 1)
    framed = pl.pallas_call(
        frame_kernel,
        out_shape=[f((rows, 256), F32)] * 6 + [f((rows, 128), F32)] * 6 + [grid] * 7,
        in_specs=[vmem()] * 11,
        out_specs=[vmem()] * 19,
        scratch_shapes=[pltpu.VMEM((rows_here, 128), F32)] * 4,
        compiler_params=pltpu.CompilerParams(vmem_limit_bytes=2 * MIB),
        name="frame",
    )(*tiles, from_east, from_west, *made[:4], made[9])

    tile = f((rows_here, cols_here), F32)

    final, adjoint, back = pl.pallas_call(
        solve_kernel,
        out_shape=[tile, tile, f((devices, 128), F32)],
        in_specs=[smem()] * 3 + [vmem()] * 38 + [smem()],
        out_specs=[vmem()] * 3,
        scratch_shapes=[pltpu.VMEM((rows, cols), F32)] * (4 * (steps - 1) + 3 * (steps - 2) + 8)
        + [
            pltpu.VMEM((rows_here // 8 * (cols_here // 128), 8, 128), F32),
            pltpu.VMEM((SLOTS, devices, 128), F32),
            pltpu.VMEM((steps * per_tile, 128), F32),
        ],
        compiler_params=pltpu.CompilerParams(vmem_limit_bytes=26 * MIB),
        name="solve",
    )(
        place, gauge_row, gauge_col, *made, *framed,
        from_north, from_south, top, bottom, count, obs, recv, block_of,
    )
    returned = lax.all_to_all(back, both, split_axis=0, concat_axis=0, tiled=True)
    readings, grad_slip = pl.pallas_call(
        closing_kernel,
        out_shape=[f((steps, gauges), F32), f((faults,), F32)],
        in_specs=[vmem()] * 3,
        out_specs=[vmem()] * 2,
        compiler_params=pltpu.CompilerParams(vmem_limit_bytes=MIB),
        name="closing",
    )(returned, table, fault_slip)
    return (final, readings, adjoint, grad_slip)


def solution(mesh):
    placed = (
        P("gx", "gy"),
        P("gx", "gy"),
        P("gx", "gy"),
        P(("gx", "gy")),
        P(("gx", "gy"), None, None),
        P(("gx", "gy"), None),
        P(("gx", "gy")),
        P(),
        P(),
        P(),
    )
    return jax.shard_map(
        body,
        mesh=mesh,
        in_specs=placed,
        out_specs=(P("gx", "gy"), P(), P("gx", "gy"), P(("gx", "gy"))),
        check_vma=False,
    )
```

```python
import math

import jax
import jax.numpy as jnp
from jax import lax
from jax.experimental import pallas as pl
from jax.experimental.pallas import tpu as pltpu
from jax.sharding import PartitionSpec as P

wave_gain = 0.2
mass_gain = 0.2
min_depth = 0.25
speed_floor = 0.01

HALO = 8
CHUNK = 33
SLOTS = 4
LN2 = math.log(2.0)
PUSH = -0.5 * wave_gain
assert abs(PUSH * PUSH - speed_floor) < 1e-12
ROUGH_SCALE = 0.5 * abs(PUSH) * 2.0 ** (7.0 / 3.0)
F32 = jnp.float32
MIB = 1 << 20
GROUP = 8
I32 = jnp.int32


def vmem():
    return pl.BlockSpec(memory_space=pltpu.VMEM)


def smem():
    return pl.BlockSpec(memory_space=pltpu.SMEM)


def hbm():
    return pl.BlockSpec(memory_space=pl.ANY)


def swapped(shard, axis, first):
    devices = lax.axis_size(axis)
    pairs = [(i, i + 1) for i in range(first, devices - 1, 2)]
    return lax.ppermute(shard, axis, pairs + [(j, i) for i, j in pairs])


def by_parity(index, even, odd):
    return jnp.where(index % 2 == 0, even, odd)


def pack_kernel(
    slip_ref, tile_ref, block_ref, pattern_hbm, out_ref, table_ref, pattern, row_v, row_s, sems
):
    load = pltpu.make_async_copy(pattern_hbm, pattern, sems.at[0])
    load.start()
    rows = out_ref.shape[0]
    tiles = rows // CHUNK
    entries = tile_ref.shape[1]
    faults = slip_ref.shape[0]
    per_fault = entries // faults
    tile_row = tile_ref[...]
    tile_f = tile_row.astype(F32)
    tile_col = jnp.broadcast_to(tile_f, (128, entries)).T
    here = lax.broadcasted_iota(I32, (entries, 128), 0)
    ranks = []
    for q in range(entries // 128):
        there = lax.broadcasted_iota(I32, (entries, 128), 1) + q * 128
        same = (tile_col == tile_f[:, q * 128 : q * 128 + 128]) & (here < there)
        ranks.append(jnp.sum(jnp.where(same, 1.0, 0.0), axis=0, keepdims=True))
    rank = jnp.concatenate(ranks, axis=1).astype(I32)
    row_v[...] = tile_row * CHUNK + rank * 8
    place_rows = pltpu.make_async_copy(row_v, row_s, sems.at[1])
    place_rows.start()
    fault = lax.broadcasted_iota(I32, (1, entries), 1) // per_fault
    slot = lax.broadcasted_iota(I32, (128, entries), 0)
    facts = jnp.where(slot == rank, block_ref[...], 0) + jnp.where(slot == rank + 8, fault + 1, 0)
    hot = jnp.where(lax.broadcasted_iota(I32, (tiles, entries), 0) == tile_row, 1.0, 0.0)
    table_ref[...] = lax.dot_general(
        hot.astype(jnp.bfloat16),
        facts.astype(F32).astype(jnp.bfloat16),
        (((1,), (1,)), ((), ())),
        preferred_element_type=F32,
    )
    zero = jnp.zeros((8, 128), F32)

    def clear(i, c):
        out_ref[pl.ds(pl.multiple_of(i * 8, 8), 8), :] = zero
        return c

    lax.fori_loop(0, rows // 8, clear, 0, unroll=16)
    for t in range(tiles):
        out_ref[t * CHUNK + 32 : t * CHUNK + 33, :] = table_ref[t : t + 1, :]
    place_rows.wait()
    load.wait()

    def place(s, c):
        slip = slip_ref[s]
        for j in range(per_fault):
            i = s * per_fault + j
            out_ref[pl.ds(row_s[0, i], 8), :] = pattern[i] * slip
        return c

    lax.fori_loop(0, faults, place, 0)


def edges_of(first, last):
    lane = lax.broadcasted_iota(I32, first.shape, 1)
    both = jnp.where(lane < 64, first, last).T
    return both[0:8], both[120:128]


def side_block(east, west):
    rows = east.shape[1]
    gap = jnp.zeros((128 - 16, rows), F32)
    return jnp.concatenate([east, gap, west], axis=0).T


def scatter_kernel(
    place_ref, recv_ref, wet_ref, west_in, east_in, top_in, bottom_in, after,
    eta_ref, one_ref, two_ref, top_ref, bottom_ref, block_out, block_s, sem, *acc,
):
    del after
    gy = place_ref[1]
    tiles = recv_ref.shape[0] // CHUNK
    facts = recv_ref[pl.ds(8 * SLOTS, tiles, stride=CHUNK), :]
    block_out[...] = facts.T[0:8].astype(I32)
    load = pltpu.make_async_copy(block_out, block_s, sem)
    load.start()
    rows, cols = eta_ref.shape
    across = cols // 128
    zero = jnp.zeros((8, 128), F32)

    def clear(i, c):
        for a in acc:
            a[i] = zero
        return c

    lax.fori_loop(0, acc[0].shape[0], clear, 0, unroll=8)
    one_ref[0:24, :] = by_parity(gy, east_in[...], west_in[...])
    two_ref[0:24, :] = by_parity(gy, west_in[...], east_in[...])
    top_ref[0:24, :] = top_in[...]
    bottom_ref[0:24, :] = bottom_in[...]
    load.wait()

    def add(i, c):
        base = pl.multiple_of(i * (8 * CHUNK), 8)
        for u in range(8):
            for j in range(SLOTS):
                b = block_s[j, i * 8 + u]
                acc[j][b] = acc[j][b] + recv_ref[pl.ds(base + (u * CHUNK + 8 * j), 8), :]
        return c

    lax.fori_loop(0, tiles // 8, add, 0)

    def merge(i, c):
        r = pl.multiple_of(i * 8, 8)
        for q in range(across):
            b = i * across + q
            total = (acc[0][b] + acc[1][b]) + (acc[2][b] + acc[3][b])
            wet = wet_ref[pl.ds(r, 8), q * 128 : q * 128 + 128].astype(F32)
            eta_ref[pl.ds(r, 8), q * 128 : q * 128 + 128] = total * wet
        return c

    lax.fori_loop(0, rows // 8, merge, 0, unroll=2)
    west, east = edges_of(eta_ref[:, 0:128], eta_ref[:, cols - 128 : cols])
    one_ref[24:32] = by_parity(gy, east, west)
    two_ref[24:32] = by_parity(gy, west, east)
    top_ref[24:32] = eta_ref[0:8, :]
    bottom_ref[24:32] = eta_ref[rows - 8 : rows, :]


def static_edge_kernel(
    depth_ref, wet_ref, fric_ref, west_ref, east_ref, top_ref, bottom_ref
):
    rows, cols = depth_ref.shape
    for n, ref in enumerate((depth_ref, wet_ref, fric_ref)):
        at = slice(8 * n, 8 * n + 8)
        west, east = edges_of(ref[:, 0:128].astype(F32), ref[:, cols - 128 : cols].astype(F32))
        west_ref[at] = west
        east_ref[at] = east
        top_ref[at] = ref[0:8, :].astype(F32)
        bottom_ref[at] = ref[rows - 8 : rows, :].astype(F32)


def rim_kernel(
    place_ref, one_in, two_in, top_in, bottom_in, after, top_ref, bottom_ref, one_ref, two_ref
):
    del after
    fields = one_in.shape[0] // 8
    rows = one_in.shape[1]
    cols = top_in.shape[1]
    gx, gy = place_ref[0], place_ref[1]
    east_ref = by_parity(gy, one_in[...], two_in[...])
    west_ref = by_parity(gy, two_in[...], one_in[...])
    lane = lax.broadcasted_iota(I32, (8, 128), 1)
    for src, out, first, keep in (
        (top_in, top_ref, 0, slice(0, 8)),
        (bottom_in, bottom_ref, rows - 128, slice(120, 128)),
    ):
        pieces = []
        for n in range(fields):
            at = slice(8 * n, 8 * n + 8)
            pieces += [west_ref[at, first : first + 128], east_ref[at, first : first + 128]]
        pieces.append(jnp.zeros((128 - 16 * fields, 128), F32))
        corners = jnp.concatenate(pieces, axis=0).T[keep]
        for n in range(fields):
            at = slice(8 * n, 8 * n + 8)
            out[at, 0:cols] = src[at, :]
            out[at, cols:] = jnp.where(
                (lane < 8) | (lane >= 120), pltpu.roll(corners, 128 - 16 * n - 8, 1), 0.0
            )
    one_ref[...] = by_parity(gx, bottom_ref[...], top_ref[...])
    two_ref[...] = by_parity(gx, top_ref[...], bottom_ref[...])


def row_iota(shape):
    return lax.broadcasted_iota(I32, shape, 0)


def gauge_kernel(place_ref, row_ref, col_ref, obs_ref, count_out, obs_out, token_out):
    token_out[...] = jnp.zeros(token_out.shape, F32)
    steps, rows, cols = obs_out.shape
    own_rows = rows - 2 * HALO
    own_cols = cols - 128
    gx, gy, wx, wy = place_ref[0], place_ref[1], place_ref[2], place_ref[3]
    per = row_ref.shape[0] // (wx * wy)
    zero = jnp.zeros((8, cols), F32)

    def clear(i, c):
        r = pl.multiple_of(i * 8, 8)
        count_out[pl.ds(r, 8), :] = zero
        for k in range(steps):
            obs_out[k, pl.ds(r, 8), :] = zero
        return c

    lax.fori_loop(0, rows // 8, clear, 0)
    sub = row_iota((8, 128))
    lane = lax.broadcasted_iota(I32, (8, 128), 1)

    for dx in (-1, 0, 1):
        for dy in (-1, 0, 1):
            tx = gx + dx
            ty = gy + dy
            inside = (tx >= 0) & (tx < wx) & (ty >= 0) & (ty < wy)
            first = jnp.where(inside, (tx * wy + ty) * per, 0)

            def one(g, c, first=first, inside=inside):
                r = row_ref[first + g] - gx * own_rows + HALO
                q = col_ref[first + g] - gy * own_cols
                ok = inside & (r >= 0) & (r < rows) & (q >= -HALO) & (q < own_cols + HALO)
                q = jnp.where(q < 0, q + cols, q)

                @pl.when(ok)
                def _():
                    rb = pl.multiple_of(r // 8 * 8, 8)
                    cb = pl.multiple_of(q // 128 * 128, 128)
                    hit = (sub == r % 8) & (lane == q % 128)
                    at = (pl.ds(rb, 8), pl.ds(cb, 128))
                    count_out[at] = count_out[at] + jnp.where(hit, 1.0, 0.0)
                    for k in range(steps):
                        at_k = (k,) + at
                        obs_out[at_k] = obs_out[at_k] + jnp.where(hit, obs_ref[k, first + g], 0.0)

                return c

            lax.fori_loop(0, per, one, 0)


def face(f, s, sn, dd, rr, ww):
    x = dd + (s + sn)
    total = jnp.maximum(x, 2.0 * min_depth)
    diff = sn - s
    push = total * diff
    if f is not None:
        push = push + f
    t = push * push + 1.0
    y = (rr * jnp.exp2(jnp.log(total) * (-7.0 / 3.0 / LN2))) * lax.rsqrt(t)
    inv = 1.0 / (t * y + 1.0)
    wi = ww * inv
    flux = wi * push
    a = (wi * inv) * (y + 1.0)
    depth_part = (flux - flux * inv) * ((7.0 / 3.0) / total)
    share = jnp.where(
        x > 2.0 * min_depth, 1.0, jnp.where(x == 2.0 * min_depth, 0.5, 0.0)
    )
    u = share * (depth_part + a * diff)
    v = a * total
    return flux, a, u + v, u - v


def merge_rows(tiles):
    sub = row_iota((8, 128))
    for width in (1, 2, 4):
        low = (sub & width) == 0
        tiles = [
            jnp.where(low, p, q) + pltpu.roll(jnp.where(low, q, p), width, 0)
            for p, q in zip(tiles[0::2], tiles[1::2])
        ]
    return tiles[0]


def statics_of(d, w, m, d_next, w_next, m_next):
    return d + d_next, ROUGH_SCALE * (m + m_next), w * w_next


def south_of(here, after):
    last = row_iota(here.shape) == 7
    return jnp.where(last, pltpu.roll(after, 7, 0), pltpu.roll(here, 7, 0))


def north_of(flux, before):
    first = row_iota(flux.shape) == 0
    return jnp.where(first, pltpu.roll(before, 1, 0), pltpu.roll(flux, 1, 0))


def rows_at(i):
    return pl.ds(pl.multiple_of(i * 8, 8), 8)


def divergence(east, south, before):
    return (east - pltpu.roll(east, 1, 1)) + (south - north_of(south, before))


def store_face(refs, at, statics, made):
    flux, _, p, q = made
    for ref, value in zip(refs, (*statics, flux, p, q)):
        ref[at] = value


def tile_kernel(eta_ref, depth_ref, wet_ref, fric_ref, *out):
    east, south = out[:6], out[6:]
    rows, cols = eta_ref.shape
    fields = (depth_ref, wet_ref, fric_ref, eta_ref)
    keep = cols - 128

    def eastward(i, c):
        here = [ref[rows_at(i), :].astype(F32) for ref in fields]
        there = [pltpu.roll(v, cols - 1, 1)[:, :keep] for v in here]
        here = [v[:, :keep] for v in here]
        statics = statics_of(*here[:3], *there[:3])
        store_face(east, (rows_at(i + 1), slice(0, keep)), statics, face(None, here[3], there[3], *statics))
        return c

    def southward(i, c):
        here = [ref[rows_at(i), :].astype(F32) for ref in fields]
        there = [south_of(v, ref[rows_at(i + 1), :].astype(F32)) for v, ref in zip(here, fields)]
        statics = statics_of(*here[:3], *there[:3])
        store_face(south, (rows_at(i + 1), slice(0, cols)), statics, face(None, here[3], there[3], *statics))
        return c

    lax.fori_loop(0, rows // 8, eastward, 0, unroll=4)
    lax.fori_loop(0, rows // 8 - 1, southward, 0, unroll=3)


def frame_kernel(
    place_ref, eta_ref, depth_ref, wet_ref, fric_ref, one_in, two_in, dde, rre, wwe, fe, fs, *refs
):
    east, south = refs[:6], refs[6:12]
    surf0, wet, surf1, fe1, ae1, pe1, qe1 = refs[12:19]
    sides = refs[19:]
    rows, cols = eta_ref.shape
    fields = (depth_ref, wet_ref, fric_ref, eta_ref)
    blocks = rows // 8
    gy = place_ref[1]
    for n, side in enumerate(sides):
        one, two = one_in[8 * n : 8 * n + 8], two_in[8 * n : 8 * n + 8]
        side[...] = side_block(by_parity(gy, one, two), by_parity(gy, two, one))

    def frame(i, c):
        at = rows_at(i)
        out = rows_at(i + 1)
        after = rows_at(jnp.minimum(i + 1, blocks - 1))
        corner = [side[at, :] for side in sides]
        tail = [ref[at, cols - 128 :].astype(F32) for ref in fields]
        head = [ref[at, 0:128].astype(F32) for ref in fields]
        here = [jnp.concatenate(p, axis=1) for p in zip(tail, corner)]
        there = [
            pltpu.roll(jnp.concatenate(p, axis=1), 3 * 128 - 1, 1)[:, :256]
            for p in zip(tail, corner, head)
        ]
        statics = statics_of(*here[:3], *there[:3])
        store_face(east, (out, slice(None)), statics, face(None, here[3], there[3], *statics))
        there = [south_of(v, side[after, :]) for v, side in zip(corner, sides)]
        statics = statics_of(*corner[:3], *there[:3])
        store_face(south, (out, slice(None)), statics, face(None, corner[3], there[3], *statics))
        for ref, n in ((wet, 1), (surf0, 3)):
            ref[out, 0:cols] = fields[n][at, :].astype(F32)
            ref[out, cols:] = corner[n]
        return c

    lax.fori_loop(0, blocks, frame, 0, unroll=4)
    cut = cols - 128

    def whole(left, right, at):
        width = left.shape[1] - right.shape[1]
        return jnp.concatenate([left[at, 0:width], right[at, :]], axis=1)

    def surface(i, before):
        at = rows_at(i)
        flux = whole(fs, south[3], at)
        div = divergence(whole(fe, east[3], at), flux, before)
        surf1[at, :] = wet[at, :] * (surf0[at, :] - (mass_gain * PUSH) * div)
        return flux

    lax.fori_loop(2, blocks, surface, whole(fs, south[3], rows_at(1)), unroll=6)

    def eastward(i, c):
        at = rows_at(i)
        s = surf1[at, :]
        statics = [whole(a, b, at) for a, b in ((dde, east[0]), (rre, east[1]), (wwe, east[2]))]
        made = face(whole(fe, east[3], at), s, pltpu.roll(s, s.shape[1] - 1, 1), *statics)
        for ref, value in zip((fe1, ae1, pe1, qe1), made):
            ref[at, :] = value
        return c

    lax.fori_loop(2, blocks, eastward, 0, unroll=6)


def solve_kernel(*refs):
    place_ref, grow_ref, gcol_ref = refs[:3]
    east0, south0, east_part, south_part = (refs[3 + 6 * n : 9 + 6 * n] for n in range(4))
    surf0, wet, surf1, fe1, ae1, pe1, qe1 = refs[27:34]
    one_in, two_in, top_ref, bottom_ref, count, obs, recv, block_ref = refs[34:42]
    final_ref, adj_ref, back_ref = refs[42:45]
    steps, rows, cols = obs.shape
    scratch = list(refs[45:])

    def take_scratch(n):
        taken = scratch[:n]
        del scratch[:n]
        return taken

    surf = [surf0, surf1] + take_scratch(steps - 1)
    ae = [None, ae1] + take_scratch(steps - 2)
    own_rows, own_cols = final_ref.shape
    dde, rre, wwe, fe0, pe0, qe0 = east0
    dds, rrs, wws, fs, ps0, qs0 = south0
    as_ = [None] + take_scratch(steps - 1)
    pe = [pe0, pe1] + take_scratch(steps - 2)
    qe = [qe0, qe1] + take_scratch(steps - 2)
    ps = [ps0] + take_scratch(steps - 1)
    qs = [qs0] + take_scratch(steps - 1)
    adj, ce, cs, spread, turned, west, xe, xs, grads, parts, reads, north_ref, south_ref = scratch
    south_ref[...] = by_parity(place_ref[0], one_in[...], two_in[...])
    north_ref[...] = by_parity(place_ref[0], two_in[...], one_in[...])
    sub = row_iota((8, cols))
    last = sub == 7
    firstrow = sub == 0
    blocks = rows // 8
    across = own_cols // 128

    def nxt(i):
        return pl.multiple_of(jnp.minimum(i * 8 + 8, rows - 8), 8)

    def take(i, c):
        at = rows_at(i)
        for whole, part in zip(east0 + south0, east_part + south_part):
            whole[at, cols - part.shape[1] :] = part[at, :]
        return c

    lax.fori_loop(1, blocks - 1, take, 0, unroll=2)

    def field(ref, n):
        return ref[8 * n : 8 * n + 8, :]

    def edge_face(refs, i, ref, neighbour):
        here = [field(ref, n) for n in range(4)]
        there = neighbour(here)
        statics = statics_of(*here[:3], *there[:3])
        store_face(refs, (rows_at(i), slice(None)), statics, face(None, here[3], there[3], *statics))

    def east_of(here):
        return [pltpu.roll(v, cols - 1, 1) for v in here]

    def above(ref):
        return lambda here: [south_of(v, field(ref, n)) for n, v in enumerate(here)]

    for i, ref in ((0, north_ref), (blocks - 1, south_ref)):
        surf0[rows_at(i), :] = field(ref, 3)
        wet[rows_at(i), :] = field(ref, 1)
        edge_face(east0, i, ref, east_of)
    edge_face(south0, 0, north_ref, above(top_ref))
    edge_face(south0, blocks - 2, bottom_ref, above(south_ref))
    edge_face(south0, blocks - 1, south_ref, above(south_ref))
    rim = (0, 1, blocks - 2, blocks - 1)
    for i in rim:
        at = rows_at(i)
        before = fs[rows_at(max(i - 1, 0)), :]
        div = divergence(fe0[at, :], fs[at, :], before)
        surf1[at, :] = wet[at, :] * (surf0[at, :] - (mass_gain * PUSH) * div)

    def pipelined(first, end, main, carry, begin, finish):
        groups = (end - first) // GROUP

        def step(g, carry):
            base = first + g * GROUP
            prior = jnp.maximum(base - GROUP, first)
            held = [begin(prior + u) for u in range(GROUP)]
            for u in range(GROUP):
                carry = main(base + u, carry)
            for u in range(GROUP):
                finish(prior + u, held[u])
            return carry

        carry = lax.fori_loop(0, groups, step, carry)
        done = first + groups * GROUP
        held = [begin(done - GROUP + u) for u in range(GROUP)]
        for i in range(done, end):
            carry = main(i, carry)
        for u in range(GROUP):
            finish(done - GROUP + u, held[u])
        held = [begin(i) for i in range(done, end)]
        for i in range(done, end):
            finish(i, held[i - done])
        return carry

    def rotate_into(src, dst, by):
        def begin(i):
            return pltpu.roll(src[rows_at(i), :], by, 1)

        def finish(i, value):
            dst[rows_at(i), :] = value

        return begin, finish

    def nothing(i, c):
        return c

    for k in range(1, steps):

        def eastward(i, c, k=k):
            here = rows_at(i)
            s = surf[k][here, :]
            s_east = pltpu.roll(s, cols - 1, 1) if k == 1 else turned[here, :]
            old = fe0 if k == 1 else fe1
            flux, a, p, q = face(old[here, :], s, s_east, dde[here, :], rre[here, :], wwe[here, :])
            fe1[here, :] = flux
            ae[k][here, :] = a
            pe[k][here, :] = p
            qe[k][here, :] = q
            return c

        def southward(i, carry, k=k):
            s, s_up, f_down = carry
            here = rows_at(i)
            sn = surf[k][pl.ds(nxt(i), 8), :]
            sn_up = pltpu.roll(sn, 7, 0)
            flux, a, p, q = face(
                fs[here, :], s, jnp.where(last, sn_up, s_up), dds[here, :], rrs[here, :], wws[here, :]
            )
            fs[here, :] = flux
            as_[k][here, :] = a
            ps[k][here, :] = p
            qs[k][here, :] = q
            down = pltpu.roll(flux, 1, 0)
            div = fe1[here, :] - west[here, :]
            div = div + (flux - jnp.where(firstrow, f_down, down))
            surf[k + 1][here, :] = wet[here, :] * (s - (mass_gain * PUSH) * div)
            return sn, sn_up, down

        turn_flux = rotate_into(fe1, west, 1)
        if k == 1:
            for i in rim:
                eastward(i, 0)
            pipelined(0, blocks, nothing, 0, *turn_flux)
        else:
            pipelined(0, blocks, eastward, 0, *turn_flux)
        s0 = surf[k][0:8, :]
        start = (s0, pltpu.roll(s0, 7, 0), jnp.zeros((8, cols), F32))
        if k < steps - 1:
            pipelined(0, blocks, southward, start, *rotate_into(surf[k + 1], turned, cols - 1))
        else:
            lax.fori_loop(0, blocks, southward, start, unroll=GROUP)

    final_ref[...] = surf[steps][HALO : HALO + own_rows, 0:own_cols]

    gx, gy = place_ref[0], place_ref[1]
    lane8 = lax.broadcasted_iota(I32, (8, 128), 1)
    sub8 = row_iota((8, 128))
    per = grow_ref.shape[0] // (place_ref[2] * place_ref[3])
    per_tile = reads.shape[0] // steps
    first = (gx * place_ref[3] + gy) * per
    for g0 in range(0, per_tile, 8):
        spots = []
        for g in range(g0, g0 + 8):
            r = jnp.clip(grow_ref[first + g] - gx * own_rows, 0, own_rows - 1) + HALO
            q = jnp.clip(gcol_ref[first + g] - gy * own_cols, 0, own_cols - 1)
            at = (
                pl.ds(pl.multiple_of(r // 8 * 8, 8), 8),
                pl.ds(pl.multiple_of(q // 128 * 128, 128), 128),
            )
            spots.append((at, (sub8 == r % 8) & (lane8 == q % 128)))
        for k in range(steps):
            picked = [jnp.where(hit, surf[k + 1][at], 0.0) for at, hit in spots]
            reads[k * per_tile + g0 : k * per_tile + g0 + 8, :] = merge_rows(picked)
    values = jnp.sum(reads[...], axis=1, keepdims=True)
    spots = row_iota(reads.shape) + SLOTS == lax.broadcasted_iota(I32, reads.shape, 1)
    reading_row = jnp.sum(jnp.where(spots, values, 0.0), axis=0, keepdims=True)

    def seed(at, k):
        return count[at, :] * surf[k + 1][at, :] - obs[k, at, :]

    def begin_adjoint(i, c):
        at = rows_at(i)
        spread[at, :] = wet[at, :] * seed(at, steps - 1)
        return c

    turn_spread = rotate_into(spread, turned, cols - 1)
    turn_x = rotate_into(xe, west, 1)
    pipelined(0, blocks, begin_adjoint, 0, *turn_spread)
    for k in reversed(range(steps)):

        def gather(i, c, k=k):
            at = rows_at(i)
            b = spread[at, :]
            ge = (mass_gain * PUSH) * (turned[at, :] - b)
            gs = (mass_gain * PUSH) * (south_of(b, spread[pl.ds(nxt(i), 8), :]) - b)
            if k < steps - 1:
                ge = ge + ce[at, :]
                gs = gs + cs[at, :]
            if k > 0:
                ce[at, :] = ge * ae[k][at, :]
                cs[at, :] = gs * as_[k][at, :]
            xe[at, :] = ge * pe[k][at, :]
            xs[at, :] = gs * ps[k][at, :]
            adj[at, :] = (b + ge * qe[k][at, :]) + gs * qs[k][at, :]
            return c

        def collect(i, c, k=k):
            at = rows_at(i)
            before = xs[pl.ds(pl.multiple_of(jnp.maximum(i * 8 - 8, 0), 8), 8), :]
            out = (adj[at, :] + west[at, :]) + north_of(xs[at, :], before)
            if k > 0:
                spread[at, :] = wet[at, :] * (out + seed(at, k - 1))
            else:
                out = out[:, 0:own_cols]
                adj_ref[rows_at(i - HALO // 8), :] = out
                scaled = out * wet[at, 0:own_cols]
                for q in range(across):
                    grads[(i - HALO // 8) * across + q] = scaled[:, q * 128 : q * 128 + 128]
            return c

        pipelined(0, blocks, gather, 0, *turn_x)
        if k > 0:
            pipelined(0, blocks, collect, 0, *turn_spread)
        else:
            lax.fori_loop(HALO // 8, blocks - HALO // 8, collect, 0, unroll=GROUP)

    tiles = recv.shape[0] // CHUNK

    def sens(i, c):
        for j in range(SLOTS):
            products = []
            for u in range(8):
                t = i * 8 + u
                b = block_ref[j, t]
                products.append(grads[b] * recv[pl.ds(t * CHUNK + 8 * j, 8), :])
            parts[j, pl.ds(pl.multiple_of(i * 8, 8), 8), :] = merge_rows(products)
        return c

    lax.fori_loop(0, tiles // 8, sens, 0)
    lanes = lax.broadcasted_iota(I32, (tiles, 128), 1)
    out = jnp.broadcast_to(reading_row, (tiles, 128))
    for j in range(SLOTS):
        out = jnp.where(lanes == j, jnp.sum(parts[j], axis=1, keepdims=True), out)
    back_ref[...] = out


def closing_kernel(back_ref, table_ref, slip_ref, readings_ref, grad_ref):
    tiles = back_ref.shape[0]
    steps, gauges = readings_ref.shape
    faults = grad_ref.shape[0]
    per = gauges // tiles
    width = 128 // per
    lane = lax.broadcasted_iota(I32, (8, 128), 1)
    sub = row_iota((8, 128))

    turned = [
        pltpu.roll(back_ref[8 * c : 8 * c + 8, :], 0, 1, stride=per, stride_axis=0)
        for c in range(tiles // width)
    ]
    for k in range(steps):
        keep = (lane + 128 - SLOTS) % 128 // per == (sub + k) % width
        for c0 in range(0, tiles // width, 8):
            rows = merge_rows([jnp.where(keep, v, 0.0) for v in turned[c0 : c0 + 8]])
            rows = pltpu.roll(rows, 128 - SLOTS - per * k, 1)
            for c in range(8):
                at = slice((c0 + c) * 128, (c0 + c + 1) * 128)
                readings_ref[k : k + 1, at] = rows[c : c + 1, :]

    totals = [jnp.zeros((8, 128), F32)] * faults
    for c in range(tiles // 8):
        fault = pltpu.roll(table_ref[8 * c : 8 * c + 8, :], 128 - 8, 1)
        value = jnp.where(lane < SLOTS, back_ref[8 * c : 8 * c + 8, :], 0.0)
        totals = [
            t + jnp.where(fault == s + 1.0, value, 0.0) for s, t in enumerate(totals)
        ]
    total = jnp.concatenate([merge_rows(totals[i : i + 8]) for i in range(0, faults, 8)], axis=0)
    total = jnp.sum(total, axis=1, keepdims=True)
    mine = row_iota((faults, 128)) == lax.broadcasted_iota(I32, (faults, 128), 1)
    grad = jnp.sum(jnp.where(mine, total, 0.0), axis=0)
    grad_ref[...] = grad[0:faults] / slip_ref[...]


def body(
    ocean_depth,
    wet_mask,
    manning,
    fault_slip,
    pattern,
    foot_tile,
    foot_block,
    gauge_row,
    gauge_col,
    observed,
):
    rows_here, cols_here = ocean_depth.shape
    steps, gauges = observed.shape
    width_x = lax.axis_size("gx")
    width_y = lax.axis_size("gy")
    devices = width_x * width_y
    entries = pattern.shape[0]
    faults = fault_slip.shape[0]
    per_fault = entries // faults
    per_tile = gauges // devices
    both = ("gx", "gy")
    rows, cols = rows_here + 2 * HALO, cols_here + 128
    f = jax.ShapeDtypeStruct

    packed, table = pl.pallas_call(
        pack_kernel,
        out_shape=[f((devices * CHUNK, 128), F32), f((devices, 128), F32)],
        in_specs=[smem(), vmem(), vmem(), hbm()],
        out_specs=[vmem()] * 2,
        scratch_shapes=[
            pltpu.VMEM(pattern.shape, F32),
            pltpu.VMEM((1, entries), I32),
            pltpu.SMEM((1, entries), I32),
            pltpu.SemaphoreType.DMA((2,)),
        ],
        name="pack",
    )(fault_slip, foot_tile.reshape(1, entries), foot_block.reshape(1, entries), pattern)
    recv_flat = lax.all_to_all(packed.reshape(-1), both, split_axis=0, concat_axis=0, tiled=True)
    recv = recv_flat.reshape(devices * CHUNK, 128)

    edge = [f((24, rows_here), F32)] * 2 + [f((24, cols_here), F32)] * 2
    edges = pl.pallas_call(
        static_edge_kernel,
        out_shape=edge,
        in_specs=[vmem()] * 3,
        out_specs=[vmem()] * 4,
        name="static_edges",
        compiler_params=pltpu.CompilerParams(vmem_limit_bytes=4 * MIB),
    )(ocean_depth, wet_mask, manning)
    grid = f((rows, cols), F32)
    place = jnp.stack(
        [lax.axis_index("gx"), lax.axis_index("gy"), jnp.int32(width_x), jnp.int32(width_y)]
    ).astype(I32)
    count, obs, token = pl.pallas_call(
        gauge_kernel,
        out_shape=[grid, f((steps, rows, cols), F32), f((8, 128), F32)],
        in_specs=[smem()] * 4,
        out_specs=[vmem()] * 3,
        name="gauges",
        compiler_params=pltpu.CompilerParams(vmem_limit_bytes=2 * MIB),
    )(place, gauge_row, gauge_col, observed)

    eta, one, two, top, bottom, block_of = pl.pallas_call(
        scatter_kernel,
        out_shape=[f((rows_here, cols_here), F32)]
        + [f((32, rows_here), F32)] * 2
        + [f((32, cols_here), F32)] * 2
        + [f((8, devices), I32)],
        in_specs=[smem()] + [vmem()] * 6 + [hbm()],
        out_specs=[vmem()] * 6,
        scratch_shapes=[pltpu.SMEM((8, devices), I32), pltpu.SemaphoreType.DMA]
        + [pltpu.VMEM((rows_here * cols_here // 1024, 8, 128), F32)] * SLOTS,
        name="scatter",
        compiler_params=pltpu.CompilerParams(vmem_limit_bytes=10 * MIB),
    )(place, recv, wet_mask, *edges, token)
    sides = swapped(one, "gy", 0), swapped(two, "gy", 1)
    tiles = (eta, ocean_depth, wet_mask, manning)
    made = pl.pallas_call(
        tile_kernel,
        out_shape=[grid] * 12,
        in_specs=[vmem()] * 4,
        out_specs=[vmem()] * 12,
        compiler_params=pltpu.CompilerParams(vmem_limit_bytes=MIB),
        name="tile",
    )(*tiles)
    top, bottom, one, two = pl.pallas_call(
        rim_kernel,
        out_shape=[f((32, cols), F32)] * 4,
        in_specs=[smem()] + [vmem()] * 4 + [hbm()],
        out_specs=[vmem()] * 4,
        compiler_params=pltpu.CompilerParams(vmem_limit_bytes=MIB),
        name="rims",
    )(place, *sides, top, bottom, made[0])
    ends = swapped(one, "gx", 0), swapped(two, "gx", 1)
    framed = pl.pallas_call(
        frame_kernel,
        out_shape=[f((rows, 256), F32)] * 6 + [f((rows, 128), F32)] * 6 + [grid] * 7,
        in_specs=[smem()] + [vmem()] * 11,
        out_specs=[vmem()] * 19,
        scratch_shapes=[pltpu.VMEM((rows_here, 128), F32)] * 4,
        compiler_params=pltpu.CompilerParams(vmem_limit_bytes=2 * MIB),
        name="frame",
    )(place, *tiles, *sides, *made[:4], made[9])

    tile = f((rows_here, cols_here), F32)

    final, adjoint, back = pl.pallas_call(
        solve_kernel,
        out_shape=[tile, tile, f((devices, 128), F32)],
        in_specs=[smem()] * 3 + [vmem()] * 38 + [smem()],
        out_specs=[vmem()] * 3,
        scratch_shapes=[pltpu.VMEM((rows, cols), F32)] * (4 * (steps - 1) + 3 * (steps - 2) + 8)
        + [
            pltpu.VMEM((rows_here // 8 * (cols_here // 128), 8, 128), F32),
            pltpu.VMEM((SLOTS, devices, 128), F32),
            pltpu.VMEM((steps * per_tile, 128), F32),
        ]
        + [pltpu.VMEM((32, cols), F32)] * 2,
        compiler_params=pltpu.CompilerParams(vmem_limit_bytes=26 * MIB),
        name="solve",
    )(
        place, gauge_row, gauge_col, *made, *framed,
        *ends, top, bottom, count, obs, recv, block_of,
    )
    returned = lax.all_to_all(back, both, split_axis=0, concat_axis=0, tiled=True)
    readings, grad_slip = pl.pallas_call(
        closing_kernel,
        out_shape=[f((steps, gauges), F32), f((faults,), F32)],
        in_specs=[vmem()] * 3,
        out_specs=[vmem()] * 2,
        compiler_params=pltpu.CompilerParams(vmem_limit_bytes=MIB),
        name="closing",
    )(returned, table, fault_slip)
    return (final, readings, adjoint, grad_slip)


def solution(mesh):
    placed = (
        P("gx", "gy"),
        P("gx", "gy"),
        P("gx", "gy"),
        P(("gx", "gy")),
        P(("gx", "gy"), None, None),
        P(("gx", "gy"), None),
        P(("gx", "gy")),
        P(),
        P(),
        P(),
    )
    return jax.shard_map(
        body,
        mesh=mesh,
        in_specs=placed,
        out_specs=(P("gx", "gy"), P(), P("gx", "gy"), P(("gx", "gy"))),
        check_vma=False,
    )
```

```python
import math

import jax
import jax.numpy as jnp
from jax import lax
from jax.experimental import pallas as pl
from jax.experimental.pallas import tpu as pltpu
from jax.sharding import PartitionSpec as P

wave_gain = 0.2
mass_gain = 0.2
min_depth = 0.25
speed_floor = 0.01

HALO = 8
CHUNK = 33
SLOTS = 4
LN2 = math.log(2.0)
PUSH = -0.5 * wave_gain
assert abs(PUSH * PUSH - speed_floor) < 1e-12
ROUGH_SCALE = 0.5 * abs(PUSH) * 2.0 ** (7.0 / 3.0)
F32 = jnp.float32
MIB = 1 << 20
GROUP = 8
I32 = jnp.int32


def vmem():
    return pl.BlockSpec(memory_space=pltpu.VMEM)


def smem():
    return pl.BlockSpec(memory_space=pltpu.SMEM)


def hbm():
    return pl.BlockSpec(memory_space=pl.ANY)


def swapped(shard, axis, first):
    devices = lax.axis_size(axis)
    pairs = [(i, i + 1) for i in range(first, devices - 1, 2)]
    return lax.ppermute(shard, axis, pairs + [(j, i) for i, j in pairs])


def choose(flags, axis, even, odd):
    flag = flags[8 * axis : 8 * axis + 8, :]
    rows, cols = even.shape
    flag = jnp.concatenate([flag] * (cols // 128), axis=1)
    flag = jnp.concatenate([flag] * (rows // 8), axis=0)
    return jnp.where(flag > 0.5, even, odd)


def pack_kernel(
    slip_ref, tile_ref, block_ref, pattern_hbm, out_ref, table_ref, pattern, row_v, row_s, sems
):
    load = pltpu.make_async_copy(pattern_hbm, pattern, sems.at[0])
    load.start()
    rows = out_ref.shape[0]
    tiles = rows // CHUNK
    entries = tile_ref.shape[1]
    faults = slip_ref.shape[0]
    per_fault = entries // faults
    tile_row = tile_ref[...]
    tile_f = tile_row.astype(F32)
    tile_col = jnp.broadcast_to(tile_f, (128, entries)).T
    here = lax.broadcasted_iota(I32, (entries, 128), 0)
    ranks = []
    for q in range(entries // 128):
        there = lax.broadcasted_iota(I32, (entries, 128), 1) + q * 128
        same = (tile_col == tile_f[:, q * 128 : q * 128 + 128]) & (here < there)
        ranks.append(jnp.sum(jnp.where(same, 1.0, 0.0), axis=0, keepdims=True))
    rank = jnp.concatenate(ranks, axis=1).astype(I32)
    row_v[...] = tile_row * CHUNK + rank * 8
    place_rows = pltpu.make_async_copy(row_v, row_s, sems.at[1])
    place_rows.start()
    fault = lax.broadcasted_iota(I32, (1, entries), 1) // per_fault
    slot = lax.broadcasted_iota(I32, (128, entries), 0)
    facts = jnp.where(slot == rank, block_ref[...], 0) + jnp.where(slot == rank + 8, fault + 1, 0)
    hot = jnp.where(lax.broadcasted_iota(I32, (tiles, entries), 0) == tile_row, 1.0, 0.0)
    table_ref[...] = lax.dot_general(
        hot.astype(jnp.bfloat16),
        facts.astype(F32).astype(jnp.bfloat16),
        (((1,), (1,)), ((), ())),
        preferred_element_type=F32,
    )
    zero = jnp.zeros((8, 128), F32)

    def clear(i, c):
        out_ref[pl.ds(pl.multiple_of(i * 8, 8), 8), :] = zero
        return c

    lax.fori_loop(0, rows // 8, clear, 0, unroll=16)
    for t in range(tiles):
        out_ref[t * CHUNK + 32 : t * CHUNK + 33, :] = table_ref[t : t + 1, :]
    place_rows.wait()
    load.wait()

    def place(s, c):
        slip = slip_ref[s]
        for j in range(per_fault):
            i = s * per_fault + j
            out_ref[pl.ds(row_s[0, i], 8), :] = pattern[i] * slip
        return c

    lax.fori_loop(0, faults, place, 0)


def edges_of(first, last):
    lane = lax.broadcasted_iota(I32, first.shape, 1)
    both = jnp.where(lane < 64, first, last).T
    return both[0:8], both[120:128]


def side_block(east, west):
    rows = east.shape[1]
    gap = jnp.zeros((128 - 16, rows), F32)
    return jnp.concatenate([east, gap, west], axis=0).T


def scatter_kernel(
    flags_ref, recv_ref, wet_ref, west_in, east_in, top_in, bottom_in,
    eta_ref, one_ref, two_ref, top_ref, bottom_ref, block_out, block_s, sem, *acc,
):
    flags = flags_ref[...]
    tiles = recv_ref.shape[0] // CHUNK
    facts = recv_ref[pl.ds(8 * SLOTS, tiles, stride=CHUNK), :]
    block_out[...] = facts.T[0:8].astype(I32)
    load = pltpu.make_async_copy(block_out, block_s, sem)
    load.start()
    rows, cols = eta_ref.shape
    across = cols // 128
    zero = jnp.zeros((8, 128), F32)

    def clear(i, c):
        for a in acc:
            a[i] = zero
        return c

    lax.fori_loop(0, acc[0].shape[0], clear, 0, unroll=8)
    one_ref[0:24, :] = choose(flags, 1, east_in[...], west_in[...])
    two_ref[0:24, :] = choose(flags, 1, west_in[...], east_in[...])
    top_ref[0:24, :] = top_in[...]
    bottom_ref[0:24, :] = bottom_in[...]
    load.wait()

    def add(i, c):
        base = pl.multiple_of(i * (8 * CHUNK), 8)
        for u in range(8):
            for j in range(SLOTS):
                b = block_s[j, i * 8 + u]
                acc[j][b] = acc[j][b] + recv_ref[pl.ds(base + (u * CHUNK + 8 * j), 8), :]
        return c

    lax.fori_loop(0, tiles // 8, add, 0)

    def merge(i, c):
        r = pl.multiple_of(i * 8, 8)
        for q in range(across):
            b = i * across + q
            total = (acc[0][b] + acc[1][b]) + (acc[2][b] + acc[3][b])
            wet = wet_ref[pl.ds(r, 8), q * 128 : q * 128 + 128].astype(F32)
            eta_ref[pl.ds(r, 8), q * 128 : q * 128 + 128] = total * wet
        return c

    lax.fori_loop(0, rows // 8, merge, 0, unroll=2)
    west, east = edges_of(eta_ref[:, 0:128], eta_ref[:, cols - 128 : cols])
    one_ref[24:32] = choose(flags, 1, east, west)
    two_ref[24:32] = choose(flags, 1, west, east)
    top_ref[24:32] = eta_ref[0:8, :]
    bottom_ref[24:32] = eta_ref[rows - 8 : rows, :]


def static_edge_kernel(
    depth_ref, wet_ref, fric_ref, west_ref, east_ref, top_ref, bottom_ref
):
    rows, cols = depth_ref.shape
    for n, ref in enumerate((depth_ref, wet_ref, fric_ref)):
        at = slice(8 * n, 8 * n + 8)
        west, east = edges_of(ref[:, 0:128].astype(F32), ref[:, cols - 128 : cols].astype(F32))
        west_ref[at] = west
        east_ref[at] = east
        top_ref[at] = ref[0:8, :].astype(F32)
        bottom_ref[at] = ref[rows - 8 : rows, :].astype(F32)


def rim_kernel(
    flags_ref, one_in, two_in, top_in, bottom_in, after, top_ref, bottom_ref, one_ref, two_ref
):
    del after
    fields = one_in.shape[0] // 8
    rows = one_in.shape[1]
    cols = top_in.shape[1]
    flags = flags_ref[...]
    east_ref = choose(flags, 1, one_in[...], two_in[...])
    west_ref = choose(flags, 1, two_in[...], one_in[...])
    lane = lax.broadcasted_iota(I32, (8, 128), 1)
    for src, out, first, keep in (
        (top_in, top_ref, 0, slice(0, 8)),
        (bottom_in, bottom_ref, rows - 128, slice(120, 128)),
    ):
        pieces = []
        for n in range(fields):
            at = slice(8 * n, 8 * n + 8)
            pieces += [west_ref[at, first : first + 128], east_ref[at, first : first + 128]]
        pieces.append(jnp.zeros((128 - 16 * fields, 128), F32))
        corners = jnp.concatenate(pieces, axis=0).T[keep]
        for n in range(fields):
            at = slice(8 * n, 8 * n + 8)
            out[at, 0:cols] = src[at, :]
            out[at, cols:] = jnp.where(
                (lane < 8) | (lane >= 120), pltpu.roll(corners, 128 - 16 * n - 8, 1), 0.0
            )
    one_ref[...] = choose(flags, 0, bottom_ref[...], top_ref[...])
    two_ref[...] = choose(flags, 0, top_ref[...], bottom_ref[...])


def row_iota(shape):
    return lax.broadcasted_iota(I32, shape, 0)


def gauge_kernel(place_ref, row_ref, col_ref, obs_ref, count_out, obs_out, flags_out):
    for n in range(2):
        even = jnp.where(place_ref[n] % 2 == 0, 1.0, 0.0)
        flags_out[8 * n : 8 * n + 8, :] = jnp.full((8, 128), even, F32)
    steps, rows, cols = obs_out.shape
    own_rows = rows - 2 * HALO
    own_cols = cols - 128
    gx, gy, wx, wy = place_ref[0], place_ref[1], place_ref[2], place_ref[3]
    per = row_ref.shape[0] // (wx * wy)
    zero = jnp.zeros((8, cols), F32)

    def clear(i, c):
        r = pl.multiple_of(i * 8, 8)
        count_out[pl.ds(r, 8), :] = zero
        for k in range(steps):
            obs_out[k, pl.ds(r, 8), :] = zero
        return c

    lax.fori_loop(0, rows // 8, clear, 0)
    sub = row_iota((8, 128))
    lane = lax.broadcasted_iota(I32, (8, 128), 1)

    for dx in (-1, 0, 1):
        for dy in (-1, 0, 1):
            tx = gx + dx
            ty = gy + dy
            inside = (tx >= 0) & (tx < wx) & (ty >= 0) & (ty < wy)
            first = jnp.where(inside, (tx * wy + ty) * per, 0)

            def one(g, c, first=first, inside=inside):
                r = row_ref[first + g] - gx * own_rows + HALO
                q = col_ref[first + g] - gy * own_cols
                ok = inside & (r >= 0) & (r < rows) & (q >= -HALO) & (q < own_cols + HALO)
                q = jnp.where(q < 0, q + cols, q)

                @pl.when(ok)
                def _():
                    rb = pl.multiple_of(r // 8 * 8, 8)
                    cb = pl.multiple_of(q // 128 * 128, 128)
                    hit = (sub == r % 8) & (lane == q % 128)
                    at = (pl.ds(rb, 8), pl.ds(cb, 128))
                    count_out[at] = count_out[at] + jnp.where(hit, 1.0, 0.0)
                    for k in range(steps):
                        at_k = (k,) + at
                        obs_out[at_k] = obs_out[at_k] + jnp.where(hit, obs_ref[k, first + g], 0.0)

                return c

            lax.fori_loop(0, per, one, 0)


def face(f, s, sn, dd, rr, ww):
    x = dd + (s + sn)
    total = jnp.maximum(x, 2.0 * min_depth)
    diff = sn - s
    push = total * diff
    if f is not None:
        push = push + f
    t = push * push + 1.0
    y = (rr * jnp.exp2(jnp.log(total) * (-7.0 / 3.0 / LN2))) * lax.rsqrt(t)
    inv = 1.0 / (t * y + 1.0)
    wi = ww * inv
    flux = wi * push
    a = (wi * inv) * (y + 1.0)
    depth_part = (flux - flux * inv) * ((7.0 / 3.0) / total)
    share = jnp.where(
        x > 2.0 * min_depth, 1.0, jnp.where(x == 2.0 * min_depth, 0.5, 0.0)
    )
    u = share * (depth_part + a * diff)
    v = a * total
    return flux, a, u + v, u - v


def merge_rows(tiles):
    sub = row_iota((8, 128))
    for width in (1, 2, 4):
        low = (sub & width) == 0
        tiles = [
            jnp.where(low, p, q) + pltpu.roll(jnp.where(low, q, p), width, 0)
            for p, q in zip(tiles[0::2], tiles[1::2])
        ]
    return tiles[0]


def statics_of(d, w, m, d_next, w_next, m_next):
    return d + d_next, ROUGH_SCALE * (m + m_next), w * w_next


def south_of(here, after):
    last = row_iota(here.shape) == 7
    return jnp.where(last, pltpu.roll(after, 7, 0), pltpu.roll(here, 7, 0))


def north_of(flux, before):
    first = row_iota(flux.shape) == 0
    return jnp.where(first, pltpu.roll(before, 1, 0), pltpu.roll(flux, 1, 0))


def rows_at(i):
    return pl.ds(pl.multiple_of(i * 8, 8), 8)


def divergence(east, south, before):
    return (east - pltpu.roll(east, 1, 1)) + (south - north_of(south, before))


def store_face(refs, at, statics, made):
    flux, _, p, q = made
    for ref, value in zip(refs, (*statics, flux, p, q)):
        ref[at] = value


def tile_kernel(eta_ref, depth_ref, wet_ref, fric_ref, *out):
    east, south = out[:6], out[6:]
    rows, cols = eta_ref.shape
    fields = (depth_ref, wet_ref, fric_ref, eta_ref)
    keep = cols - 128

    def eastward(i, c):
        here = [ref[rows_at(i), :].astype(F32) for ref in fields]
        there = [pltpu.roll(v, cols - 1, 1)[:, :keep] for v in here]
        here = [v[:, :keep] for v in here]
        statics = statics_of(*here[:3], *there[:3])
        store_face(east, (rows_at(i + 1), slice(0, keep)), statics, face(None, here[3], there[3], *statics))
        return c

    def southward(i, c):
        here = [ref[rows_at(i), :].astype(F32) for ref in fields]
        there = [south_of(v, ref[rows_at(i + 1), :].astype(F32)) for v, ref in zip(here, fields)]
        statics = statics_of(*here[:3], *there[:3])
        store_face(south, (rows_at(i + 1), slice(0, cols)), statics, face(None, here[3], there[3], *statics))
        return c

    lax.fori_loop(0, rows // 8, eastward, 0, unroll=4)
    lax.fori_loop(0, rows // 8 - 1, southward, 0, unroll=3)


def frame_kernel(
    flags_ref, eta_ref, depth_ref, wet_ref, fric_ref, one_in, two_in, dde, rre, wwe, fe, fs, *refs
):
    east, south = refs[:6], refs[6:12]
    surf0, wet, surf1, fe1, ae1, pe1, qe1 = refs[12:19]
    sides = refs[19:]
    rows, cols = eta_ref.shape
    fields = (depth_ref, wet_ref, fric_ref, eta_ref)
    blocks = rows // 8
    flags = flags_ref[...]
    for n, side in enumerate(sides):
        one, two = one_in[8 * n : 8 * n + 8], two_in[8 * n : 8 * n + 8]
        side[...] = side_block(choose(flags, 1, one, two), choose(flags, 1, two, one))

    def frame(i, c):
        at = rows_at(i)
        out = rows_at(i + 1)
        after = rows_at(jnp.minimum(i + 1, blocks - 1))
        corner = [side[at, :] for side in sides]
        tail = [ref[at, cols - 128 :].astype(F32) for ref in fields]
        head = [ref[at, 0:128].astype(F32) for ref in fields]
        here = [jnp.concatenate(p, axis=1) for p in zip(tail, corner)]
        there = [
            pltpu.roll(jnp.concatenate(p, axis=1), 3 * 128 - 1, 1)[:, :256]
            for p in zip(tail, corner, head)
        ]
        statics = statics_of(*here[:3], *there[:3])
        store_face(east, (out, slice(None)), statics, face(None, here[3], there[3], *statics))
        there = [south_of(v, side[after, :]) for v, side in zip(corner, sides)]
        statics = statics_of(*corner[:3], *there[:3])
        store_face(south, (out, slice(None)), statics, face(None, corner[3], there[3], *statics))
        for ref, n in ((wet, 1), (surf0, 3)):
            ref[out, 0:cols] = fields[n][at, :].astype(F32)
            ref[out, cols:] = corner[n]
        return c

    lax.fori_loop(0, blocks, frame, 0, unroll=4)
    cut = cols - 128

    def whole(left, right, at):
        width = left.shape[1] - right.shape[1]
        return jnp.concatenate([left[at, 0:width], right[at, :]], axis=1)

    def surface(i, before):
        at = rows_at(i)
        flux = whole(fs, south[3], at)
        div = divergence(whole(fe, east[3], at), flux, before)
        surf1[at, :] = wet[at, :] * (surf0[at, :] - (mass_gain * PUSH) * div)
        return flux

    lax.fori_loop(2, blocks, surface, whole(fs, south[3], rows_at(1)), unroll=6)

    def eastward(i, c):
        at = rows_at(i)
        s = surf1[at, :]
        statics = [whole(a, b, at) for a, b in ((dde, east[0]), (rre, east[1]), (wwe, east[2]))]
        made = face(whole(fe, east[3], at), s, pltpu.roll(s, s.shape[1] - 1, 1), *statics)
        for ref, value in zip((fe1, ae1, pe1, qe1), made):
            ref[at, :] = value
        return c

    lax.fori_loop(2, blocks, eastward, 0, unroll=6)


def solve_kernel(*refs):
    late = refs[:3] + (refs[42],)
    east0, south0, east_part, south_part = (refs[3 + 6 * n : 9 + 6 * n] for n in range(4))
    surf0, wet, surf1, fe1, ae1, pe1, qe1 = refs[27:34]
    flags_ref, one_in, two_in, top_ref, bottom_ref, count, obs, recv, _ = refs[34:43]
    final_ref, adj_ref, back_ref = refs[43:46]
    steps, rows, cols = obs.shape
    scratch = list(refs[46:])

    def take_scratch(n):
        taken = scratch[:n]
        del scratch[:n]
        return taken

    surf = [surf0, surf1] + take_scratch(steps - 1)
    ae = [None, ae1] + take_scratch(steps - 2)
    own_rows, own_cols = final_ref.shape
    dde, rre, wwe, fe0, pe0, qe0 = east0
    dds, rrs, wws, fs, ps0, qs0 = south0
    as_ = [None] + take_scratch(steps - 1)
    pe = [pe0, pe1] + take_scratch(steps - 2)
    qe = [qe0, qe1] + take_scratch(steps - 2)
    ps = [ps0] + take_scratch(steps - 1)
    qs = [qs0] + take_scratch(steps - 1)
    adj, ce, cs, spread, turned, west, xe, xs, grads, parts, reads, north_ref, south_ref = scratch[:-5]
    place_ref, grow_ref, gcol_ref, block_ref, sems = scratch[-5:]
    loads = [
        pltpu.make_async_copy(src, dst, sems.at[n])
        for n, (src, dst) in enumerate(zip(late, scratch[-5:-1]))
    ]
    for load in loads:
        load.start()
    flags = flags_ref[...]
    south_ref[...] = choose(flags, 0, one_in[...], two_in[...])
    north_ref[...] = choose(flags, 0, two_in[...], one_in[...])
    sub = row_iota((8, cols))
    last = sub == 7
    firstrow = sub == 0
    blocks = rows // 8
    across = own_cols // 128

    def nxt(i):
        return pl.multiple_of(jnp.minimum(i * 8 + 8, rows - 8), 8)

    def take(i, c):
        at = rows_at(i)
        for whole, part in zip(east0 + south0, east_part + south_part):
            whole[at, cols - part.shape[1] :] = part[at, :]
        return c

    lax.fori_loop(1, blocks - 1, take, 0, unroll=2)

    def field(ref, n):
        return ref[8 * n : 8 * n + 8, :]

    def edge_face(refs, i, ref, neighbour):
        here = [field(ref, n) for n in range(4)]
        there = neighbour(here)
        statics = statics_of(*here[:3], *there[:3])
        store_face(refs, (rows_at(i), slice(None)), statics, face(None, here[3], there[3], *statics))

    def east_of(here):
        return [pltpu.roll(v, cols - 1, 1) for v in here]

    def above(ref):
        return lambda here: [south_of(v, field(ref, n)) for n, v in enumerate(here)]

    for i, ref in ((0, north_ref), (blocks - 1, south_ref)):
        surf0[rows_at(i), :] = field(ref, 3)
        wet[rows_at(i), :] = field(ref, 1)
        edge_face(east0, i, ref, east_of)
    edge_face(south0, 0, north_ref, above(top_ref))
    edge_face(south0, blocks - 2, bottom_ref, above(south_ref))
    edge_face(south0, blocks - 1, south_ref, above(south_ref))
    rim = (0, 1, blocks - 2, blocks - 1)
    for i in rim:
        at = rows_at(i)
        before = fs[rows_at(max(i - 1, 0)), :]
        div = divergence(fe0[at, :], fs[at, :], before)
        surf1[at, :] = wet[at, :] * (surf0[at, :] - (mass_gain * PUSH) * div)

    def pipelined(first, end, main, carry, begin, finish):
        groups = (end - first) // GROUP

        def step(g, carry):
            base = first + g * GROUP
            prior = jnp.maximum(base - GROUP, first)
            held = [begin(prior + u) for u in range(GROUP)]
            for u in range(GROUP):
                carry = main(base + u, carry)
            for u in range(GROUP):
                finish(prior + u, held[u])
            return carry

        carry = lax.fori_loop(0, groups, step, carry)
        done = first + groups * GROUP
        held = [begin(done - GROUP + u) for u in range(GROUP)]
        for i in range(done, end):
            carry = main(i, carry)
        for u in range(GROUP):
            finish(done - GROUP + u, held[u])
        held = [begin(i) for i in range(done, end)]
        for i in range(done, end):
            finish(i, held[i - done])
        return carry

    def rotate_into(src, dst, by):
        def begin(i):
            return pltpu.roll(src[rows_at(i), :], by, 1)

        def finish(i, value):
            dst[rows_at(i), :] = value

        return begin, finish

    def nothing(i, c):
        return c

    for k in range(1, steps):

        def eastward(i, c, k=k):
            here = rows_at(i)
            s = surf[k][here, :]
            s_east = pltpu.roll(s, cols - 1, 1) if k == 1 else turned[here, :]
            old = fe0 if k == 1 else fe1
            flux, a, p, q = face(old[here, :], s, s_east, dde[here, :], rre[here, :], wwe[here, :])
            fe1[here, :] = flux
            ae[k][here, :] = a
            pe[k][here, :] = p
            qe[k][here, :] = q
            return c

        def southward(i, carry, k=k):
            s, s_up, f_down = carry
            here = rows_at(i)
            sn = surf[k][pl.ds(nxt(i), 8), :]
            sn_up = pltpu.roll(sn, 7, 0)
            flux, a, p, q = face(
                fs[here, :], s, jnp.where(last, sn_up, s_up), dds[here, :], rrs[here, :], wws[here, :]
            )
            fs[here, :] = flux
            as_[k][here, :] = a
            ps[k][here, :] = p
            qs[k][here, :] = q
            down = pltpu.roll(flux, 1, 0)
            div = fe1[here, :] - west[here, :]
            div = div + (flux - jnp.where(firstrow, f_down, down))
            surf[k + 1][here, :] = wet[here, :] * (s - (mass_gain * PUSH) * div)
            return sn, sn_up, down

        turn_flux = rotate_into(fe1, west, 1)
        if k == 1:
            for i in rim:
                eastward(i, 0)
            pipelined(0, blocks, nothing, 0, *turn_flux)
        else:
            pipelined(0, blocks, eastward, 0, *turn_flux)
        s0 = surf[k][0:8, :]
        start = (s0, pltpu.roll(s0, 7, 0), jnp.zeros((8, cols), F32))
        if k < steps - 1:
            pipelined(0, blocks, southward, start, *rotate_into(surf[k + 1], turned, cols - 1))
        else:
            lax.fori_loop(0, blocks, southward, start, unroll=GROUP)

    final_ref[...] = surf[steps][HALO : HALO + own_rows, 0:own_cols]

    for load in loads:
        load.wait()
    gx, gy = place_ref[0], place_ref[1]
    lane8 = lax.broadcasted_iota(I32, (8, 128), 1)
    sub8 = row_iota((8, 128))
    per = grow_ref.shape[0] // (place_ref[2] * place_ref[3])
    per_tile = reads.shape[0] // steps
    first = (gx * place_ref[3] + gy) * per
    for g0 in range(0, per_tile, 8):
        spots = []
        for g in range(g0, g0 + 8):
            r = jnp.clip(grow_ref[first + g] - gx * own_rows, 0, own_rows - 1) + HALO
            q = jnp.clip(gcol_ref[first + g] - gy * own_cols, 0, own_cols - 1)
            at = (
                pl.ds(pl.multiple_of(r // 8 * 8, 8), 8),
                pl.ds(pl.multiple_of(q // 128 * 128, 128), 128),
            )
            spots.append((at, (sub8 == r % 8) & (lane8 == q % 128)))
        for k in range(steps):
            picked = [jnp.where(hit, surf[k + 1][at], 0.0) for at, hit in spots]
            reads[k * per_tile + g0 : k * per_tile + g0 + 8, :] = merge_rows(picked)
    values = jnp.sum(reads[...], axis=1, keepdims=True)
    spots = row_iota(reads.shape) + SLOTS == lax.broadcasted_iota(I32, reads.shape, 1)
    reading_row = jnp.sum(jnp.where(spots, values, 0.0), axis=0, keepdims=True)

    def seed(at, k):
        return count[at, :] * surf[k + 1][at, :] - obs[k, at, :]

    def begin_adjoint(i, c):
        at = rows_at(i)
        spread[at, :] = wet[at, :] * seed(at, steps - 1)
        return c

    turn_spread = rotate_into(spread, turned, cols - 1)
    turn_x = rotate_into(xe, west, 1)
    pipelined(0, blocks, begin_adjoint, 0, *turn_spread)
    for k in reversed(range(steps)):

        def gather(i, c, k=k):
            at = rows_at(i)
            b = spread[at, :]
            ge = (mass_gain * PUSH) * (turned[at, :] - b)
            gs = (mass_gain * PUSH) * (south_of(b, spread[pl.ds(nxt(i), 8), :]) - b)
            if k < steps - 1:
                ge = ge + ce[at, :]
                gs = gs + cs[at, :]
            if k > 0:
                ce[at, :] = ge * ae[k][at, :]
                cs[at, :] = gs * as_[k][at, :]
            xe[at, :] = ge * pe[k][at, :]
            xs[at, :] = gs * ps[k][at, :]
            adj[at, :] = (b + ge * qe[k][at, :]) + gs * qs[k][at, :]
            return c

        def collect(i, c, k=k):
            at = rows_at(i)
            before = xs[pl.ds(pl.multiple_of(jnp.maximum(i * 8 - 8, 0), 8), 8), :]
            out = (adj[at, :] + west[at, :]) + north_of(xs[at, :], before)
            if k > 0:
                spread[at, :] = wet[at, :] * (out + seed(at, k - 1))
            else:
                out = out[:, 0:own_cols]
                adj_ref[rows_at(i - HALO // 8), :] = out
                scaled = out * wet[at, 0:own_cols]
                for q in range(across):
                    grads[(i - HALO // 8) * across + q] = scaled[:, q * 128 : q * 128 + 128]
            return c

        pipelined(0, blocks, gather, 0, *turn_x)
        if k > 0:
            pipelined(0, blocks, collect, 0, *turn_spread)
        else:
            lax.fori_loop(HALO // 8, blocks - HALO // 8, collect, 0, unroll=GROUP)

    tiles = recv.shape[0] // CHUNK

    def sens(i, c):
        for j in range(SLOTS):
            products = []
            for u in range(8):
                t = i * 8 + u
                b = block_ref[j, t]
                products.append(grads[b] * recv[pl.ds(t * CHUNK + 8 * j, 8), :])
            parts[j, pl.ds(pl.multiple_of(i * 8, 8), 8), :] = merge_rows(products)
        return c

    lax.fori_loop(0, tiles // 8, sens, 0)
    lanes = lax.broadcasted_iota(I32, (tiles, 128), 1)
    out = jnp.broadcast_to(reading_row, (tiles, 128))
    for j in range(SLOTS):
        out = jnp.where(lanes == j, jnp.sum(parts[j], axis=1, keepdims=True), out)
    back_ref[...] = out


def closing_kernel(back_ref, table_ref, slip_ref, readings_ref, grad_ref):
    tiles = back_ref.shape[0]
    steps, gauges = readings_ref.shape
    faults = grad_ref.shape[0]
    per = gauges // tiles
    width = 128 // per
    lane = lax.broadcasted_iota(I32, (8, 128), 1)
    sub = row_iota((8, 128))

    turned = [
        pltpu.roll(back_ref[8 * c : 8 * c + 8, :], 0, 1, stride=per, stride_axis=0)
        for c in range(tiles // width)
    ]
    for k in range(steps):
        keep = (lane + 128 - SLOTS) % 128 // per == (sub + k) % width
        for c0 in range(0, tiles // width, 8):
            rows = merge_rows([jnp.where(keep, v, 0.0) for v in turned[c0 : c0 + 8]])
            rows = pltpu.roll(rows, 128 - SLOTS - per * k, 1)
            for c in range(8):
                at = slice((c0 + c) * 128, (c0 + c + 1) * 128)
                readings_ref[k : k + 1, at] = rows[c : c + 1, :]

    totals = [jnp.zeros((8, 128), F32)] * faults
    for c in range(tiles // 8):
        fault = pltpu.roll(table_ref[8 * c : 8 * c + 8, :], 128 - 8, 1)
        value = jnp.where(lane < SLOTS, back_ref[8 * c : 8 * c + 8, :], 0.0)
        totals = [
            t + jnp.where(fault == s + 1.0, value, 0.0) for s, t in enumerate(totals)
        ]
    total = jnp.concatenate([merge_rows(totals[i : i + 8]) for i in range(0, faults, 8)], axis=0)
    total = jnp.sum(total, axis=1, keepdims=True)
    mine = row_iota((faults, 128)) == lax.broadcasted_iota(I32, (faults, 128), 1)
    grad = jnp.sum(jnp.where(mine, total, 0.0), axis=0)
    grad_ref[...] = grad[0:faults] / slip_ref[...]


def body(
    ocean_depth,
    wet_mask,
    manning,
    fault_slip,
    pattern,
    foot_tile,
    foot_block,
    gauge_row,
    gauge_col,
    observed,
):
    rows_here, cols_here = ocean_depth.shape
    steps, gauges = observed.shape
    width_x = lax.axis_size("gx")
    width_y = lax.axis_size("gy")
    devices = width_x * width_y
    entries = pattern.shape[0]
    faults = fault_slip.shape[0]
    per_fault = entries // faults
    per_tile = gauges // devices
    both = ("gx", "gy")
    rows, cols = rows_here + 2 * HALO, cols_here + 128
    f = jax.ShapeDtypeStruct

    packed, table = pl.pallas_call(
        pack_kernel,
        out_shape=[f((devices * CHUNK, 128), F32), f((devices, 128), F32)],
        in_specs=[smem(), vmem(), vmem(), hbm()],
        out_specs=[vmem()] * 2,
        scratch_shapes=[
            pltpu.VMEM(pattern.shape, F32),
            pltpu.VMEM((1, entries), I32),
            pltpu.SMEM((1, entries), I32),
            pltpu.SemaphoreType.DMA((2,)),
        ],
        name="pack",
    )(fault_slip, foot_tile.reshape(1, entries), foot_block.reshape(1, entries), pattern)
    recv_flat = lax.all_to_all(packed.reshape(-1), both, split_axis=0, concat_axis=0, tiled=True)
    recv = recv_flat.reshape(devices * CHUNK, 128)

    edge = [f((24, rows_here), F32)] * 2 + [f((24, cols_here), F32)] * 2
    edges = pl.pallas_call(
        static_edge_kernel,
        out_shape=edge,
        in_specs=[vmem()] * 3,
        out_specs=[vmem()] * 4,
        name="static_edges",
        compiler_params=pltpu.CompilerParams(vmem_limit_bytes=4 * MIB),
    )(ocean_depth, wet_mask, manning)
    grid = f((rows, cols), F32)
    place = jnp.stack(
        [lax.axis_index("gx"), lax.axis_index("gy"), jnp.int32(width_x), jnp.int32(width_y)]
    ).astype(I32)
    count, obs, flags = pl.pallas_call(
        gauge_kernel,
        out_shape=[grid, f((steps, rows, cols), F32), f((16, 128), F32)],
        in_specs=[smem()] * 4,
        out_specs=[vmem()] * 3,
        name="gauges",
        compiler_params=pltpu.CompilerParams(vmem_limit_bytes=2 * MIB),
    )(place, gauge_row, gauge_col, observed)

    eta, one, two, top, bottom, block_of = pl.pallas_call(
        scatter_kernel,
        out_shape=[f((rows_here, cols_here), F32)]
        + [f((32, rows_here), F32)] * 2
        + [f((32, cols_here), F32)] * 2
        + [f((8, devices), I32)],
        in_specs=[vmem()] * 7,
        out_specs=[vmem()] * 6,
        scratch_shapes=[pltpu.SMEM((8, devices), I32), pltpu.SemaphoreType.DMA]
        + [pltpu.VMEM((rows_here * cols_here // 1024, 8, 128), F32)] * SLOTS,
        name="scatter",
        compiler_params=pltpu.CompilerParams(vmem_limit_bytes=10 * MIB),
    )(flags, recv, wet_mask, *edges)
    sides = swapped(one, "gy", 0), swapped(two, "gy", 1)
    tiles = (eta, ocean_depth, wet_mask, manning)
    made = pl.pallas_call(
        tile_kernel,
        out_shape=[grid] * 12,
        in_specs=[vmem()] * 4,
        out_specs=[vmem()] * 12,
        compiler_params=pltpu.CompilerParams(vmem_limit_bytes=MIB),
        name="tile",
    )(*tiles)
    top, bottom, one, two = pl.pallas_call(
        rim_kernel,
        out_shape=[f((32, cols), F32)] * 4,
        in_specs=[vmem()] * 5 + [hbm()],
        out_specs=[vmem()] * 4,
        compiler_params=pltpu.CompilerParams(vmem_limit_bytes=MIB),
        name="rims",
    )(flags, *sides, top, bottom, made[0])
    ends = swapped(one, "gx", 0), swapped(two, "gx", 1)
    framed = pl.pallas_call(
        frame_kernel,
        out_shape=[f((rows, 256), F32)] * 6 + [f((rows, 128), F32)] * 6 + [grid] * 7,
        in_specs=[vmem()] * 12,
        out_specs=[vmem()] * 19,
        scratch_shapes=[pltpu.VMEM((rows_here, 128), F32)] * 4,
        compiler_params=pltpu.CompilerParams(vmem_limit_bytes=2 * MIB),
        name="frame",
    )(flags, *tiles, *sides, *made[:4], made[9])

    tile = f((rows_here, cols_here), F32)

    final, adjoint, back = pl.pallas_call(
        solve_kernel,
        out_shape=[tile, tile, f((devices, 128), F32)],
        in_specs=[hbm()] * 3 + [vmem()] * 39 + [hbm()],
        out_specs=[vmem()] * 3,
        scratch_shapes=[pltpu.VMEM((rows, cols), F32)] * (4 * (steps - 1) + 3 * (steps - 2) + 8)
        + [
            pltpu.VMEM((rows_here // 8 * (cols_here // 128), 8, 128), F32),
            pltpu.VMEM((SLOTS, devices, 128), F32),
            pltpu.VMEM((steps * per_tile, 128), F32),
        ]
        + [pltpu.VMEM((32, cols), F32)] * 2
        + [pltpu.SMEM(v.shape, I32) for v in (place, gauge_row, gauge_col, block_of)]
        + [pltpu.SemaphoreType.DMA((4,))],
        compiler_params=pltpu.CompilerParams(vmem_limit_bytes=26 * MIB),
        name="solve",
    )(
        place, gauge_row, gauge_col, *made, *framed,
        flags, *ends, top, bottom, count, obs, recv, block_of,
    )
    returned = lax.all_to_all(back, both, split_axis=0, concat_axis=0, tiled=True)
    readings, grad_slip = pl.pallas_call(
        closing_kernel,
        out_shape=[f((steps, gauges), F32), f((faults,), F32)],
        in_specs=[vmem()] * 3,
        out_specs=[vmem()] * 2,
        compiler_params=pltpu.CompilerParams(vmem_limit_bytes=MIB),
        name="closing",
    )(returned, table, fault_slip)
    return (final, readings, adjoint, grad_slip)


def solution(mesh):
    placed = (
        P("gx", "gy"),
        P("gx", "gy"),
        P("gx", "gy"),
        P(("gx", "gy")),
        P(("gx", "gy"), None, None),
        P(("gx", "gy"), None),
        P(("gx", "gy")),
        P(),
        P(),
        P(),
    )
    return jax.shard_map(
        body,
        mesh=mesh,
        in_specs=placed,
        out_specs=(P("gx", "gy"), P(), P("gx", "gy"), P(("gx", "gy"))),
        check_vma=False,
    )
```
